32 devices in a mesh: grp: 2 (over y), req: 4 (over z), kvh: 4 (over x, core).
Axes of the slice: x: 2, y: 2, z: 4, core: 2. Of those that a mesh axis runs over, the one named last changes fastest.
Arguments:
- store_kv: bfloat16 [32, 128, 8, 256], P(('grp', 'req'), None, 'kvh'), parts along dimension 0, may hold values from -7.25 to 7.25
- block_owner: int32 [8, 24, 1], P(('grp', 'req')), parts along dimension 0, may hold values from 0 to 3; in each aligned block of 24 rows (0 to 23, 24 to 47, ..., all dimensions but the last counted through in order) at most 6 rows name the same one
- block_slot: int32 [8, 24], P(('grp', 'req')), parts along dimension 0, may hold values from 0 to 3
- span_len: int32 [8, 4], P(('grp', 'req')), parts along dimension 0, may hold values from 1 to 12, 24 in all within a row
- row_index: int32 [8, 384], P(('grp', 'req')), parts along dimension 0, may hold values from 0 to 3071, as said below
- fresh_q: bfloat16 [8, 384, 8192], P(('grp', 'req'), None, 'kvh'), parts along dimension 0, may hold values from -12 to 12
- fresh_kv: bfloat16 [8, 384, 8, 256], P(('grp', 'req'), None, 'kvh'), parts along dimension 0, may hold values from -6 to 6
Outputs:
- attended: bfloat16 [8, 384, 8192], P(('grp', 'req'), None, 'kvh'), parts along dimension 0
The draws below stay inside these ranges and needn't reach their ends.
There are 2 independent parts, one for each index of `grp`. The reference program is written for one: setup_inputs(seed, part) draws one part's arguments, and reference() takes and returns one part's arrays. A program takes and returns all parts, laid end to end along the dimension named above; each array names one. Nothing has to cross between parts.
Inputs may be any that keep to these rules, and one draw needn't show every extreme that they name: `block_owner`: among the 24 blocks of one request no store shard appears more than 6 times; in every draw some shard appears exactly 6 times for some request. `span_len`: each row sums to 24; its largest entry is 12. `row_index`: each row is ascending without repeats, starts with 0 and ends with 3071.
All inputs are finite; a program needn't handle non-finite values.
Results may differ from the reference program's by a relative error of at most 0.0095.
Values may be sent and summed in bfloat16 or wider, within the bound.
No kernel may reach another device: no remote copies, remote signals or barrier semaphores. Data moves between devices by JAX's collectives and lax.ppermute only.
A program may use at most 64 MiB of HBM per device.

```python
import math
import jax
import jax.numpy as jnp
import numpy as np
from jax import lax

HD = 128
KVH = 8
HQ = 64
BLK = 128
RB = 24
ROWS = 384
SB = 4
NCH = 4
MOSTLEN = 12
REQS = 4
CTX = 3072
STORE = 16
CAP = 6
N_REQ = 4


def draw_fresh_q(key, part):
    shape = (REQS, ROWS, HQ * HD)
    field = jnp.clip(2.0 * jax.random.normal(jax.random.fold_in(key, 3), shape), -10.0, 10.0)
    return field.astype(jnp.bfloat16)


def draw_store_kv(key, part):
    shape = (STORE, BLK, KVH, 2 * HD)
    field = jnp.clip(1.25 * jax.random.normal(jax.random.fold_in(key, 7), shape), -6.0, 6.0)
    return field.astype(jnp.bfloat16)


def draw_row_index(key, part):

    def one_row(request):
        inner = jax.random.permutation(jax.random.fold_in(key, request), CTX - 2)[:ROWS - 2] + 1
        return jnp.concatenate([jnp.zeros((1,), jnp.int32), jnp.sort(inner).astype(jnp.int32), jnp.full((1,), CTX - 1, jnp.int32)])
    return jax.vmap(one_row)(jnp.arange(REQS))


def set_ends(entries, stream_key, least, high):
    spot = [jax.random.randint(jax.random.fold_in(stream_key, axis), (), 0, length) for axis, length in enumerate(entries.shape)]
    main_axis = entries.shape.index(max(entries.shape))
    beside = spot[:main_axis] + [(spot[main_axis] + 1) % entries.shape[main_axis]] + spot[main_axis + 1:]
    return entries.at[tuple(spot)].set(least).at[tuple(beside)].set(high)


def block_scale(key, extent, split, least, high):
    def one(dim, shards_of):
        steps = jax.random.uniform(jax.random.fold_in(jax.random.fold_in(key, 6), dim), (shards_of,), jnp.float32, least / len(split), high / len(split))
        return jnp.repeat(jnp.exp(steps), extent[dim] // shards_of).reshape((-1,) + (1,) * (len(extent) - dim - 1))

    loudness = one(*split[0])
    for cut in split[1:]:
        loudness = loudness * one(*cut)
    return loudness


def split_up(amount, total, most, slope):
    loads = [(1 << 20) // math.isqrt(rank ** slope) + 1 for rank in range(2, amount + 1)]
    rest, counts = total - most - (amount - 1), [1] * (amount - 1)
    while rest > 0:
        free = [i for i in range(amount - 1) if counts[i] < most]
        pool, left = sum([loads[i] for i in free]), rest
        for i in free:
            extra = min(most - counts[i], max(1, left * loads[i] // pool), rest)
            counts[i] = counts[i] + extra
            rest = rest - extra
    return np.array([most] + counts)


def uneven(stream_key, count, total, limit, lean):
    if count == 2:
        one = jax.random.randint(stream_key, (), max(1, total - limit), min(limit, total - 1) + 1)
        return jnp.stack([one, total - one])
    sizes = jnp.asarray(split_up(count, total, limit, lean), jnp.int32)
    couples = (count - 1) // 2
    source_of, sink = sizes[1:1 + 2 * couples:2], sizes[2:2 + 2 * couples:2]
    margin = jnp.minimum(source_of - 1, limit - sink)
    moved = jax.random.randint(jax.random.fold_in(stream_key, 1), (couples,), 0, 1 << 20) % (margin + 1)
    sizes = sizes.at[1:1 + 2 * couples:2].set(source_of - moved).at[2:2 + 2 * couples:2].set(sink + moved)
    return sizes[jax.random.permutation(jax.random.fold_in(stream_key, 2), count)]


def shared_out(own_key, own, number, rows, number_of, top, most, skew):
    order = jax.random.permutation(own_key, number_of)
    crowded, common = portions_of(number_of, rows * top, most, skew, True), portions_of(number_of, rows * top, most, skew, False)
    places = jnp.arange(number_of)

    def named(tallies, turn):
        used = int((tallies > 0).sum())
        fixed = max(1, used // 4)
        passed = fixed + (places - fixed + turn * (used - fixed)) % max(1, number_of - fixed)
        return jnp.zeros((number_of,), jnp.int32).at[order[jnp.where(places < fixed, places, passed)]].set(jnp.asarray(tallies, jnp.int32))

    tallies = jnp.where(number % 4 == 0, named(crowded, number // 4), named(common, number - number // 4 - 1))
    mixed = jax.random.permutation(jax.random.fold_in(own, 3), number_of)
    donor, sink = mixed[0:number_of // 2 * 2:2], mixed[1:number_of // 2 * 2:2]
    margin = jnp.minimum(tallies[donor] - 1, most - tallies[sink]) // 2
    margin = jnp.where((donor == order[0]) | (sink == order[0]) | (tallies[sink] == 0), 0, jnp.maximum(margin, 0))
    passed = jax.random.randint(jax.random.fold_in(own, 4), (number_of // 2,), 0, 1 << 20) % (margin + 1)
    tallies = tallies.at[donor].add(-passed).at[sink].add(passed)
    items = jnp.searchsorted(jnp.cumsum(tallies), jnp.arange(rows * top), side="right").astype(jnp.int32)
    grid = items.reshape(top, rows).T
    grid = grid[jax.random.permutation(jax.random.fold_in(own, 1), rows)]
    turn = jax.random.randint(jax.random.fold_in(own, 2), (rows, 1), 0, top)
    return jnp.take_along_axis(grid, (jnp.arange(top)[None, :] + turn) % top, axis=1)


def portions_of(amount, total, reach, skew, full):
    portions = [(1 << 20) // math.isqrt(grade ** skew) + 1 for grade in range(1, amount + 1)]
    largest = reach if full else min(reach, max(-(-total // amount), total * portions[0] // sum(portions)))
    least = 1 if total - largest >= amount - 1 else 0
    given, rest = [largest] + [least] * (amount - 1), total - largest - least * (amount - 1)
    while rest > 0:
        free = [i for i in range(1, amount) if given[i] < largest] or [i for i in range(1, amount) if given[i] < reach]
        mass, left = sum([portions[i] for i in free]), rest
        for i in free:
            extra = min(reach - given[i], max(1, left * portions[i] // mass), rest)
            given[i] = given[i] + extra
            rest = rest - extra
    return np.array(given)


def scatter_about(own_key, extent, scale, reach, cuts=(), kind=jnp.bfloat16):
    gain = block_scale(own_key, extent, cuts, -0.22, 0.18) if cuts else 1.0
    values = jax.random.normal(own_key, extent, jnp.float32) * scale * gain
    return jnp.minimum(jnp.maximum(values, -reach), reach).astype(kind)


def setup_inputs(seed: int = 0, part: int = 0) -> dict:
    arg_keys = jax.random.split(jax.random.key(seed), 8)
    part_keys = jax.random.split(jax.random.fold_in(arg_keys[7], part), 8)
    store_kv = draw_store_kv(jax.random.fold_in(jax.random.fold_in(arg_keys[7], part), 71), part)
    block_owner_keys = jax.random.split(jax.random.fold_in(part_keys[1], 1), REQS * RB // RB)
    block_owner_turns = jax.random.permutation(jax.random.fold_in(part_keys[1], 3), REQS * RB // RB)
    block_owner = jax.vmap(lambda own, number: shared_out(jax.random.fold_in(part_keys[1], 2), own, number, RB, N_REQ, 1, CAP, 2))(block_owner_keys, block_owner_turns).reshape((REQS, RB, 1))
    block_slot = set_ends(jax.random.randint(part_keys[2], (REQS, RB), 0, SB), jax.random.fold_in(part_keys[2], 1), 0, SB - 1).astype(jnp.int32)
    span_len = jax.vmap(lambda own: uneven(own, NCH, RB, MOSTLEN, 1))(jax.random.split(part_keys[3], REQS)).reshape((REQS, NCH)).astype(jnp.int32)
    row_index = draw_row_index(jax.random.fold_in(jax.random.fold_in(arg_keys[7], part), 71), part)
    fresh_q = draw_fresh_q(jax.random.fold_in(jax.random.fold_in(arg_keys[7], part), 71), part)
    fresh_kv = scatter_about(part_keys[6], (REQS, ROWS, KVH, 2 * HD), 1.25, 6.0, ((0, 4), (2, 4)))
    return {"store_kv": store_kv, "block_owner": block_owner, "block_slot": block_slot, "span_len": span_len, "row_index": row_index, "fresh_q": fresh_q, "fresh_kv": fresh_kv}


rope_base = 500000.0


def rotate(field, position):
    half_dim = field.shape[-1] // 2
    pair_index = jnp.arange(half_dim, dtype=jnp.float32)
    inv_freq = jnp.exp(pair_index * (-2.0 / field.shape[-1]) * jnp.log(jnp.float32(rope_base)))
    angles = position[..., None] * inv_freq
    cosine = jnp.cos(angles)
    sine_part = jnp.sin(angles)
    first_half = field[..., :half_dim]
    second = field[..., half_dim:]
    return jnp.concatenate([first_half * cosine - second * sine_part, second * cosine + first_half * sine_part], axis=-1)


def span_offsets(lengths, block_count, block_len):
    starts = jnp.cumsum(lengths) - lengths
    block_ids = jnp.arange(block_count, dtype=jnp.int32)
    began = jnp.where(starts[None, :] <= block_ids[:, None], starts[None, :], 0)
    return (jnp.max(began, axis=1) * block_len).astype(jnp.int32)


def attend_head(query_rows, key_rows, value_rows, query_pos):
    key_pos = jnp.arange(key_rows.shape[0], dtype=jnp.int32)
    scores = lax.dot_general(query_rows, key_rows, (((1,), (1,)), ((), ())), preferred_element_type=jnp.float32)
    scores = scores * (key_rows.shape[1] ** -0.5)
    scores = jnp.where(key_pos[None, :] <= query_pos[:, None], scores, -jnp.inf)
    largest = jnp.max(scores, axis=1, keepdims=True)
    weights = jnp.exp(scores - largest)
    probs = (weights / jnp.sum(weights, axis=1, keepdims=True)).astype(jnp.bfloat16)
    return jnp.dot(probs, value_rows, preferred_element_type=jnp.float32).astype(jnp.bfloat16)


def reference(store_kv, block_owner, block_slot, span_len, row_index, fresh_q, fresh_kv):
    def one_request(inputs):
        owners, slot_ids, lengths, row_pos, query, fresh = inputs
        cached = store_kv[owners[:, 0] * SB + slot_ids]
        offset = span_offsets(lengths, RB, BLK)
        key_rows = rotate(cached[..., :HD].astype(jnp.float32), offset[:, None, None].astype(jnp.float32))
        key_rows = key_rows.astype(jnp.bfloat16).reshape(CTX, KVH, HD)
        value_rows = cached[..., HD:].reshape(CTX, KVH, HD)
        position = row_pos.astype(jnp.float32)
        fresh_keys = rotate(fresh[..., :HD].astype(jnp.float32), position[:, None]).astype(jnp.bfloat16)
        key_rows = key_rows.at[row_pos].set(fresh_keys)
        value_rows = value_rows.at[row_pos].set(fresh[..., HD:])
        query_group = HQ // KVH
        queries = rotate(query.reshape(ROWS, KVH, query_group, HD).astype(jnp.float32), position[:, None, None])
        queries = queries.astype(jnp.bfloat16)
        query_pos = jnp.repeat(row_pos, query_group)

        def per_head(operands):
            head_queries, head_keys, head_values = operands
            return attend_head(head_queries.reshape(ROWS * query_group, HD), head_keys, head_values, query_pos)

        result = lax.map(per_head, (jnp.transpose(queries, (1, 0, 2, 3)), jnp.transpose(key_rows, (1, 0, 2)), jnp.transpose(value_rows, (1, 0, 2))))
        return jnp.transpose(result.reshape(KVH, ROWS, query_group, HD), (1, 0, 2, 3)).reshape(ROWS, HQ * HD)

    return lax.map(one_request, (block_owner, block_slot, span_len, row_index, fresh_q, fresh_kv))
```

```python
import functools
import math

import jax
import jax.numpy as jnp
from jax import lax
from jax.experimental import pallas as pl
from jax.experimental.pallas import tpu as pltpu
from jax.sharding import PartitionSpec as P

rope_base = 500000.0
tile_rows = 32
low = -1e30
far = 1 << 20
vmem = pl.BlockSpec(memory_space=pltpu.VMEM)
smem = pl.BlockSpec(memory_space=pltpu.SMEM)
anywhere = pl.BlockSpec(memory_space=pl.ANY)
params = pltpu.CompilerParams(vmem_limit_bytes=56 << 20)


def tables(position, head_dim):
    half_dim = head_dim // 2
    pair_index = jnp.arange(half_dim, dtype=jnp.float32)
    inv_freq = jnp.exp(pair_index * (-2.0 / head_dim) * jnp.log(jnp.float32(rope_base)))
    angles = position[:, None] * inv_freq
    cosine = jnp.cos(angles)
    sine = jnp.sin(angles)
    return (
        jnp.concatenate([cosine, cosine], axis=1),
        jnp.concatenate([-sine, sine], axis=1),
    )


def span_offsets(lengths, block_count, block_len):
    starts = jnp.cumsum(lengths) - lengths
    block_ids = jnp.arange(block_count, dtype=jnp.int32)
    began = jnp.where(starts[None, :] <= block_ids[:, None], starts[None, :], 0)
    return jnp.max(began, axis=1) * block_len


def turn(field, cosine, sine):
    return field * cosine + pltpu.roll(field, field.shape[1] // 2, 1) * sine


def prepare(query_ref, fresh_ref, cos_ref, sin_ref, pos_ref, turned_ref, placed_ref, wide_ref, all_ref):
    heads, tiles, lanes_rows, dim = turned_ref.shape
    group = lanes_rows // tile_rows
    blocks, block_len, _ = placed_ref.shape
    rows = cos_ref.shape[0]

    def turn_tile(tile, carry):
        at = pl.ds(pl.multiple_of(tile * tile_rows, tile_rows), tile_rows)
        cosine = cos_ref[at, :]
        sine = sin_ref[at, :]
        for head in range(heads):
            for member in range(group):
                column = (head * group + member) * dim
                field = query_ref[at, column : column + dim].astype(jnp.float32)
                turned_ref[head, tile, member * tile_rows : (member + 1) * tile_rows, :] = turn(
                    field, cosine, sine
                ).astype(jnp.bfloat16)
        return carry

    lax.fori_loop(0, tiles, turn_tile, 0)
    wide_ref[...] = fresh_ref[...].astype(jnp.float32)
    for head in range(heads):
        key = wide_ref[pl.ds(head, rows, stride=2 * heads), :]
        value = wide_ref[pl.ds(heads + head, rows, stride=2 * heads), :]
        all_ref[:, head * 2 * dim : head * 2 * dim + dim] = turn(
            key, cos_ref[...], sin_ref[...]
        ).astype(jnp.bfloat16)
        all_ref[:, head * 2 * dim + dim : (head + 1) * 2 * dim] = value.astype(jnp.bfloat16)
    all_ref[:, heads * 2 * dim :] = jnp.ones((rows, dim), jnp.bfloat16)

    def place(block, carry):
        spot = lax.broadcasted_iota(jnp.int32, (block_len, rows), 0) + block * block_len
        chosen = jnp.where(spot == pos_ref[...], 1.0, 0.0).astype(jnp.bfloat16)
        placed_ref[block] = jnp.dot(
            chosen, all_ref[...], preferred_element_type=jnp.float32
        ).astype(jnp.bfloat16)
        return carry

    lax.fori_loop(0, blocks, place, 0)


def attend(counts, blocks, slots, first, last, *refs):
    given = len(counts)
    sources = refs[:given]
    meta_ref, turned_ref, placed_ref, cos_ref, sin_ref, row_ref = refs[given : given + 6]
    refs = refs[given + 6 :]
    if not first:
        most_in, sum_in, acc_in = refs[:3]
        refs = refs[3:]
    if last:
        out_ref = refs[0]
        refs = refs[1:]
    else:
        most_out, sum_out, acc_out = refs[:3]
        refs = refs[3:]
    raw_ref, wide_ref, key_ref, value_ref, score_ref, list_ref, sems = refs
    heads, tiles, lanes_rows, dim = turned_ref.shape
    group = lanes_rows // tile_rows
    block_len = placed_ref.shape[1]
    stride = 2 * heads
    raw_rows = block_len * stride
    scale = dim**-0.5 * math.log2(math.e)
    bounds_at = 2 * blocks
    first_at = bounds_at + blocks + 1

    def find(block, found):
        owner = meta_ref[block]
        slot = meta_ref[blocks + block]
        hit = owner < 0
        for number in range(given):
            lowest = meta_ref[first_at + number]
            here = (owner >= lowest) & (owner < lowest + counts[number])
            hit = hit | here

            @pl.when(here)
            def _(number=number, lowest=lowest):
                start = pl.multiple_of(((owner - lowest) * slots + slot) * raw_rows, raw_rows)
                pltpu.make_async_copy(
                    sources[number].at[pl.ds(start, raw_rows), :], raw_ref.at[found], sems.at[found]
                ).start()

        list_ref[found] = block
        return found + hit.astype(jnp.int32)

    found = lax.fori_loop(0, blocks, find, jnp.int32(0))

    def load(spot, carry):
        block = list_ref[spot]
        pltpu.make_async_copy(
            sources[0].at[pl.ds(0, raw_rows), :], raw_ref.at[spot], sems.at[spot]
        ).wait()
        wide_ref[...] = raw_ref[spot].astype(jnp.float32)
        cosine = cos_ref[pl.ds(block, 1), :]
        sine = sin_ref[pl.ds(block, 1), :]
        fresh = placed_ref[block].astype(jnp.float32)
        renewed = fresh[:, heads * 2 * dim :] > 0.5
        at = pl.ds(pl.multiple_of(spot * block_len, block_len), block_len)
        for head in range(heads):
            key = turn(wide_ref[pl.ds(head, block_len, stride=stride), :], cosine, sine)
            value = wide_ref[pl.ds(heads + head, block_len, stride=stride), :]
            begin = head * 2 * dim
            key_ref[head, at, :] = jnp.where(renewed, fresh[:, begin : begin + dim], key).astype(
                jnp.bfloat16
            )
            value_ref[head, at, :] = jnp.where(
                renewed, fresh[:, begin + dim : begin + 2 * dim], value
            ).astype(jnp.bfloat16)
        return carry

    lax.fori_loop(0, found, load, 0)
    list_ref[found] = far

    @pl.when(found % 2 == 1)
    def _():
        at = pl.ds(pl.multiple_of(found * block_len, block_len), block_len)
        for head in range(heads):
            key_ref[head, at, :] = jnp.zeros((block_len, dim), jnp.bfloat16)
            value_ref[head, at, :] = jnp.zeros((block_len, dim), jnp.bfloat16)

    pairs = (found + 1) // 2

    def per_tile(tile, carry):
        def reach(pair, tally):
            early = list_ref[2 * pair]
            late = list_ref[2 * pair + 1]
            begins = meta_ref[bounds_at + early] < (tile + 1) * tile_rows
            past = (late < blocks) & (
                meta_ref[bounds_at + jnp.minimum(late, blocks - 1) + 1] <= tile * tile_rows
            )
            return tally[0] + begins.astype(jnp.int32), tally[1] + past.astype(jnp.int32)

        active, clear = lax.fori_loop(0, pairs, reach, (jnp.int32(0), jnp.int32(0)))
        clear = jnp.minimum(clear, active)

        def score(pair, masked, most):
            at = pl.ds(pl.multiple_of(pair * 2 * block_len, 2 * block_len), 2 * block_len)
            if masked:
                row_at = pl.ds(pl.multiple_of(tile * tile_rows, tile_rows), tile_rows)
                lane = lax.broadcasted_iota(jnp.int32, (tile_rows, block_len), 1)
                row_pos = row_ref[row_at, :]
                seen = jnp.concatenate(
                    [
                        lane + list_ref[2 * pair + side] * block_len <= row_pos
                        for side in range(2)
                    ],
                    axis=1,
                )
            after = []
            for head in range(heads):
                scores = lax.dot_general(
                    turned_ref[head, tile],
                    key_ref[head, at, :],
                    (((1,), (1,)), ((), ())),
                    preferred_element_type=jnp.float32,
                )
                if masked:
                    scores = jnp.where(
                        seen[None], scores.reshape(group, tile_rows, 2 * block_len), 2 * low
                    ).reshape(lanes_rows, 2 * block_len)
                score_ref[head, pair] = scores
                after.append(
                    jnp.maximum(
                        most[head],
                        jnp.maximum(scores[:, :block_len], scores[:, block_len:]),
                    )
                )
            return tuple(after)

        start = tuple(jnp.full((lanes_rows, block_len), low, jnp.float32) for _ in range(heads))
        most = lax.fori_loop(0, clear, lambda pair, now: score(pair, False, now), start)
        most = lax.fori_loop(clear, active, lambda pair, now: score(pair, True, now), most)
        tops = []
        begun = []
        for head in range(heads):
            top = jnp.broadcast_to(jnp.max(most[head], axis=1, keepdims=True), (lanes_rows, dim))
            if first:
                begun.append(jnp.zeros((lanes_rows, dim), jnp.float32))
                begun.append(jnp.zeros((lanes_rows, dim), jnp.float32))
            else:
                before = most_in[head, tile]
                top = jnp.maximum(top, before)
                shrink = jnp.exp2((before - top) * scale)
                begun.append(sum_in[head, tile] * shrink)
                begun.append(acc_in[head, tile] * shrink)
            tops.append(top)

        def gather(pair, now):
            at = pl.ds(pl.multiple_of(pair * 2 * block_len, 2 * block_len), 2 * block_len)
            after = []
            for head in range(heads):
                scores = score_ref[head, pair]
                left = jnp.exp2((scores[:, :block_len] - tops[head]) * scale)
                right = jnp.exp2((scores[:, block_len:] - tops[head]) * scale)
                after.append(now[2 * head] + (left + right))
                weights = jnp.concatenate(
                    [left.astype(jnp.bfloat16), right.astype(jnp.bfloat16)], axis=1
                )
                after.append(
                    now[2 * head + 1]
                    + jnp.dot(
                        weights, value_ref[head, at, :], preferred_element_type=jnp.float32
                    )
                )
            return tuple(after)

        ended = lax.fori_loop(0, active, gather, tuple(begun))
        for head in range(heads):
            if last:
                total = jnp.sum(ended[2 * head], axis=1, keepdims=True)
                result = (ended[2 * head + 1] / total).astype(jnp.bfloat16)
                row_at = pl.ds(pl.multiple_of(tile * tile_rows, tile_rows), tile_rows)
                for member in range(group):
                    column = (head * group + member) * dim
                    out_ref[row_at, column : column + dim] = result[
                        member * tile_rows : (member + 1) * tile_rows
                    ]
            else:
                most_out[head, tile] = tops[head]
                sum_out[head, tile] = ended[2 * head]
                acc_out[head, tile] = ended[2 * head + 1]
        return carry

    lax.fori_loop(0, tiles, per_tile, 0)


def on_device(count, store_kv, block_owner, block_slot, span_len, row_index, fresh_q, fresh_kv):
    stored, block_len, heads, pair_width = store_kv.shape
    dim = pair_width // 2
    blocks = block_slot.shape[1]
    rows = row_index.shape[1]
    group = fresh_q.shape[2] // (heads * dim)
    tiles = rows // tile_rows
    lanes_rows = tile_rows * group
    raw_rows = block_len * 2 * heads

    def flat(array):
        lead = math.prod(array.shape[:-2])
        split = array.reshape(lead, heads, 2, dim)
        return split.transpose(0, 2, 1, 3).reshape(lead * 2 * heads, dim)

    place = lax.axis_index("req")
    store = flat(store_kv)
    none = jnp.int32(-(1 << 16))
    if count == 4:
        outer = [(0, 1), (1, 0), (2, 3), (3, 2)]
        inner = [(1, 2), (2, 1)]
        outward = [(1, 0), (2, 3)]
        send = lambda array, pairs: lax.ppermute(array, "req", pairs)
        beside = send(store, outer)
        across = send(store, inner)
        second = send(across, outward)
        third_in = send(beside, inner)
        third = send(third_in, outward)
        middle = (place == 1) | (place == 2)
        far_two = jnp.where(place == 0, 2, 1)
        far_three = jnp.where(place == 0, 3, 0)
        phases = [
            ((store, place, 1), (beside, place ^ 1, 1)),
            (
                (second, jnp.where(middle, none, far_two), 1),
                (across, jnp.where(middle, 3 - place, none), 1),
            ),
            (
                (third, jnp.where(middle, none, far_three), 1),
                (third_in, jnp.where(middle, (3 - place) ^ 1, none), 1),
            ),
        ]
    else:
        everything = lax.all_gather(store, "req", axis=0, tiled=True)
        phases = [((everything, jnp.int32(0), count),)]

    row_pos = row_index[0]
    bounds = jnp.sum(
        row_pos[None, :] < block_len * jnp.arange(blocks + 1, dtype=jnp.int32)[:, None],
        axis=1,
        dtype=jnp.int32,
    )
    row_cos, row_sin = tables(row_pos.astype(jnp.float32), dim)
    offset = span_offsets(span_len[0], blocks, block_len)
    cos, sin = tables(offset.astype(jnp.float32), dim)
    row_lanes = jnp.broadcast_to(row_pos[:, None], (rows, block_len))
    turned, placed = pl.pallas_call(
        prepare,
        out_shape=(
            jax.ShapeDtypeStruct((heads, tiles, lanes_rows, dim), jnp.bfloat16),
            jax.ShapeDtypeStruct((blocks, block_len, heads * 2 * dim + dim), jnp.bfloat16),
        ),
        in_specs=[vmem] * 5,
        out_specs=(vmem, vmem),
        scratch_shapes=[
            pltpu.VMEM((rows * 2 * heads, dim), jnp.float32),
            pltpu.VMEM((rows, heads * 2 * dim + dim), jnp.bfloat16),
        ],
        compiler_params=params,
        name="prepare",
    )(fresh_q[0], flat(fresh_kv), row_cos, row_sin, row_pos[None])
    state_shape = jax.ShapeDtypeStruct((heads, tiles, lanes_rows, dim), jnp.float32)
    state = ()
    for number, phase in enumerate(phases):
        begin = number == 0
        end = number == len(phases) - 1
        meta = jnp.concatenate(
            [block_owner[0, :, 0], block_slot[0], bounds, jnp.stack([entry[1] for entry in phase])]
        )
        inputs = [entry[0] for entry in phase] + [meta, turned, placed, cos, sin, row_lanes]
        specs = [anywhere] * len(phase) + [smem] + [vmem] * 5
        most = blocks if len(phases) == 1 else min(blocks, 24)
        state = pl.pallas_call(
            functools.partial(
                attend, tuple(entry[2] for entry in phase), blocks, stored, begin, end
            ),
            out_shape=jax.ShapeDtypeStruct((rows, heads * group * dim), jnp.bfloat16)
            if end
            else (state_shape,) * 3,
            in_specs=specs + [vmem] * len(state),
            out_specs=vmem if end else (vmem,) * 3,
            scratch_shapes=[
                pltpu.VMEM((most, raw_rows, dim), jnp.bfloat16),
                pltpu.VMEM((raw_rows, dim), jnp.float32),
                pltpu.VMEM((heads, (most + 2) * block_len, dim), jnp.bfloat16),
                pltpu.VMEM((heads, (most + 2) * block_len, dim), jnp.bfloat16),
                pltpu.VMEM((heads, most // 2 + 1, lanes_rows, 2 * block_len), jnp.float32),
                pltpu.SMEM((most + 2,), jnp.int32),
                pltpu.SemaphoreType.DMA((most,)),
            ],
            compiler_params=params,
            name=f"attend_{number}",
        )(*inputs, *state)
    return state[None]


def solution(mesh):
    placed = (
        P(("grp", "req"), None, "kvh", None),
        P(("grp", "req"), None, None),
        P(("grp", "req"), None),
        P(("grp", "req"), None),
        P(("grp", "req"), None),
        P(("grp", "req"), None, "kvh"),
        P(("grp", "req"), None, "kvh", None),
    )
    return jax.shard_map(
        functools.partial(on_device, mesh.shape["req"]),
        mesh=mesh,
        in_specs=placed,
        out_specs=P(("grp", "req"), None, "kvh"),
        check_vma=False,
    )
```

```python
import functools
import math

import jax
import jax.numpy as jnp
from jax import lax
from jax.experimental import pallas as pl
from jax.experimental.pallas import tpu as pltpu
from jax.sharding import PartitionSpec as P

rope_base = 500000.0
tile_rows = 64
unit_blocks = 6
low = -1e30
vmem = pl.BlockSpec(memory_space=pltpu.VMEM)
smem = pl.BlockSpec(memory_space=pltpu.SMEM)
params = pltpu.CompilerParams(vmem_limit_bytes=28 << 20)


def near(array):
    return pltpu.with_memory_space_constraint(array, pltpu.VMEM)


def tables(position, head_dim):
    lane = lax.broadcasted_iota(jnp.int32, (position.shape[0], head_dim), 1)
    half_dim = head_dim // 2
    pair_index = (lane % half_dim).astype(jnp.float32)
    inv_freq = jnp.exp(pair_index * (-2.0 / head_dim) * jnp.log(jnp.float32(rope_base)))
    angles = position[:, None] * inv_freq
    sine = jnp.sin(angles)
    return jnp.cos(angles), jnp.where(lane < half_dim, -sine, sine)


def turn(field, cosine, sine):
    return field * cosine + pltpu.roll(field, field.shape[1] // 2, 1) * sine


def prepare(query_ref, fresh_ref, cos_ref, sin_ref, pos_ref, turned_ref, placed_ref, wide_ref, all_ref):
    heads, tiles, lanes_rows, dim = turned_ref.shape
    group = lanes_rows // tile_rows
    placed_rows = placed_ref.shape[0]
    rows = cos_ref.shape[0]

    def turn_tile(tile, carry):
        at = pl.ds(pl.multiple_of(tile * tile_rows, tile_rows), tile_rows)
        cosine = cos_ref[at, :]
        sine = sin_ref[at, :]
        for head in range(heads):
            for member in range(group):
                column = (head * group + member) * dim
                field = query_ref[at, column : column + dim].astype(jnp.float32)
                turned_ref[head, tile, member * tile_rows : (member + 1) * tile_rows, :] = turn(
                    field, cosine, sine
                ).astype(jnp.bfloat16)
        return carry

    lax.fori_loop(0, tiles, turn_tile, 0)
    wide_ref[...] = fresh_ref[...].astype(jnp.float32)
    for head in range(heads):
        key = wide_ref[pl.ds(head, rows, stride=2 * heads), :]
        value = wide_ref[pl.ds(heads + head, rows, stride=2 * heads), :]
        all_ref[:, head * 2 * dim : head * 2 * dim + dim] = turn(
            key, cos_ref[...], sin_ref[...]
        ).astype(jnp.bfloat16)
        all_ref[:, head * 2 * dim + dim : (head + 1) * 2 * dim] = value.astype(jnp.bfloat16)
    all_ref[:, heads * 2 * dim :] = jnp.ones((rows, dim), jnp.bfloat16)
    step = 512

    def place(number, carry):
        at = pl.ds(pl.multiple_of(number * step, step), step)
        spot = lax.broadcasted_iota(jnp.int32, (step, rows), 0) + number * step
        chosen = jnp.where(spot == pos_ref[...], 1.0, 0.0).astype(jnp.bfloat16)
        placed_ref[at, :] = jnp.dot(
            chosen, all_ref[...], preferred_element_type=jnp.float32
        ).astype(jnp.bfloat16)
        return carry

    lax.fori_loop(0, placed_rows // step, place, 0)


def attend(spans, shards, pick, units, first, last, *refs):
    given = len(pick)
    sources = refs[:given]
    place_ref, owner_ref, slot_ref, span_ref, pos_ref = refs[given : given + 5]
    turned_ref, placed_ref, cos_ref, sin_ref, row_ref = refs[given + 5 : given + 10]
    refs = refs[given + 10 :]
    if not first:
        most_in, sum_in, acc_in = refs[:3]
        refs = refs[3:]
    if last:
        out_ref = refs[0]
        refs = refs[1:]
    else:
        most_out, sum_out, acc_out = refs[:3]
        refs = refs[3:]
    wide_ref, key_ref, value_ref, list_ref = refs[:4]
    if last and units > 1:
        most_out, sum_out, acc_out = refs[4:]
    heads, tiles, lanes_rows, dim = turned_ref.shape
    group = lanes_rows // tile_rows
    blocks = slot_ref.shape[1]
    block_len = placed_ref.shape[0] // blocks
    stride = 2 * heads
    raw_rows = block_len * stride
    slots = sources[0].shape[0] // raw_rows // shards
    scale = dim**-0.5 * math.log2(math.e)
    lowest = [choose(place_ref[0]) for choose in pick]

    def find(block, found):
        owner = owner_ref[0, block]
        hit = jnp.bool_(False)
        for base in lowest:
            hit = hit | ((owner >= base) & (owner < base + shards))
        list_ref[found] = block
        return found + hit.astype(jnp.int32)

    lax.fori_loop(0, blocks, find, jnp.int32(0))

    def load(spot, carry):
        block = list_ref[spot]
        owner = owner_ref[0, block]
        for source, base in zip(sources, lowest):

            @pl.when((owner >= base) & (owner < base + shards))
            def _(source=source, base=base):
                start = ((owner - base) * slots + slot_ref[0, block]) * raw_rows
                wide_ref[...] = source[pl.ds(pl.multiple_of(start, raw_rows), raw_rows), :].astype(
                    jnp.float32
                )

        began = jnp.int32(0)
        start = jnp.int32(0)
        for span in range(spans):
            began = jnp.where(start <= block, start, began)
            start = start + span_ref[0, span]
        cosine = cos_ref[pl.ds(began, 1), :]
        sine = sin_ref[pl.ds(began, 1), :]
        fresh = placed_ref[
            pl.ds(pl.multiple_of(block * block_len, block_len), block_len), :
        ].astype(jnp.float32)
        renewed = fresh[:, heads * 2 * dim :] > 0.5
        at = pl.ds(pl.multiple_of(spot * block_len, block_len), block_len)
        for head in range(heads):
            key = turn(wide_ref[pl.ds(head, block_len, stride=stride), :], cosine, sine)
            value = wide_ref[pl.ds(heads + head, block_len, stride=stride), :]
            begin = head * 2 * dim
            key_ref[head, at, :] = jnp.where(renewed, fresh[:, begin : begin + dim], key).astype(
                jnp.bfloat16
            )
            value_ref[head, at, :] = jnp.where(
                renewed, fresh[:, begin + dim : begin + 2 * dim], value
            ).astype(jnp.bfloat16)
        return carry

    lax.fori_loop(0, units * unit_blocks, load, 0)

    def write(head, tile, state):
        most, total, acc = state
        most_out[head, tile] = most
        sum_out[head, tile] = total
        acc_out[head, tile] = acc

    def extend(tile, unit, count, before, after):
        row_at = pl.ds(pl.multiple_of(tile * tile_rows, tile_rows), tile_rows)
        row_pos = row_ref[row_at, :]
        lane = lax.broadcasted_iota(jnp.int32, (tile_rows, block_len), 1)
        first_spot = unit * unit_blocks
        seen = [
            lane + list_ref[first_spot + spot] * block_len <= row_pos for spot in range(count)
        ]
        at = pl.ds(first_spot * block_len, count * block_len)
        for head in range(heads):
            scores = lax.dot_general(
                turned_ref[head, tile],
                key_ref[head, at, :],
                (((1,), (1,)), ((), ())),
                preferred_element_type=jnp.float32,
            )
            parts = [
                jnp.where(
                    seen[spot][None],
                    scores[:, spot * block_len : (spot + 1) * block_len].reshape(
                        group, tile_rows, block_len
                    ),
                    2 * low,
                ).reshape(lanes_rows, block_len)
                for spot in range(count)
            ]
            most = functools.reduce(jnp.maximum, parts)
            most = jnp.broadcast_to(
                jnp.maximum(jnp.max(most, axis=1, keepdims=True), low), (lanes_rows, block_len)
            )
            if before is not None:
                was_most, was_sum, was_acc = [ref[head, tile] for ref in before]
                most = jnp.maximum(most, was_most)
            parts = [jnp.exp2((part - most) * scale) for part in parts]
            total = functools.reduce(jnp.add, parts)
            acc = jnp.dot(
                jnp.concatenate([part.astype(jnp.bfloat16) for part in parts], axis=1),
                value_ref[head, at, :],
                preferred_element_type=jnp.float32,
            )
            if before is not None:
                shrink = jnp.exp2((was_most - most) * scale)
                total = was_sum * shrink + total
                acc = was_acc * shrink + acc
            after(head, tile, (most, total, acc))

    def finish(head, tile, state):
        most, total, acc = state
        result = (acc / jnp.sum(total, axis=1, keepdims=True)).astype(jnp.bfloat16)
        row_at = pl.ds(pl.multiple_of(tile * tile_rows, tile_rows), tile_rows)
        for member in range(group):
            column = (head * group + member) * dim
            out_ref[row_at, column : column + dim] = result[
                member * tile_rows : (member + 1) * tile_rows
            ]

    def keep(tile, before, after):
        for head in range(heads):
            if before is None:
                nothing = jnp.zeros((lanes_rows, dim), jnp.float32)
                after(head, tile, (nothing + low, nothing, nothing))
            else:
                after(head, tile, tuple(ref[head, tile] for ref in before))

    def per_tile(tile, carry):
        furthest = pos_ref[0, (tile + 1) * tile_rows - 1]
        for unit in range(units):
            ends = last and unit == units - 1
            fresh = first and unit == 0
            if fresh:
                before = None
            elif unit == 0:
                before = (most_in, sum_in, acc_in)
            else:
                before = (most_out, sum_out, acc_out)
            active = jnp.int32(0)
            for spot in range(unit_blocks):
                begins = list_ref[unit * unit_blocks + spot] * block_len
                active = active + (begins <= furthest).astype(jnp.int32)
            after = finish if ends else write
            for count in range(0, unit_blocks + 1, 2):

                @pl.when((active + 1) // 2 == count // 2)
                def _(count=count):
                    if count:
                        extend(tile, unit, count, before, after)
                    elif fresh or ends:
                        keep(tile, before, after)

        return carry

    lax.fori_loop(0, tiles, per_tile, 0)


def on_device(count, store_kv, block_owner, block_slot, span_len, row_index, fresh_q, fresh_kv):
    stored, block_len, heads, pair_width = store_kv.shape
    dim = pair_width // 2
    blocks = block_slot.shape[1]
    rows = row_index.shape[1]
    group = fresh_q.shape[2] // (heads * dim)
    tiles = rows // tile_rows
    lanes_rows = tile_rows * group
    raw_rows = block_len * 2 * heads

    def flat(array):
        lead = math.prod(array.shape[:-2])
        split = array.reshape(lead, heads, 2, dim)
        return split.transpose(0, 2, 1, 3).reshape(lead * 2 * heads, dim)

    store = flat(store_kv)
    place = lax.axis_index("req").reshape(1)
    row_pos = row_index[0]
    row_cos, row_sin = tables(row_pos.astype(jnp.float32), dim)
    cos, sin = tables(block_len * jnp.arange(blocks, dtype=jnp.float32), dim)
    row_lanes = jnp.broadcast_to(row_pos[:, None], (rows, block_len))
    turned, placed = pl.pallas_call(
        prepare,
        out_shape=(
            pltpu.VMEM((heads, tiles, lanes_rows, dim), jnp.bfloat16),
            pltpu.VMEM((blocks * block_len, heads * 2 * dim + dim), jnp.bfloat16),
        ),
        in_specs=[vmem] * 5,
        out_specs=(vmem, vmem),
        scratch_shapes=[
            pltpu.VMEM((rows * 2 * heads, dim), jnp.float32),
            pltpu.VMEM((rows, heads * 2 * dim + dim), jnp.bfloat16),
        ],
        compiler_params=params,
        name="prepare",
    )(fresh_q[0], flat(fresh_kv), row_cos, row_sin, row_index)

    def attention(number, last, sources, pick, shards, units, state):
        first = not state
        state_shape = pltpu.VMEM((heads, tiles, lanes_rows, dim), jnp.float32)
        inputs = [near(source) for source in sources]
        inputs += [place, block_owner[:, :, 0], block_slot, span_len, row_index]
        inputs += [near(turned), near(placed), cos, sin, row_lanes]
        specs = [vmem] * len(sources) + [smem] * 5 + [vmem] * 5
        spots = units * unit_blocks
        return pl.pallas_call(
            functools.partial(attend, span_len.shape[1], shards, pick, units, first, last),
            out_shape=jax.ShapeDtypeStruct((rows, heads * group * dim), jnp.bfloat16)
            if last
            else (state_shape,) * 3,
            in_specs=specs + [vmem] * len(state),
            out_specs=vmem if last else (vmem,) * 3,
            input_output_aliases={}
            if last or first
            else {len(specs) + entry: entry for entry in range(3)},
            scratch_shapes=[
                pltpu.VMEM((raw_rows, dim), jnp.float32),
                pltpu.VMEM((heads, spots * block_len, dim), jnp.bfloat16),
                pltpu.VMEM((heads, spots * block_len, dim), jnp.bfloat16),
                pltpu.SMEM((blocks + 1,), jnp.int32),
            ]
            + ([pltpu.VMEM((heads, tiles, lanes_rows, dim), jnp.float32)] * 3 if last and units > 1 else []),
            compiler_params=params,
            name=f"attend_{number}",
        )(*inputs, *[near(entry) for entry in state])

    if count != 4:
        everything = lax.all_gather(store, "req", axis=0, tiled=True)
        units = blocks // unit_blocks
        state = ()
        result = attention(0, True, [everything], [lambda at: 0], count, units, state)
        return result[None]
    outer = [(0, 1), (1, 0), (2, 3), (3, 2)]
    inner = [(1, 2), (2, 1)]
    outward = [(1, 0), (2, 3)]
    none = -(1 << 16)
    is_end = lambda at: (at == 0) | (at == 3)

    def send(array, pairs):
        return lax.ppermute(array, "req", pairs)

    beside = send(store, outer)
    across = send(store, inner)
    state = attention(0, False, [store], [lambda at: at], 1, 1, ())
    beside, across, state = lax.optimization_barrier((beside, across, state))
    second = send(across, outward)
    third_in = send(beside, inner)
    state = attention(1, False, [beside], [lambda at: at ^ 1], 1, 1, state)
    second, third_in, state = lax.optimization_barrier((second, third_in, state))
    third = send(third_in, outward)
    state = attention(
        2,
        False,
        [second, across],
        [
            lambda at: jnp.where(is_end(at), jnp.where(at == 0, 2, 1), none),
            lambda at: jnp.where(is_end(at), none, 3 - at),
        ],
        1,
        1,
        state,
    )
    third, state = lax.optimization_barrier((third, state))
    result = attention(
        3,
        True,
        [third, third_in],
        [
            lambda at: jnp.where(is_end(at), 3 - at, none),
            lambda at: jnp.where(is_end(at), none, (3 - at) ^ 1),
        ],
        1,
        1,
        state,
    )
    return result[None]


def solution(mesh):
    placed = (
        P(("grp", "req"), None, "kvh", None),
        P(("grp", "req"), None, None),
        P(("grp", "req"), None),
        P(("grp", "req"), None),
        P(("grp", "req"), None),
        P(("grp", "req"), None, "kvh"),
        P(("grp", "req"), None, "kvh", None),
    )
    return jax.shard_map(
        functools.partial(on_device, mesh.shape["req"]),
        mesh=mesh,
        in_specs=placed,
        out_specs=P(("grp", "req"), None, "kvh"),
        check_vma=False,
    )
```

```python
import functools
import math

import jax
import jax.numpy as jnp
from jax import lax
from jax.experimental import pallas as pl
from jax.experimental.pallas import tpu as pltpu
from jax.sharding import PartitionSpec as P

rope_base = 500000.0
tile_rows = 64
unit_blocks = 6
low = -1e30
bound = 105.0
grain = 2
chunk = 3
vmem = pl.BlockSpec(memory_space=pltpu.VMEM)
smem = pl.BlockSpec(memory_space=pltpu.SMEM)
anywhere = pl.BlockSpec(memory_space=pl.ANY)
params = pltpu.CompilerParams(vmem_limit_bytes=28 << 20)


def near(array):
    return pltpu.with_memory_space_constraint(array, pltpu.VMEM)


def held(array):
    return pltpu.with_memory_space_constraint(array, pltpu.SMEM)


def away(array):
    return pltpu.with_memory_space_constraint(array, pltpu.HBM)


def tables(position, head_dim):
    lane = lax.broadcasted_iota(jnp.int32, (position.shape[0], head_dim), 1)
    half_dim = head_dim // 2
    pair_index = (lane % half_dim).astype(jnp.float32)
    inv_freq = jnp.exp(pair_index * (-2.0 / head_dim) * jnp.log(jnp.float32(rope_base)))
    angles = position[:, None] * inv_freq
    sine = jnp.sin(angles)
    return jnp.cos(angles), jnp.where(lane < half_dim, -sine, sine)


def turn(field, cosine, sine):
    return field * cosine + pltpu.roll(field, field.shape[1] // 2, 1) * sine


def prepare(
    query_ref, fresh_ref, store_ref, owner_ref, slot_ref, span_ref, pos_ref, place_ref, cos_ref, sin_ref,
    turned_ref, placed_ref, near_ref, table_ref, peak_ref,
    raw_ref, flat_ref, wide_ref, all_ref, lanes_ref, row_smem, owner_smem, slot_smem, span_smem, sems,
):
    heads, tiles, lanes_rows, dim = turned_ref.shape
    group = lanes_rows // tile_rows
    placed_rows = placed_ref.shape[0]
    rows = cos_ref.shape[0]
    blocks = slot_ref.shape[1]

    def load_query(tile):
        at = pl.ds(pl.multiple_of(tile * tile_rows, tile_rows), tile_rows)
        return pltpu.make_async_copy(query_ref.at[at, :], raw_ref.at[at, :], sems.at[tile])

    small = [
        pltpu.make_async_copy(source, target, sems.at[tiles + number])
        for number, (source, target) in enumerate(
            (
                (pos_ref, lanes_ref),
                (fresh_ref, flat_ref),
                (pos_ref, row_smem),
                (owner_ref, owner_smem),
                (slot_ref, slot_smem),
                (span_ref, span_smem),
                (store_ref, near_ref),
            )
        )
    ]
    for copy in small[:-1]:
        copy.start()
    for tile in range(tiles):
        load_query(tile).start()
    small[-1].start()
    for copy in small[:-1]:
        copy.wait()
    wide_ref[...] = flat_ref[...].astype(jnp.float32)
    for head in range(heads):
        key = wide_ref[pl.ds(head, rows, stride=2 * heads), :]
        value = wide_ref[pl.ds(heads + head, rows, stride=2 * heads), :]
        all_ref[:, head * 2 * dim : head * 2 * dim + dim] = turn(
            key, cos_ref[...], sin_ref[...]
        ).astype(jnp.bfloat16)
        all_ref[:, head * 2 * dim + dim : (head + 1) * 2 * dim] = value.astype(jnp.bfloat16)
    all_ref[:, heads * 2 * dim :] = jnp.ones((rows, dim), jnp.bfloat16)
    step = 512

    def place(number, carry):
        at = pl.ds(pl.multiple_of(number * step, step), step)
        spot = lax.broadcasted_iota(jnp.int32, (step, rows), 0) + number * step
        chosen = jnp.where(spot == lanes_ref[...], 1.0, 0.0).astype(jnp.bfloat16)
        placed_ref[at, :] = jnp.dot(
            chosen, all_ref[...], preferred_element_type=jnp.float32
        ).astype(jnp.bfloat16)
        return carry

    lax.fori_loop(0, placed_rows // step, place, 0)

    def note(block, carry):
        began = jnp.int32(0)
        start = jnp.int32(0)
        for span in range(span_ref.shape[1]):
            began = jnp.where(start <= block, start, began)
            start = start + span_smem[0, span]
        table_ref[block] = owner_smem[0, block]
        table_ref[blocks + block] = slot_smem[0, block]
        table_ref[2 * blocks + block] = began
        return carry

    lax.fori_loop(0, blocks, note, 0)
    for tile in range(tiles):
        table_ref[3 * blocks + tile] = row_smem[0, (tile + 1) * tile_rows - 1]
    table_ref[3 * blocks + tiles] = place_ref[0]
    ones = jnp.ones((dim, dim), jnp.bfloat16)

    def turn_tile(tile, peak):
        load_query(tile).wait()
        at = pl.ds(pl.multiple_of(tile * tile_rows, tile_rows), tile_rows)
        cosine = cos_ref[at, :]
        sine = sin_ref[at, :]
        for head in range(heads):
            squares = []
            for member in range(group):
                column = (head * group + member) * dim
                field = raw_ref[at, column : column + dim].astype(jnp.float32)
                turned_ref[head, tile, member * tile_rows : (member + 1) * tile_rows, :] = turn(
                    field, cosine, sine
                ).astype(jnp.bfloat16)
                squares.append((field * field).astype(jnp.bfloat16))
            lengths = jnp.dot(
                jnp.concatenate(squares, axis=0), ones, preferred_element_type=jnp.float32
            )
            peak = jnp.maximum(peak, jnp.max(lengths.reshape(-1, 8, dim), axis=0))
        return peak

    peak = lax.fori_loop(0, tiles, turn_tile, jnp.zeros((8, dim), jnp.float32))
    peak_ref[0] = jnp.max(peak)
    small[-1].wait()


def attend(shards, pick, units, first, last, *refs):
    given = len(pick)
    sources = refs[:given]
    table_ref, calm_in, turned_ref, placed_ref, cos_ref, sin_ref, row_ref = refs[given : given + 7]
    refs = refs[given + 7 :]
    if not first:
        most_in, sum_in, acc_in = refs[:3]
        refs = refs[3:]
    most_out, sum_out, acc_out, calm_out = refs[:4]
    refs = refs[4:]
    if last:
        out_ref = refs[0]
        refs = refs[1:]
    wide_ref, key_ref, value_ref, list_ref = refs
    heads, tiles, lanes_rows, dim = turned_ref.shape
    group = lanes_rows // tile_rows
    blocks = cos_ref.shape[0]
    block_len = placed_ref.shape[0] // blocks
    stride = 2 * heads
    raw_rows = block_len * stride
    slots = sources[0].shape[0] // raw_rows // shards
    scale = dim**-0.5 * math.log2(math.e)
    lowest = [choose(table_ref[3 * blocks + tiles]) for choose in pick]
    spots = units * unit_blocks

    def find(block, found):
        owner = table_ref[block]
        hit = jnp.bool_(False)
        for base in lowest:
            hit = hit | ((owner >= base) & (owner < base + shards))
        list_ref[found] = block
        return found + hit.astype(jnp.int32)

    lax.fori_loop(0, blocks, find, jnp.int32(0))
    ones = jnp.ones((dim, dim), jnp.bfloat16)

    def load(turn_number, peak):
        for lane in range(chunk):
            spot = turn_number * chunk + lane
            block = list_ref[spot]
            owner = table_ref[block]
            raw = None
            for source, base in zip(sources, lowest):
                here = (owner >= base) & (owner < base + shards)
                start = ((owner - base) * slots + table_ref[blocks + block]) * raw_rows
                start = pl.multiple_of(jnp.where(here, start, 0), raw_rows)
                found = source[pl.ds(start, raw_rows), :].astype(jnp.float32)
                raw = found if raw is None else jnp.where(here, found, raw)
            wide_ref[lane] = raw
            began = table_ref[2 * blocks + block]
            cosine = cos_ref[pl.ds(began, 1), :]
            sine = sin_ref[pl.ds(began, 1), :]
            fresh = placed_ref[
                pl.ds(pl.multiple_of(block * block_len, block_len), block_len), :
            ].astype(jnp.float32)
            renewed = fresh[:, heads * 2 * dim :] > 0.5
            at = pl.ds(pl.multiple_of(spot * block_len, block_len), block_len)
            for head in range(heads):
                key = turn(wide_ref[lane, pl.ds(head, block_len, stride=stride), :], cosine, sine)
                value = wide_ref[lane, pl.ds(heads + head, block_len, stride=stride), :]
                begin = head * 2 * dim
                key = jnp.where(renewed, fresh[:, begin : begin + dim], key)
                key_ref[head, at, :] = key.astype(jnp.bfloat16)
                value_ref[head, at, :] = jnp.where(
                    renewed, fresh[:, begin + dim : begin + 2 * dim], value
                ).astype(jnp.bfloat16)
                lengths = jnp.dot(
                    (key * key).astype(jnp.bfloat16), ones, preferred_element_type=jnp.float32
                )
                peak = jnp.maximum(peak, jnp.max(lengths.reshape(-1, 8, dim), axis=0))
        return peak

    peak = lax.fori_loop(0, spots // chunk, load, jnp.zeros((8, dim), jnp.float32))
    room = (calm_in[0] < 1e38) & (calm_in[0] * jnp.max(peak) <= (bound / scale) ** 2)
    calm = room.astype(jnp.float32)
    calm_out[0] = jnp.where(room, calm_in[0], jnp.float32(3e38))

    def query_mask(tile):
        row_at = pl.ds(pl.multiple_of(tile * tile_rows, tile_rows), tile_rows)
        row_pos = row_ref[row_at, :]
        lane = lax.broadcasted_iota(jnp.int32, (tile_rows, block_len), 1)
        return lambda spot: (lane + list_ref[spot] * block_len <= row_pos)[None]

    def scored(head, tile, first_spot, count, seen):
        at = pl.ds(pl.multiple_of(first_spot * block_len, block_len), count * block_len)
        scores = lax.dot_general(
            turned_ref[head, tile],
            key_ref[head, at, :],
            (((1,), (1,)), ((), ())),
            preferred_element_type=jnp.float32,
        )
        return at, [
            jnp.where(
                seen[spot],
                scores[:, spot * block_len : (spot + 1) * block_len].reshape(
                    group, tile_rows, block_len
                ),
                2 * low,
            ).reshape(lanes_rows, block_len)
            for spot in range(count)
        ]

    def weighed(head, at, parts):
        return functools.reduce(jnp.add, parts), jnp.dot(
            jnp.concatenate([part.astype(jnp.bfloat16) for part in parts], axis=1),
            value_ref[head, at, :],
            preferred_element_type=jnp.float32,
        )

    def write(head, tile, total, acc):
        sum_out[head, tile] = total
        acc_out[head, tile] = acc

    def finish(head, tile, total, acc):
        result = (acc / jnp.sum(total, axis=1, keepdims=True)).astype(jnp.bfloat16)
        row_at = pl.ds(pl.multiple_of(tile * tile_rows, tile_rows), tile_rows)
        for member in range(group):
            column = (head * group + member) * dim
            out_ref[row_at, column : column + dim] = result[
                member * tile_rows : (member + 1) * tile_rows
            ]

    def quick(tile, carry):
        furthest = table_ref[3 * blocks + tile]
        visible = query_mask(tile)
        for unit in range(units):
            fresh = first and unit == 0
            ends = last and unit == units - 1
            before = (sum_in, acc_in) if unit == 0 and not first else (sum_out, acc_out)
            first_spot = unit * unit_blocks
            active = jnp.int32(0)
            for spot in range(unit_blocks):
                begins = list_ref[first_spot + spot] * block_len
                active = active + (begins <= furthest).astype(jnp.int32)
            after = finish if ends else write
            for count in range(0, unit_blocks + 1, grain):

                @pl.when((active + grain - 1) // grain == count // grain)
                def _(count=count):
                    if not count and not fresh and not ends:
                        return
                    seen = [visible(first_spot + spot) for spot in range(count)]
                    for head in range(heads):
                        total = acc = jnp.zeros((lanes_rows, dim), jnp.float32)
                        if count:
                            at, parts = scored(head, tile, first_spot, count, seen)
                            parts = [jnp.exp2(part * scale) for part in parts]
                            total, acc = weighed(head, at, parts)
                        if not fresh:
                            total = before[0][head, tile] + total
                            acc = before[1][head, tile] + acc
                        after(head, tile, total, acc)

        return carry

    def careful(tile, carry):
        furthest = table_ref[3 * blocks + tile]
        visible = query_mask(tile)

        def begin(head, ignored):
            if first:
                nothing = jnp.zeros((lanes_rows, dim), jnp.float32)
                most_out[head, tile] = nothing + low
                write(head, tile, nothing, nothing)
            else:
                total = sum_in[head, tile]
                most_out[head, tile] = jnp.where(
                    calm_in[0] < 1e38,
                    jnp.where(jnp.max(total, axis=1, keepdims=True) > 0, 0.0, low),
                    most_in[head, tile],
                )
                write(head, tile, total, acc_in[head, tile])
            return ignored

        lax.fori_loop(0, heads, begin, 0)

        def one(step, ignored):
            head = step % heads
            spot = step // heads

            @pl.when(list_ref[spot] * block_len <= furthest)
            def _():
                at, parts = scored(head, tile, spot, 1, [visible(spot)])
                was = most_out[head, tile]
                most = jnp.maximum(was, jnp.max(parts[0], axis=1, keepdims=True))
                total, acc = weighed(head, at, [jnp.exp2((parts[0] - most) * scale)])
                shrink = jnp.exp2((was - most) * scale)
                most_out[head, tile] = most
                write(
                    head,
                    tile,
                    sum_out[head, tile] * shrink + total,
                    acc_out[head, tile] * shrink + acc,
                )

            return ignored

        lax.fori_loop(0, spots * heads, one, 0)
        if last:
            for head in range(heads):
                finish(head, tile, sum_out[head, tile], acc_out[head, tile])
        return carry

    @pl.when(calm > 0.5)
    def _():
        lax.fori_loop(0, tiles, quick, 0)

    @pl.when(calm < 0.5)
    def _():
        lax.fori_loop(0, tiles, careful, 0)


def on_device(count, store_kv, block_owner, block_slot, span_len, row_index, fresh_q, fresh_kv):
    stored, block_len, heads, pair_width = store_kv.shape
    dim = pair_width // 2
    blocks = block_slot.shape[1]
    rows = row_index.shape[1]
    group = fresh_q.shape[2] // (heads * dim)
    tiles = rows // tile_rows
    lanes_rows = tile_rows * group
    raw_rows = block_len * 2 * heads

    def flat(array):
        lead = math.prod(array.shape[:-2])
        split = array.reshape(lead, heads, 2, dim)
        return split.transpose(0, 2, 1, 3).reshape(lead * 2 * heads, dim)

    store = flat(store_kv)
    place = lax.axis_index("req").reshape(1)
    row_pos = row_index[0]
    row_cos, row_sin = tables(row_pos.astype(jnp.float32), dim)
    cos, sin = tables(block_len * jnp.arange(blocks, dtype=jnp.float32), dim)
    row_lanes = jnp.broadcast_to(row_pos[:, None], (rows, block_len))
    wide = heads * 2 * dim + dim
    turned, placed, close, table, peak = pl.pallas_call(
        prepare,
        out_shape=(
            pltpu.VMEM((heads, tiles, lanes_rows, dim), jnp.bfloat16),
            pltpu.VMEM((blocks * block_len, wide), jnp.bfloat16),
            pltpu.VMEM(store.shape, jnp.bfloat16),
            pltpu.SMEM((3 * blocks + tiles + 1,), jnp.int32),
            pltpu.SMEM((1,), jnp.float32),
        ),
        in_specs=[anywhere] * 7 + [smem, vmem, vmem],
        out_specs=(vmem, vmem, vmem, smem, smem),
        scratch_shapes=[
            pltpu.VMEM((rows, heads * group * dim), jnp.bfloat16),
            pltpu.VMEM((rows * 2 * heads, dim), jnp.bfloat16),
            pltpu.VMEM((rows * 2 * heads, dim), jnp.float32),
            pltpu.VMEM((rows, wide), jnp.bfloat16),
            pltpu.VMEM((1, rows), jnp.int32),
            pltpu.SMEM((1, rows), jnp.int32),
            pltpu.SMEM((1, blocks), jnp.int32),
            pltpu.SMEM((1, blocks), jnp.int32),
            pltpu.SMEM(span_len.shape, jnp.int32),
            pltpu.SemaphoreType.DMA((tiles + 7,)),
        ],
        compiler_params=params,
        name="prepare",
    )(
        away(fresh_q[0]), away(flat(fresh_kv)), away(store), away(block_owner[:, :, 0]),
        away(block_slot), away(span_len), away(row_index), place, near(row_cos), near(row_sin),
    )

    def attention(number, last, sources, pick, shards, units, state):
        first = len(state) == 1
        state_shape = pltpu.VMEM((heads, tiles, lanes_rows, dim), jnp.float32)
        inputs = [near(source) for source in sources]
        inputs += [held(table), held(state[-1])]
        inputs += [near(array) for array in (turned, placed, cos, sin, row_lanes)]
        specs = [vmem] * len(sources) + [smem] * 2 + [vmem] * 5
        spots = units * unit_blocks
        result = [jax.ShapeDtypeStruct((rows, heads * group * dim), jnp.bfloat16)] if last else []
        return pl.pallas_call(
            functools.partial(attend, shards, pick, units, first, last),
            out_shape=[state_shape] * 3 + [pltpu.SMEM((1,), jnp.float32)] + result,
            in_specs=specs + [vmem] * (len(state) - 1),
            out_specs=[vmem] * 3 + [smem] + [vmem] * len(result),
            input_output_aliases={}
            if first
            else {len(specs) + entry: entry for entry in range(3)},
            scratch_shapes=[
                pltpu.VMEM((chunk, raw_rows, dim), jnp.float32),
                pltpu.VMEM((heads, spots * block_len, dim), jnp.bfloat16),
                pltpu.VMEM((heads, spots * block_len, dim), jnp.bfloat16),
                pltpu.SMEM((blocks + 1,), jnp.int32),
            ],
            compiler_params=params,
            name=f"attend_{number}",
        )(*inputs, *[near(entry) for entry in state[:-1]])

    if count != 4:
        everything = lax.all_gather(store, "req", axis=0, tiled=True)
        return attention(
            0, True, [everything], [lambda at: 0], count, blocks // unit_blocks, (peak,)
        )[-1][None]
    outer = [(0, 1), (1, 0), (2, 3), (3, 2)]
    inner = [(1, 2), (2, 1)]
    outward = [(1, 0), (2, 3)]
    none = -(1 << 16)
    is_end = lambda at: (at == 0) | (at == 3)

    def send(array, pairs):
        return lax.ppermute(array, "req", pairs)

    beside = send(store, outer)
    across = send(store, inner)
    beside, across, close, turned = lax.optimization_barrier((beside, across, close, turned))
    second = send(across, outward)
    third_in = send(beside, inner)
    state = attention(0, False, [close, beside], [lambda at: at, lambda at: at ^ 1], 1, 2, (peak,))
    second, third_in, state = lax.optimization_barrier((second, third_in, state))
    third = send(third_in, outward)
    state = attention(
        1,
        False,
        [second, across],
        [
            lambda at: jnp.where(is_end(at), jnp.where(at == 0, 2, 1), none),
            lambda at: jnp.where(is_end(at), none, 3 - at),
        ],
        1,
        1,
        state,
    )
    third, state = lax.optimization_barrier((third, state))
    return attention(
        2,
        True,
        [third, third_in],
        [
            lambda at: jnp.where(is_end(at), 3 - at, none),
            lambda at: jnp.where(is_end(at), none, (3 - at) ^ 1),
        ],
        1,
        1,
        state,
    )[-1][None]


def solution(mesh):
    placed = (
        P(("grp", "req"), None, "kvh", None),
        P(("grp", "req"), None, None),
        P(("grp", "req"), None),
        P(("grp", "req"), None),
        P(("grp", "req"), None),
        P(("grp", "req"), None, "kvh"),
        P(("grp", "req"), None, "kvh", None),
    )
    return jax.shard_map(
        functools.partial(on_device, mesh.shape["req"]),
        mesh=mesh,
        in_specs=placed,
        out_specs=P(("grp", "req"), None, "kvh"),
        check_vma=False,
    )
```

```python
import functools
import math

import jax
import jax.numpy as jnp
from jax import lax
from jax.experimental import pallas as pl
from jax.experimental.pallas import tpu as pltpu
from jax.sharding import PartitionSpec as P

rope_base = 500000.0
tile_rows = 64
unit_blocks = 6
low = -1e30
far = 1 << 20
cut = 2
bound = 105.0
grain = 2
chunk = 3
vmem = pl.BlockSpec(memory_space=pltpu.VMEM)
smem = pl.BlockSpec(memory_space=pltpu.SMEM)
anywhere = pl.BlockSpec(memory_space=pl.ANY)
params = pltpu.CompilerParams(vmem_limit_bytes=28 << 20)


def near(array):
    return pltpu.with_memory_space_constraint(array, pltpu.VMEM)


def held(array):
    return pltpu.with_memory_space_constraint(array, pltpu.SMEM)


def away(array):
    return pltpu.with_memory_space_constraint(array, pltpu.HBM)


def tables(position, head_dim):
    lane = lax.broadcasted_iota(jnp.int32, (position.shape[0], head_dim), 1)
    half_dim = head_dim // 2
    pair_index = (lane % half_dim).astype(jnp.float32)
    inv_freq = jnp.exp(pair_index * (-2.0 / head_dim) * jnp.log(jnp.float32(rope_base)))
    angles = position[:, None] * inv_freq
    sine = jnp.sin(angles)
    return jnp.cos(angles), jnp.where(lane < half_dim, -sine, sine)


def turn(field, cosine, sine):
    return field * cosine + pltpu.roll(field, field.shape[1] // 2, 1) * sine


def prepare(
    query_ref, fresh_ref, store_ref, owner_ref, slot_ref, span_ref, pos_ref, place_ref, cos_ref, sin_ref,
    turned_ref, placed_ref, near_ref, table_ref, peak_ref,
    raw_ref, flat_ref, wide_ref, all_ref, lanes_ref, row_smem, owner_smem, slot_smem, span_smem, sems,
):
    heads, tiles, lanes_rows, dim = turned_ref.shape
    group = lanes_rows // tile_rows
    placed_rows = placed_ref.shape[0]
    rows = cos_ref.shape[0]
    blocks = slot_ref.shape[1]

    def load_query(tile):
        at = pl.ds(pl.multiple_of(tile * tile_rows, tile_rows), tile_rows)
        return pltpu.make_async_copy(query_ref.at[at, :], raw_ref.at[at, :], sems.at[tile])

    small = [
        pltpu.make_async_copy(source, target, sems.at[tiles + number])
        for number, (source, target) in enumerate(
            (
                (pos_ref, lanes_ref),
                (fresh_ref, flat_ref),
                (pos_ref, row_smem),
                (owner_ref, owner_smem),
                (slot_ref, slot_smem),
                (span_ref, span_smem),
                (store_ref, near_ref),
            )
        )
    ]
    for copy in small[:-1]:
        copy.start()
    for tile in range(tiles):
        load_query(tile).start()
    small[-1].start()
    for copy in small[:-1]:
        copy.wait()
    wide_ref[...] = flat_ref[...].astype(jnp.float32)
    for head in range(heads):
        key = wide_ref[pl.ds(head, rows, stride=2 * heads), :]
        value = wide_ref[pl.ds(heads + head, rows, stride=2 * heads), :]
        all_ref[:, head * 2 * dim : head * 2 * dim + dim] = turn(
            key, cos_ref[...], sin_ref[...]
        ).astype(jnp.bfloat16)
        all_ref[:, head * 2 * dim + dim : (head + 1) * 2 * dim] = value.astype(jnp.bfloat16)
    all_ref[:, heads * 2 * dim :] = jnp.ones((rows, dim), jnp.bfloat16)
    step = 512

    def place(number, carry):
        at = pl.ds(pl.multiple_of(number * step, step), step)
        spot = lax.broadcasted_iota(jnp.int32, (step, rows), 0) + number * step
        chosen = jnp.where(spot == lanes_ref[...], 1.0, 0.0).astype(jnp.bfloat16)
        placed_ref[at, :] = jnp.dot(
            chosen, all_ref[...], preferred_element_type=jnp.float32
        ).astype(jnp.bfloat16)
        return carry

    lax.fori_loop(0, placed_rows // step, place, 0)

    def note(block, carry):
        began = jnp.int32(0)
        start = jnp.int32(0)
        for span in range(span_ref.shape[1]):
            began = jnp.where(start <= block, start, began)
            start = start + span_smem[0, span]
        table_ref[block] = owner_smem[0, block]
        table_ref[blocks + block] = slot_smem[0, block]
        table_ref[2 * blocks + block] = began
        return carry

    lax.fori_loop(0, blocks, note, 0)
    for tile in range(tiles):
        table_ref[3 * blocks + tile] = row_smem[0, (tile + 1) * tile_rows - 1]
    table_ref[3 * blocks + tiles] = place_ref[0]
    ones = jnp.ones((dim, dim), jnp.bfloat16)

    def turn_tile(tile, peak):
        load_query(tile).wait()
        at = pl.ds(pl.multiple_of(tile * tile_rows, tile_rows), tile_rows)
        cosine = cos_ref[at, :]
        sine = sin_ref[at, :]
        for head in range(heads):
            squares = []
            for member in range(group):
                column = (head * group + member) * dim
                field = raw_ref[at, column : column + dim].astype(jnp.float32)
                turned_ref[head, tile, member * tile_rows : (member + 1) * tile_rows, :] = turn(
                    field, cosine, sine
                ).astype(jnp.bfloat16)
                squares.append((field * field).astype(jnp.bfloat16))
            lengths = jnp.dot(
                jnp.concatenate(squares, axis=0), ones, preferred_element_type=jnp.float32
            )
            peak = jnp.maximum(peak, jnp.max(lengths.reshape(-1, 8, dim), axis=0))
        return peak

    peak = lax.fori_loop(0, tiles, turn_tile, jnp.zeros((8, dim), jnp.float32))
    peak_ref[0] = jnp.max(peak)
    small[-1].wait()


def attend(shards, pick, parts_of, units, first, last, *refs):
    given = len(pick)
    sources = refs[:given]
    table_ref, calm_in, turned_ref, placed_ref, cos_ref, sin_ref, row_ref = refs[given : given + 7]
    refs = refs[given + 7 :]
    if not first:
        most_in, sum_in, acc_in = refs[:3]
        refs = refs[3:]
    most_out, sum_out, acc_out, calm_out = refs[:4]
    refs = refs[4:]
    if last:
        out_ref = refs[0]
        refs = refs[1:]
    wide_ref, key_ref, value_ref, list_ref = refs
    heads, tiles, lanes_rows, dim = turned_ref.shape
    group = lanes_rows // tile_rows
    blocks = cos_ref.shape[0]
    block_len = placed_ref.shape[0] // blocks
    stride = 2 * heads
    raw_rows = block_len * stride
    slots = sources[0].shape[0] // raw_rows // shards if parts_of is None else None
    scale = dim**-0.5 * math.log2(math.e)
    lowest = [choose(table_ref[3 * blocks + tiles]) for choose in pick]
    spots = units * unit_blocks

    whole = parts_of is None
    low_slot, high_slot = (0, slots) if whole else parts_of

    def find(block, found):
        owner = table_ref[block]
        hit = jnp.bool_(False)
        for base in lowest:
            hit = hit | ((owner >= base) & (owner < base + shards))
        if not whole:
            slot = table_ref[blocks + block]
            hit = hit & (slot >= low_slot) & (slot < high_slot)
        list_ref[found] = block
        return found + hit.astype(jnp.int32)

    found = lax.fori_loop(0, blocks, find, jnp.int32(0))
    if not whole:

        def clear(spot, carry):
            list_ref[spot] = far
            return carry

        lax.fori_loop(found, spots, clear, 0)
    ones = jnp.ones((dim, dim), jnp.bfloat16)

    def load(turn_number, peak):
        for lane in range(chunk):
            spot = turn_number * chunk + lane
            block = list_ref[spot] if whole else jnp.minimum(list_ref[spot], blocks - 1)
            owner = table_ref[block]
            raw = None
            for source, base in zip(sources, lowest):
                here = (owner >= base) & (owner < base + shards)
                slot = table_ref[blocks + block]
                if whole:
                    start = jnp.where(here, (owner - base) * slots + slot, 0)
                else:
                    start = jnp.clip(slot - low_slot, 0, high_slot - low_slot - 1)
                start = pl.multiple_of(start * raw_rows, raw_rows)
                found = source[pl.ds(start, raw_rows), :].astype(jnp.float32)
                raw = found if raw is None else jnp.where(here, found, raw)
            wide_ref[lane] = raw
            began = table_ref[2 * blocks + block]
            cosine = cos_ref[pl.ds(began, 1), :]
            sine = sin_ref[pl.ds(began, 1), :]
            fresh = placed_ref[
                pl.ds(pl.multiple_of(block * block_len, block_len), block_len), :
            ].astype(jnp.float32)
            renewed = fresh[:, heads * 2 * dim :] > 0.5
            at = pl.ds(pl.multiple_of(spot * block_len, block_len), block_len)
            for head in range(heads):
                key = turn(wide_ref[lane, pl.ds(head, block_len, stride=stride), :], cosine, sine)
                value = wide_ref[lane, pl.ds(heads + head, block_len, stride=stride), :]
                begin = head * 2 * dim
                key = jnp.where(renewed, fresh[:, begin : begin + dim], key)
                key_ref[head, at, :] = key.astype(jnp.bfloat16)
                value_ref[head, at, :] = jnp.where(
                    renewed, fresh[:, begin + dim : begin + 2 * dim], value
                ).astype(jnp.bfloat16)
                lengths = jnp.dot(
                    (key * key).astype(jnp.bfloat16), ones, preferred_element_type=jnp.float32
                )
                peak = jnp.maximum(peak, jnp.max(lengths.reshape(-1, 8, dim), axis=0))
        return peak

    turns = spots // chunk if whole else (found + chunk - 1) // chunk
    peak = lax.fori_loop(0, turns, load, jnp.zeros((8, dim), jnp.float32))
    room = (calm_in[0] < 1e38) & (calm_in[0] * jnp.max(peak) <= (bound / scale) ** 2)
    calm = room.astype(jnp.float32)
    calm_out[0] = jnp.where(room, calm_in[0], jnp.float32(3e38))

    def query_mask(tile):
        row_at = pl.ds(pl.multiple_of(tile * tile_rows, tile_rows), tile_rows)
        row_pos = row_ref[row_at, :]
        lane = lax.broadcasted_iota(jnp.int32, (tile_rows, block_len), 1)
        return lambda spot: (lane + list_ref[spot] * block_len <= row_pos)[None]

    def scored(head, tile, first_spot, count, seen):
        at = pl.ds(pl.multiple_of(first_spot * block_len, block_len), count * block_len)
        scores = lax.dot_general(
            turned_ref[head, tile],
            key_ref[head, at, :],
            (((1,), (1,)), ((), ())),
            preferred_element_type=jnp.float32,
        )
        return at, [
            jnp.where(
                seen[spot],
                scores[:, spot * block_len : (spot + 1) * block_len].reshape(
                    group, tile_rows, block_len
                ),
                2 * low,
            ).reshape(lanes_rows, block_len)
            for spot in range(count)
        ]

    def weighed(head, at, parts):
        return functools.reduce(jnp.add, parts), jnp.dot(
            jnp.concatenate([part.astype(jnp.bfloat16) for part in parts], axis=1),
            value_ref[head, at, :],
            preferred_element_type=jnp.float32,
        )

    def write(head, tile, total, acc):
        sum_out[head, tile] = total
        acc_out[head, tile] = acc

    def finish(head, tile, total, acc):
        result = (acc / jnp.sum(total, axis=1, keepdims=True)).astype(jnp.bfloat16)
        row_at = pl.ds(pl.multiple_of(tile * tile_rows, tile_rows), tile_rows)
        for member in range(group):
            column = (head * group + member) * dim
            out_ref[row_at, column : column + dim] = result[
                member * tile_rows : (member + 1) * tile_rows
            ]

    def quick(tile, carry):
        furthest = table_ref[3 * blocks + tile]
        visible = query_mask(tile)
        for unit in range(units):
            fresh = first and unit == 0
            ends = last and unit == units - 1
            before = (sum_in, acc_in) if unit == 0 and not first else (sum_out, acc_out)
            first_spot = unit * unit_blocks
            active = jnp.int32(0)
            for spot in range(unit_blocks):
                begins = list_ref[first_spot + spot] * block_len
                active = active + (begins <= furthest).astype(jnp.int32)
            after = finish if ends else write
            for count in range(0, unit_blocks + 1, grain):

                @pl.when((active + grain - 1) // grain == count // grain)
                def _(count=count):
                    if not count and not fresh and not ends:
                        return
                    seen = [visible(first_spot + spot) for spot in range(count)]
                    for head in range(heads):
                        total = acc = jnp.zeros((lanes_rows, dim), jnp.float32)
                        if count:
                            at, parts = scored(head, tile, first_spot, count, seen)
                            parts = [jnp.exp2(part * scale) for part in parts]
                            total, acc = weighed(head, at, parts)
                        if not fresh:
                            total = before[0][head, tile] + total
                            acc = before[1][head, tile] + acc
                        after(head, tile, total, acc)

        return carry

    def careful(tile, carry):
        furthest = table_ref[3 * blocks + tile]
        visible = query_mask(tile)

        def begin(head, ignored):
            if first:
                nothing = jnp.zeros((lanes_rows, dim), jnp.float32)
                most_out[head, tile] = nothing + low
                write(head, tile, nothing, nothing)
            else:
                total = sum_in[head, tile]
                most_out[head, tile] = jnp.where(
                    calm_in[0] < 1e38,
                    jnp.where(jnp.max(total, axis=1, keepdims=True) > 0, 0.0, low),
                    most_in[head, tile],
                )
                write(head, tile, total, acc_in[head, tile])
            return ignored

        lax.fori_loop(0, heads, begin, 0)

        def one(step, ignored):
            head = step % heads
            spot = step // heads

            @pl.when(list_ref[spot] * block_len <= furthest)
            def _():
                at, parts = scored(head, tile, spot, 1, [visible(spot)])
                was = most_out[head, tile]
                most = jnp.maximum(was, jnp.max(parts[0], axis=1, keepdims=True))
                total, acc = weighed(head, at, [jnp.exp2((parts[0] - most) * scale)])
                shrink = jnp.exp2((was - most) * scale)
                most_out[head, tile] = most
                write(
                    head,
                    tile,
                    sum_out[head, tile] * shrink + total,
                    acc_out[head, tile] * shrink + acc,
                )

            return ignored

        lax.fori_loop(0, spots * heads, one, 0)
        if last:
            for head in range(heads):
                finish(head, tile, sum_out[head, tile], acc_out[head, tile])
        return carry

    @pl.when(calm > 0.5)
    def _():
        lax.fori_loop(0, tiles, quick, 0)

    @pl.when(calm < 0.5)
    def _():
        lax.fori_loop(0, tiles, careful, 0)


def on_device(count, store_kv, block_owner, block_slot, span_len, row_index, fresh_q, fresh_kv):
    stored, block_len, heads, pair_width = store_kv.shape
    dim = pair_width // 2
    blocks = block_slot.shape[1]
    rows = row_index.shape[1]
    group = fresh_q.shape[2] // (heads * dim)
    tiles = rows // tile_rows
    lanes_rows = tile_rows * group
    raw_rows = block_len * 2 * heads

    def flat(array):
        lead = math.prod(array.shape[:-2])
        split = array.reshape(lead, heads, 2, dim)
        return split.transpose(0, 2, 1, 3).reshape(lead * 2 * heads, dim)

    store = flat(store_kv)
    place = lax.axis_index("req").reshape(1)
    row_pos = row_index[0]
    row_cos, row_sin = tables(row_pos.astype(jnp.float32), dim)
    outer = [(0, 1), (1, 0), (2, 3), (3, 2)]
    inner = [(1, 2), (2, 1)]
    outward = [(1, 0), (2, 3)]
    none = -(1 << 16)
    is_end = lambda at: (at == 0) | (at == 3)

    def send(array, pairs):
        return lax.ppermute(array, "req", pairs)

    if count == 4:
        beside = send(store, outer)
        across = send(store, inner)
    cos, sin = tables(block_len * jnp.arange(blocks, dtype=jnp.float32), dim)
    row_lanes = jnp.broadcast_to(row_pos[:, None], (rows, block_len))
    wide = heads * 2 * dim + dim
    turned, placed, close, table, peak = pl.pallas_call(
        prepare,
        out_shape=(
            pltpu.VMEM((heads, tiles, lanes_rows, dim), jnp.bfloat16),
            pltpu.VMEM((blocks * block_len, wide), jnp.bfloat16),
            pltpu.VMEM(store.shape, jnp.bfloat16),
            pltpu.SMEM((3 * blocks + tiles + 1,), jnp.int32),
            pltpu.SMEM((1,), jnp.float32),
        ),
        in_specs=[anywhere] * 7 + [smem, vmem, vmem],
        out_specs=(vmem, vmem, vmem, smem, smem),
        scratch_shapes=[
            pltpu.VMEM((rows, heads * group * dim), jnp.bfloat16),
            pltpu.VMEM((rows * 2 * heads, dim), jnp.bfloat16),
            pltpu.VMEM((rows * 2 * heads, dim), jnp.float32),
            pltpu.VMEM((rows, wide), jnp.bfloat16),
            pltpu.VMEM((1, rows), jnp.int32),
            pltpu.SMEM((1, rows), jnp.int32),
            pltpu.SMEM((1, blocks), jnp.int32),
            pltpu.SMEM((1, blocks), jnp.int32),
            pltpu.SMEM(span_len.shape, jnp.int32),
            pltpu.SemaphoreType.DMA((tiles + 7,)),
        ],
        compiler_params=params,
        name="prepare",
    )(
        away(fresh_q[0]), away(flat(fresh_kv)), away(store), away(block_owner[:, :, 0]),
        away(block_slot), away(span_len), away(row_index), place, near(row_cos), near(row_sin),
    )

    def attention(number, last, sources, pick, shards, units, state, parts_of=None):
        first = len(state) == 1
        state_shape = pltpu.VMEM((heads, tiles, lanes_rows, dim), jnp.float32)
        inputs = [near(source) for source in sources]
        inputs += [held(table), held(state[-1])]
        inputs += [near(array) for array in (turned, placed, cos, sin, row_lanes)]
        specs = [vmem] * len(sources) + [smem] * 2 + [vmem] * 5
        spots = units * unit_blocks
        result = [jax.ShapeDtypeStruct((rows, heads * group * dim), jnp.bfloat16)] if last else []
        return pl.pallas_call(
            functools.partial(attend, shards, pick, parts_of, units, first, last),
            out_shape=[state_shape] * 3 + [pltpu.SMEM((1,), jnp.float32)] + result,
            in_specs=specs + [vmem] * (len(state) - 1),
            out_specs=[vmem] * 3 + [smem] + [vmem] * len(result),
            input_output_aliases={}
            if first
            else {len(specs) + entry: entry for entry in range(3)},
            scratch_shapes=[
                pltpu.VMEM((chunk, raw_rows, dim), jnp.float32),
                pltpu.VMEM((heads, spots * block_len, dim), jnp.bfloat16),
                pltpu.VMEM((heads, spots * block_len, dim), jnp.bfloat16),
                pltpu.SMEM((blocks + 1,), jnp.int32),
            ],
            compiler_params=params,
            name=f"attend_{number}",
        )(*inputs, *[near(entry) for entry in state[:-1]])

    if count != 4:
        everything = lax.all_gather(store, "req", axis=0, tiled=True)
        return attention(
            0, True, [everything], [lambda at: 0], count, blocks // unit_blocks, (peak,)
        )[-1][None]
    beside, across, close, turned = lax.optimization_barrier((beside, across, close, turned))
    second = send(across, outward)
    halves = ((0, cut), (cut, stored))
    third_in = [send(beside[begin * raw_rows : end * raw_rows], inner) for begin, end in halves]
    state = attention(0, False, [close, beside], [lambda at: at, lambda at: at ^ 1], 1, 2, (peak,))
    third = []
    for number in range(2):
        third_in[number], second, state = lax.optimization_barrier(
            (third_in[number], second, state)
        )
        third.append(send(third_in[number], outward))
    state = attention(
        1,
        False,
        [second, across],
        [
            lambda at: jnp.where(is_end(at), jnp.where(at == 0, 2, 1), none),
            lambda at: jnp.where(is_end(at), none, 3 - at),
        ],
        1,
        1,
        state,
    )
    for number in range(2):
        third[number], state = lax.optimization_barrier((third[number], state))
        state = attention(
            2 + number,
            number == 1,
            [third[number], third_in[number]],
            [
                lambda at: jnp.where(is_end(at), 3 - at, none),
                lambda at: jnp.where(is_end(at), none, (3 - at) ^ 1),
            ],
            1,
            1,
            state,
            halves[number],
        )
    return state[-1][None]


def solution(mesh):
    placed = (
        P(("grp", "req"), None, "kvh", None),
        P(("grp", "req"), None, None),
        P(("grp", "req"), None),
        P(("grp", "req"), None),
        P(("grp", "req"), None),
        P(("grp", "req"), None, "kvh"),
        P(("grp", "req"), None, "kvh", None),
    )
    return jax.shard_map(
        functools.partial(on_device, mesh.shape["req"]),
        mesh=mesh,
        in_specs=placed,
        out_specs=P(("grp", "req"), None, "kvh"),
        check_vma=False,
    )
```

```python
import functools
import math

import jax
import jax.numpy as jnp
from jax import lax
from jax.experimental import pallas as pl
from jax.experimental.pallas import tpu as pltpu
from jax.sharding import PartitionSpec as P

rope_base = 500000.0
tile_rows = 64
unit_blocks = 6
low = -1e30
far = 1 << 20
cut = 2
bound = 105.0
grain = 2
chunk = 3
vmem = pl.BlockSpec(memory_space=pltpu.VMEM)
smem = pl.BlockSpec(memory_space=pltpu.SMEM)
anywhere = pl.BlockSpec(memory_space=pl.ANY)
params = pltpu.CompilerParams(vmem_limit_bytes=28 << 20)


def near(array):
    return pltpu.with_memory_space_constraint(array, pltpu.VMEM)


def held(array):
    return pltpu.with_memory_space_constraint(array, pltpu.SMEM)


def away(array):
    return pltpu.with_memory_space_constraint(array, pltpu.HBM)


def tables(position, head_dim):
    lane = lax.broadcasted_iota(jnp.int32, (position.shape[0], head_dim), 1)
    half_dim = head_dim // 2
    pair_index = (lane % half_dim).astype(jnp.float32)
    inv_freq = jnp.exp(pair_index * (-2.0 / head_dim) * jnp.log(jnp.float32(rope_base)))
    angles = position[:, None] * inv_freq
    sine = jnp.sin(angles)
    return jnp.cos(angles), jnp.where(lane < half_dim, -sine, sine)


def turn(field, cosine, sine):
    return field * cosine + pltpu.roll(field, field.shape[1] // 2, 1) * sine


def prepare(
    query_ref, fresh_ref, store_ref, owner_ref, slot_ref, span_ref, pos_ref, place_ref, cos_ref, sin_ref,
    turned_ref, placed_ref, near_ref, table_ref, peak_ref,
    raw_ref, flat_ref, wide_ref, all_ref, lanes_ref, row_smem, owner_smem, slot_smem, span_smem, sems,
):
    heads, tiles, lanes_rows, dim = turned_ref.shape
    group = lanes_rows // tile_rows
    placed_rows = placed_ref.shape[0]
    rows = cos_ref.shape[0]
    blocks = slot_ref.shape[1]

    def load_query(tile):
        at = pl.ds(pl.multiple_of(tile * tile_rows, tile_rows), tile_rows)
        return pltpu.make_async_copy(query_ref.at[at, :], raw_ref.at[at, :], sems.at[tile])

    small = [
        pltpu.make_async_copy(source, target, sems.at[tiles + number])
        for number, (source, target) in enumerate(
            (
                (pos_ref, lanes_ref),
                (fresh_ref, flat_ref),
                (pos_ref, row_smem),
                (owner_ref, owner_smem),
                (slot_ref, slot_smem),
                (span_ref, span_smem),
                (store_ref, near_ref),
            )
        )
    ]
    for copy in small[:-1]:
        copy.start()
    for tile in range(tiles):
        load_query(tile).start()
    small[-1].start()
    for copy in small[:-1]:
        copy.wait()
    wide_ref[...] = flat_ref[...].astype(jnp.float32)
    for head in range(heads):
        key = wide_ref[pl.ds(head, rows, stride=2 * heads), :]
        value = wide_ref[pl.ds(heads + head, rows, stride=2 * heads), :]
        all_ref[:, head * 2 * dim : head * 2 * dim + dim] = turn(
            key, cos_ref[...], sin_ref[...]
        ).astype(jnp.bfloat16)
        all_ref[:, head * 2 * dim + dim : (head + 1) * 2 * dim] = value.astype(jnp.bfloat16)
    all_ref[:, heads * 2 * dim :] = jnp.ones((rows, dim), jnp.bfloat16)
    step = 512

    def place(number, carry):
        at = pl.ds(pl.multiple_of(number * step, step), step)
        spot = lax.broadcasted_iota(jnp.int32, (step, rows), 0) + number * step
        chosen = jnp.where(spot == lanes_ref[...], 1.0, 0.0).astype(jnp.bfloat16)
        placed_ref[at, :] = jnp.dot(
            chosen, all_ref[...], preferred_element_type=jnp.float32
        ).astype(jnp.bfloat16)
        return carry

    lax.fori_loop(0, placed_rows // step, place, 0)

    def note(block, carry):
        began = jnp.int32(0)
        start = jnp.int32(0)
        for span in range(span_ref.shape[1]):
            began = jnp.where(start <= block, start, began)
            start = start + span_smem[0, span]
        table_ref[block] = owner_smem[0, block]
        table_ref[blocks + block] = slot_smem[0, block]
        table_ref[2 * blocks + block] = began
        return carry

    lax.fori_loop(0, blocks, note, 0)
    for tile in range(tiles):
        table_ref[3 * blocks + tile] = row_smem[0, (tile + 1) * tile_rows - 1]
    table_ref[3 * blocks + tiles] = place_ref[0]
    ones = jnp.ones((dim, dim), jnp.bfloat16)

    def turn_tile(tile, peak):
        load_query(tile).wait()
        at = pl.ds(pl.multiple_of(tile * tile_rows, tile_rows), tile_rows)
        cosine = cos_ref[at, :]
        sine = sin_ref[at, :]
        for head in range(heads):
            squares = []
            for member in range(group):
                column = (head * group + member) * dim
                field = raw_ref[at, column : column + dim].astype(jnp.float32)
                turned_ref[head, tile, member * tile_rows : (member + 1) * tile_rows, :] = turn(
                    field, cosine, sine
                ).astype(jnp.bfloat16)
                squares.append((field * field).astype(jnp.bfloat16))
            lengths = jnp.dot(
                jnp.concatenate(squares, axis=0), ones, preferred_element_type=jnp.float32
            )
            peak = jnp.maximum(peak, jnp.max(lengths.reshape(-1, 8, dim), axis=0))
        return peak

    peak = lax.fori_loop(0, tiles, turn_tile, jnp.zeros((8, dim), jnp.float32))
    peak_ref[0] = jnp.max(peak)
    small[-1].wait()


def attend(shards, pick, parts_of, units, first, last, *refs):
    given = len(pick)
    sources = refs[:given]
    table_ref, calm_in, turned_ref, placed_ref, cos_ref, sin_ref, row_ref = refs[given : given + 7]
    refs = refs[given + 7 :]
    if not first:
        most_in, sum_in, acc_in = refs[:3]
        refs = refs[3:]
    most_out, sum_out, acc_out, calm_out = refs[:4]
    refs = refs[4:]
    if last:
        out_ref = refs[0]
        refs = refs[1:]
    wide_ref, key_ref, value_ref, list_ref = refs
    heads, tiles, lanes_rows, dim = turned_ref.shape
    group = lanes_rows // tile_rows
    blocks = cos_ref.shape[0]
    block_len = placed_ref.shape[0] // blocks
    stride = 2 * heads
    raw_rows = block_len * stride
    slots = sources[0].shape[0] // raw_rows // shards if parts_of is None else None
    scale = dim**-0.5 * math.log2(math.e)
    lowest = [choose(table_ref[3 * blocks + tiles]) for choose in pick]
    spots = units * unit_blocks

    whole = parts_of is None
    low_slot, high_slot = (0, slots) if whole else parts_of

    def find(block, found):
        owner = table_ref[block]
        hit = jnp.bool_(False)
        for base in lowest:
            hit = hit | ((owner >= base) & (owner < base + shards))
        if not whole:
            slot = table_ref[blocks + block]
            hit = hit & (slot >= low_slot) & (slot < high_slot)
        list_ref[found] = block
        return found + hit.astype(jnp.int32)

    found = lax.fori_loop(0, blocks, find, jnp.int32(0))
    if not whole:

        def clear(spot, carry):
            list_ref[spot] = far
            return carry

        lax.fori_loop(found, spots, clear, 0)
    ones = jnp.ones((dim, dim), jnp.bfloat16)

    def load(turn_number, peak):
        for lane in range(chunk):
            spot = turn_number * chunk + lane
            block = list_ref[spot] if whole else jnp.minimum(list_ref[spot], blocks - 1)
            owner = table_ref[block]
            raw = None
            for source, base in zip(sources, lowest):
                here = (owner >= base) & (owner < base + shards)
                slot = table_ref[blocks + block]
                if whole:
                    start = jnp.where(here, (owner - base) * slots + slot, 0)
                else:
                    start = jnp.clip(slot - low_slot, 0, high_slot - low_slot - 1)
                start = pl.multiple_of(start * raw_rows, raw_rows)
                found = source[pl.ds(start, raw_rows), :].astype(jnp.float32)
                raw = found if raw is None else jnp.where(here, found, raw)
            wide_ref[lane] = raw
            began = table_ref[2 * blocks + block]
            cosine = cos_ref[pl.ds(began, 1), :]
            sine = sin_ref[pl.ds(began, 1), :]
            fresh = placed_ref[
                pl.ds(pl.multiple_of(block * block_len, block_len), block_len), :
            ].astype(jnp.float32)
            renewed = fresh[:, heads * 2 * dim :] > 0.5
            at = pl.ds(pl.multiple_of(spot * block_len, block_len), block_len)
            for head in range(heads):
                key = turn(wide_ref[lane, pl.ds(head, block_len, stride=stride), :], cosine, sine)
                value = wide_ref[lane, pl.ds(heads + head, block_len, stride=stride), :]
                begin = head * 2 * dim
                key = jnp.where(renewed, fresh[:, begin : begin + dim], key)
                key_ref[head, at, :] = key.astype(jnp.bfloat16)
                value_ref[head, at, :] = jnp.where(
                    renewed, fresh[:, begin + dim : begin + 2 * dim], value
                ).astype(jnp.bfloat16)
                lengths = jnp.dot(
                    (key * key).astype(jnp.bfloat16), ones, preferred_element_type=jnp.float32
                )
                peak = jnp.maximum(peak, jnp.max(lengths.reshape(-1, 8, dim), axis=0))
        return peak

    turns = spots // chunk if whole else (found + chunk - 1) // chunk
    peak = lax.fori_loop(0, turns, load, jnp.zeros((8, dim), jnp.float32))
    room = (calm_in[0] < 1e38) & (calm_in[0] * jnp.max(peak) <= (bound / scale) ** 2)
    calm = room.astype(jnp.float32)
    calm_out[0] = jnp.where(room, calm_in[0], jnp.float32(3e38))

    def query_mask(tile):
        row_at = pl.ds(pl.multiple_of(tile * tile_rows, tile_rows), tile_rows)
        row_pos = row_ref[row_at, :]
        lane = lax.broadcasted_iota(jnp.int32, (tile_rows, block_len), 1)
        return lambda spot: (lane + list_ref[spot] * block_len <= row_pos)[None]

    def scored(head, tile, first_spot, count, seen):
        at = pl.ds(pl.multiple_of(first_spot * block_len, block_len), count * block_len)
        scores = lax.dot_general(
            turned_ref[head, tile],
            key_ref[head, at, :],
            (((1,), (1,)), ((), ())),
            preferred_element_type=jnp.float32,
        )
        return at, [
            jnp.where(
                seen[spot],
                scores[:, spot * block_len : (spot + 1) * block_len].reshape(
                    group, tile_rows, block_len
                ),
                2 * low,
            ).reshape(lanes_rows, block_len)
            for spot in range(count)
        ]

    def weighed(head, at, parts):
        return functools.reduce(jnp.add, parts), jnp.dot(
            jnp.concatenate([part.astype(jnp.bfloat16) for part in parts], axis=1),
            value_ref[head, at, :],
            preferred_element_type=jnp.float32,
        )

    def write(head, tile, total, acc):
        sum_out[head, tile] = total
        acc_out[head, tile] = acc

    def finish(head, tile, total, acc):
        result = (acc / jnp.sum(total, axis=1, keepdims=True)).astype(jnp.bfloat16)
        row_at = pl.ds(pl.multiple_of(tile * tile_rows, tile_rows), tile_rows)
        for member in range(group):
            column = (head * group + member) * dim
            out_ref[row_at, column : column + dim] = result[
                member * tile_rows : (member + 1) * tile_rows
            ]

    def quick(tile, carry):
        furthest = table_ref[3 * blocks + tile]
        visible = query_mask(tile)
        for unit in range(units):
            fresh = first and unit == 0
            ends = last and unit == units - 1
            before = (sum_in, acc_in) if unit == 0 and not first else (sum_out, acc_out)
            first_spot = unit * unit_blocks
            active = jnp.int32(0)
            for spot in range(unit_blocks):
                begins = list_ref[first_spot + spot] * block_len
                active = active + (begins <= furthest).astype(jnp.int32)
            after = finish if ends else write
            for count in range(0, unit_blocks + 1, grain):

                @pl.when((active + grain - 1) // grain == count // grain)
                def _(count=count):
                    if not count and not fresh and not ends:
                        return
                    seen = [visible(first_spot + spot) for spot in range(count)]
                    for head in range(heads):
                        total = acc = jnp.zeros((lanes_rows, dim), jnp.float32)
                        if count:
                            at, parts = scored(head, tile, first_spot, count, seen)
                            parts = [jnp.exp2(part * scale) for part in parts]
                            total, acc = weighed(head, at, parts)
                        if not fresh:
                            total = before[0][head, tile] + total
                            acc = before[1][head, tile] + acc
                        after(head, tile, total, acc)

        return carry

    def careful(tile, carry):
        furthest = table_ref[3 * blocks + tile]
        visible = query_mask(tile)

        def begin(head, ignored):
            if first:
                nothing = jnp.zeros((lanes_rows, dim), jnp.float32)
                most_out[head, tile] = nothing + low
                write(head, tile, nothing, nothing)
            else:
                total = sum_in[head, tile]
                most_out[head, tile] = jnp.where(
                    calm_in[0] < 1e38,
                    jnp.where(jnp.max(total, axis=1, keepdims=True) > 0, 0.0, low),
                    most_in[head, tile],
                )
                write(head, tile, total, acc_in[head, tile])
            return ignored

        lax.fori_loop(0, heads, begin, 0)

        def one(step, ignored):
            head = step % heads
            spot = step // heads

            @pl.when(list_ref[spot] * block_len <= furthest)
            def _():
                at, parts = scored(head, tile, spot, 1, [visible(spot)])
                was = most_out[head, tile]
                most = jnp.maximum(was, jnp.max(parts[0], axis=1, keepdims=True))
                total, acc = weighed(head, at, [jnp.exp2((parts[0] - most) * scale)])
                shrink = jnp.exp2((was - most) * scale)
                most_out[head, tile] = most
                write(
                    head,
                    tile,
                    sum_out[head, tile] * shrink + total,
                    acc_out[head, tile] * shrink + acc,
                )

            return ignored

        lax.fori_loop(0, spots * heads, one, 0)
        if last:
            for head in range(heads):
                finish(head, tile, sum_out[head, tile], acc_out[head, tile])
        return carry

    @pl.when(calm > 0.5)
    def _():
        lax.fori_loop(0, tiles, quick, 0)

    @pl.when(calm < 0.5)
    def _():
        lax.fori_loop(0, tiles, careful, 0)


def on_device(count, store_kv, block_owner, block_slot, span_len, row_index, fresh_q, fresh_kv):
    stored, block_len, heads, pair_width = store_kv.shape
    dim = pair_width // 2
    blocks = block_slot.shape[1]
    rows = row_index.shape[1]
    group = fresh_q.shape[2] // (heads * dim)
    tiles = rows // tile_rows
    lanes_rows = tile_rows * group
    raw_rows = block_len * 2 * heads

    def flat(array):
        lead = math.prod(array.shape[:-2])
        split = array.reshape(lead, heads, 2, dim)
        return split.transpose(0, 2, 1, 3).reshape(lead * 2 * heads, dim)

    store = flat(store_kv)
    place = lax.axis_index("req").reshape(1)
    row_pos = row_index[0]
    row_cos, row_sin = tables(row_pos.astype(jnp.float32), dim)
    outer = [(0, 1), (1, 0), (2, 3), (3, 2)]
    inner = [(1, 2), (2, 1)]
    outward = [(1, 0), (2, 3)]
    none = -(1 << 16)
    is_end = lambda at: (at == 0) | (at == 3)

    def send(array, pairs):
        return lax.ppermute(array, "req", pairs)

    if count == 4:
        beside = send(store, outer)
        across = send(store, inner)
    cos, sin = tables(block_len * jnp.arange(blocks, dtype=jnp.float32), dim)
    row_lanes = jnp.broadcast_to(row_pos[:, None], (rows, block_len))
    wide = heads * 2 * dim + dim
    turned, placed, close, table, peak = pl.pallas_call(
        prepare,
        out_shape=(
            pltpu.VMEM((heads, tiles, lanes_rows, dim), jnp.bfloat16),
            pltpu.VMEM((blocks * block_len, wide), jnp.bfloat16),
            pltpu.VMEM(store.shape, jnp.bfloat16),
            pltpu.SMEM((3 * blocks + tiles + 1,), jnp.int32),
            pltpu.SMEM((1,), jnp.float32),
        ),
        in_specs=[anywhere] * 7 + [smem, vmem, vmem],
        out_specs=(vmem, vmem, vmem, smem, smem),
        scratch_shapes=[
            pltpu.VMEM((rows, heads * group * dim), jnp.bfloat16),
            pltpu.VMEM((rows * 2 * heads, dim), jnp.bfloat16),
            pltpu.VMEM((rows * 2 * heads, dim), jnp.float32),
            pltpu.VMEM((rows, wide), jnp.bfloat16),
            pltpu.VMEM((1, rows), jnp.int32),
            pltpu.SMEM((1, rows), jnp.int32),
            pltpu.SMEM((1, blocks), jnp.int32),
            pltpu.SMEM((1, blocks), jnp.int32),
            pltpu.SMEM(span_len.shape, jnp.int32),
            pltpu.SemaphoreType.DMA((tiles + 7,)),
        ],
        compiler_params=params,
        name="prepare",
    )(
        away(fresh_q[0]), away(flat(fresh_kv)), away(store), away(block_owner[:, :, 0]),
        away(block_slot), away(span_len), away(row_index), place, near(row_cos), near(row_sin),
    )

    def attention(number, last, sources, pick, shards, units, state, parts_of=None):
        first = len(state) == 1
        state_shape = pltpu.VMEM((heads, tiles, lanes_rows, dim), jnp.float32)
        inputs = [near(source) for source in sources]
        inputs += [held(table), held(state[-1])]
        inputs += [near(array) for array in (turned, placed, cos, sin, row_lanes)]
        specs = [vmem] * len(sources) + [smem] * 2 + [vmem] * 5
        spots = units * unit_blocks
        result = [jax.ShapeDtypeStruct((rows, heads * group * dim), jnp.bfloat16)] if last else []
        return pl.pallas_call(
            functools.partial(attend, shards, pick, parts_of, units, first, last),
            out_shape=[state_shape] * 3 + [pltpu.SMEM((1,), jnp.float32)] + result,
            in_specs=specs + [vmem] * (len(state) - 1),
            out_specs=[vmem] * 3 + [smem] + [vmem] * len(result),
            input_output_aliases={}
            if first
            else {len(specs) + entry: entry for entry in range(3)},
            scratch_shapes=[
                pltpu.VMEM((chunk, raw_rows, dim), jnp.float32),
                pltpu.VMEM((heads, spots * block_len, dim), jnp.bfloat16),
                pltpu.VMEM((heads, spots * block_len, dim), jnp.bfloat16),
                pltpu.SMEM((blocks + 1,), jnp.int32),
            ],
            compiler_params=params,
            name=f"attend_{number}",
        )(*inputs, *[near(entry) for entry in state[:-1]])

    if count != 4:
        everything = lax.all_gather(store, "req", axis=0, tiled=True)
        return attention(
            0, True, [everything], [lambda at: 0], count, blocks // unit_blocks, (peak,)
        )[-1][None]
    beside, across, close, turned, store = lax.optimization_barrier(
        (beside, across, close, turned, store)
    )
    second = send(across, outward)
    third = send(store, [(0, 2), (3, 1)])
    state = attention(0, False, [close], [lambda at: at], 1, 1, (peak,))
    later, state = lax.optimization_barrier((store, state))
    opposite = send(later, [(0, 3), (3, 0)])
    state = attention(1, False, [beside], [lambda at: at ^ 1], 1, 1, state)
    second, state = lax.optimization_barrier((second, state))
    state = attention(
        2,
        False,
        [second, across],
        [
            lambda at: jnp.where(is_end(at), jnp.where(at == 0, 2, 1), none),
            lambda at: jnp.where(is_end(at), none, 3 - at),
        ],
        1,
        1,
        state,
    )
    opposite, third, state = lax.optimization_barrier((opposite, third, state))
    return attention(
        3,
        True,
        [opposite, third],
        [
            lambda at: jnp.where(is_end(at), 3 - at, none),
            lambda at: jnp.where(is_end(at), none, (3 - at) ^ 1),
        ],
        1,
        1,
        state,
    )[-1][None]


def solution(mesh):
    placed = (
        P(("grp", "req"), None, "kvh", None),
        P(("grp", "req"), None, None),
        P(("grp", "req"), None),
        P(("grp", "req"), None),
        P(("grp", "req"), None),
        P(("grp", "req"), None, "kvh"),
        P(("grp", "req"), None, "kvh", None),
    )
    return jax.shard_map(
        functools.partial(on_device, mesh.shape["req"]),
        mesh=mesh,
        in_specs=placed,
        out_specs=P(("grp", "req"), None, "kvh"),
        check_vma=False,
    )
```

```python
import functools
import math

import jax
import jax.numpy as jnp
from jax import lax
from jax.experimental import pallas as pl
from jax.experimental.pallas import tpu as pltpu
from jax.sharding import PartitionSpec as P

rope_base = 500000.0
tile_rows = 64
unit_blocks = 6
low = -1e30
bound = 105.0
grain = 2
chunk = 3
vmem = pl.BlockSpec(memory_space=pltpu.VMEM)
smem = pl.BlockSpec(memory_space=pltpu.SMEM)
anywhere = pl.BlockSpec(memory_space=pl.ANY)
params = pltpu.CompilerParams(vmem_limit_bytes=28 << 20)


def near(array):
    return pltpu.with_memory_space_constraint(array, pltpu.VMEM)


def held(array):
    return pltpu.with_memory_space_constraint(array, pltpu.SMEM)


def away(array):
    return pltpu.with_memory_space_constraint(array, pltpu.HBM)


def tables(position, head_dim):
    lane = lax.broadcasted_iota(jnp.int32, (position.shape[0], head_dim), 1)
    half_dim = head_dim // 2
    pair_index = (lane % half_dim).astype(jnp.float32)
    inv_freq = jnp.exp(pair_index * (-2.0 / head_dim) * jnp.log(jnp.float32(rope_base)))
    angles = position[:, None] * inv_freq
    sine = jnp.sin(angles)
    return jnp.cos(angles), jnp.where(lane < half_dim, -sine, sine)


def turn(field, cosine, sine):
    return field * cosine + pltpu.roll(field, field.shape[1] // 2, 1) * sine


def prepare(
    query_ref, fresh_ref, store_ref, owner_ref, slot_ref, span_ref, pos_ref, place_ref, cos_ref, sin_ref,
    turned_ref, placed_ref, near_ref, table_ref, peak_ref,
    raw_ref, flat_ref, wide_ref, all_ref, lanes_ref, row_smem, owner_smem, slot_smem, span_smem, sems,
):
    heads, tiles, lanes_rows, dim = turned_ref.shape
    group = lanes_rows // tile_rows
    placed_rows = placed_ref.shape[0]
    rows = cos_ref.shape[0]
    blocks = slot_ref.shape[1]

    def load_query(tile):
        at = pl.ds(pl.multiple_of(tile * tile_rows, tile_rows), tile_rows)
        return pltpu.make_async_copy(query_ref.at[at, :], raw_ref.at[at, :], sems.at[tile])

    small = [
        pltpu.make_async_copy(source, target, sems.at[tiles + number])
        for number, (source, target) in enumerate(
            (
                (pos_ref, lanes_ref),
                (fresh_ref, flat_ref),
                (pos_ref, row_smem),
                (owner_ref, owner_smem),
                (slot_ref, slot_smem),
                (span_ref, span_smem),
                (store_ref, near_ref),
            )
        )
    ]
    for copy in small[:-1]:
        copy.start()
    for tile in range(tiles):
        load_query(tile).start()
    small[-1].start()
    for copy in small[:-1]:
        copy.wait()
    wide_ref[...] = flat_ref[...].astype(jnp.float32)
    for head in range(heads):
        key = wide_ref[pl.ds(head, rows, stride=2 * heads), :]
        value = wide_ref[pl.ds(heads + head, rows, stride=2 * heads), :]
        all_ref[:, head * 2 * dim : head * 2 * dim + dim] = turn(
            key, cos_ref[...], sin_ref[...]
        ).astype(jnp.bfloat16)
        all_ref[:, head * 2 * dim + dim : (head + 1) * 2 * dim] = value.astype(jnp.bfloat16)
    all_ref[:, heads * 2 * dim :] = jnp.ones((rows, dim), jnp.bfloat16)
    step = 512

    def place(number, carry):
        at = pl.ds(pl.multiple_of(number * step, step), step)
        spot = lax.broadcasted_iota(jnp.int32, (step, rows), 0) + number * step
        chosen = jnp.where(spot == lanes_ref[...], 1.0, 0.0).astype(jnp.bfloat16)
        placed_ref[at, :] = jnp.dot(
            chosen, all_ref[...], preferred_element_type=jnp.float32
        ).astype(jnp.bfloat16)
        return carry

    lax.fori_loop(0, placed_rows // step, place, 0)

    def note(block, carry):
        began = jnp.int32(0)
        start = jnp.int32(0)
        for span in range(span_ref.shape[1]):
            began = jnp.where(start <= block, start, began)
            start = start + span_smem[0, span]
        table_ref[block] = owner_smem[0, block]
        table_ref[blocks + block] = slot_smem[0, block]
        table_ref[2 * blocks + block] = began
        return carry

    lax.fori_loop(0, blocks, note, 0)
    for tile in range(tiles):
        table_ref[3 * blocks + tile] = row_smem[0, (tile + 1) * tile_rows - 1]
    table_ref[3 * blocks + tiles] = place_ref[0]
    ones = jnp.ones((dim, dim), jnp.bfloat16)

    def turn_tile(tile, peak):
        load_query(tile).wait()
        at = pl.ds(pl.multiple_of(tile * tile_rows, tile_rows), tile_rows)
        cosine = cos_ref[at, :]
        sine = sin_ref[at, :]
        for head in range(heads):
            squares = []
            for member in range(group):
                column = (head * group + member) * dim
                field = raw_ref[at, column : column + dim].astype(jnp.float32)
                turned_ref[head, tile, member * tile_rows : (member + 1) * tile_rows, :] = turn(
                    field, cosine, sine
                ).astype(jnp.bfloat16)
                squares.append((field * field).astype(jnp.bfloat16))
            lengths = jnp.dot(
                jnp.concatenate(squares, axis=0), ones, preferred_element_type=jnp.float32
            )
            peak = jnp.maximum(peak, jnp.max(lengths.reshape(-1, 8, dim), axis=0))
        return peak

    peak = lax.fori_loop(0, tiles, turn_tile, jnp.zeros((8, dim), jnp.float32))
    peak_ref[0] = jnp.max(peak)
    small[-1].wait()


def attend(shards, pick, units, first, last, *refs):
    given = len(pick)
    sources = refs[:given]
    table_ref, calm_in, turned_ref, placed_ref, cos_ref, sin_ref, row_ref = refs[given : given + 7]
    refs = refs[given + 7 :]
    if not first:
        most_in, sum_in, acc_in = refs[:3]
        refs = refs[3:]
    most_out, sum_out, acc_out, calm_out = refs[:4]
    refs = refs[4:]
    if last:
        out_ref = refs[0]
        refs = refs[1:]
    wide_ref, key_ref, value_ref, list_ref = refs
    heads, tiles, lanes_rows, dim = turned_ref.shape
    group = lanes_rows // tile_rows
    blocks = cos_ref.shape[0]
    block_len = placed_ref.shape[0] // blocks
    stride = 2 * heads
    raw_rows = block_len * stride
    slots = sources[0].shape[0] // raw_rows // shards
    scale = dim**-0.5 * math.log2(math.e)
    lowest = [choose(table_ref[3 * blocks + tiles]) for choose in pick]
    spots = units * unit_blocks

    def find(block, found):
        owner = table_ref[block]
        hit = jnp.bool_(False)
        for base in lowest:
            hit = hit | ((owner >= base) & (owner < base + shards))
        list_ref[found] = block
        return found + hit.astype(jnp.int32)

    lax.fori_loop(0, blocks, find, jnp.int32(0))
    ones = jnp.ones((dim, dim), jnp.bfloat16)

    def load(turn_number, peak):
        for lane in range(chunk):
            spot = turn_number * chunk + lane
            block = list_ref[spot]
            owner = table_ref[block]
            raw = None
            for source, base in zip(sources, lowest):
                here = (owner >= base) & (owner < base + shards)
                start = ((owner - base) * slots + table_ref[blocks + block]) * raw_rows
                start = pl.multiple_of(jnp.where(here, start, 0), raw_rows)
                found = source[pl.ds(start, raw_rows), :].astype(jnp.float32)
                raw = found if raw is None else jnp.where(here, found, raw)
            wide_ref[lane] = raw
            began = table_ref[2 * blocks + block]
            cosine = cos_ref[pl.ds(began, 1), :]
            sine = sin_ref[pl.ds(began, 1), :]
            fresh = placed_ref[
                pl.ds(pl.multiple_of(block * block_len, block_len), block_len), :
            ].astype(jnp.float32)
            renewed = fresh[:, heads * 2 * dim :] > 0.5
            at = pl.ds(pl.multiple_of(spot * block_len, block_len), block_len)
            for head in range(heads):
                key = turn(wide_ref[lane, pl.ds(head, block_len, stride=stride), :], cosine, sine)
                value = wide_ref[lane, pl.ds(heads + head, block_len, stride=stride), :]
                begin = head * 2 * dim
                key = jnp.where(renewed, fresh[:, begin : begin + dim], key)
                key_ref[head, at, :] = key.astype(jnp.bfloat16)
                value_ref[head, at, :] = jnp.where(
                    renewed, fresh[:, begin + dim : begin + 2 * dim], value
                ).astype(jnp.bfloat16)
                lengths = jnp.dot(
                    (key * key).astype(jnp.bfloat16), ones, preferred_element_type=jnp.float32
                )
                peak = jnp.maximum(peak, jnp.max(lengths.reshape(-1, 8, dim), axis=0))
        return peak

    peak = lax.fori_loop(0, spots // chunk, load, jnp.zeros((8, dim), jnp.float32))
    room = (calm_in[0] < 1e38) & (calm_in[0] * jnp.max(peak) <= (bound / scale) ** 2)
    calm = room.astype(jnp.float32)
    calm_out[0] = jnp.where(room, calm_in[0], jnp.float32(3e38))

    def query_mask(tile):
        row_at = pl.ds(pl.multiple_of(tile * tile_rows, tile_rows), tile_rows)
        row_pos = row_ref[row_at, :]
        lane = lax.broadcasted_iota(jnp.int32, (tile_rows, block_len), 1)
        return lambda spot: (lane + list_ref[spot] * block_len <= row_pos)[None]

    def scored(head, tile, first_spot, count, seen):
        at = pl.ds(pl.multiple_of(first_spot * block_len, block_len), count * block_len)
        scores = lax.dot_general(
            turned_ref[head, tile],
            key_ref[head, at, :],
            (((1,), (1,)), ((), ())),
            preferred_element_type=jnp.float32,
        )
        return at, [
            jnp.where(
                seen[spot],
                scores[:, spot * block_len : (spot + 1) * block_len].reshape(
                    group, tile_rows, block_len
                ),
                2 * low,
            ).reshape(lanes_rows, block_len)
            for spot in range(count)
        ]

    def weighed(head, at, parts):
        return functools.reduce(jnp.add, parts), jnp.dot(
            jnp.concatenate([part.astype(jnp.bfloat16) for part in parts], axis=1),
            value_ref[head, at, :],
            preferred_element_type=jnp.float32,
        )

    def write(head, tile, total, acc):
        sum_out[head, tile] = total
        acc_out[head, tile] = acc

    def finish(head, tile, total, acc):
        result = (acc / jnp.sum(total, axis=1, keepdims=True)).astype(jnp.bfloat16)
        row_at = pl.ds(pl.multiple_of(tile * tile_rows, tile_rows), tile_rows)
        for member in range(group):
            column = (head * group + member) * dim
            out_ref[row_at, column : column + dim] = result[
                member * tile_rows : (member + 1) * tile_rows
            ]

    def quick(tile, carry):
        furthest = table_ref[3 * blocks + tile]
        visible = query_mask(tile)
        for unit in range(units):
            fresh = first and unit == 0
            ends = last and unit == units - 1
            before = (sum_in, acc_in) if unit == 0 and not first else (sum_out, acc_out)
            first_spot = unit * unit_blocks
            active = jnp.int32(0)
            for spot in range(unit_blocks):
                begins = list_ref[first_spot + spot] * block_len
                active = active + (begins <= furthest).astype(jnp.int32)
            after = finish if ends else write
            for count in range(0, unit_blocks + 1, grain):

                @pl.when((active + grain - 1) // grain == count // grain)
                def _(count=count):
                    if not count and not fresh and not ends:
                        return
                    seen = [visible(first_spot + spot) for spot in range(count)]
                    for head in range(heads):
                        total = acc = jnp.zeros((lanes_rows, dim), jnp.float32)
                        if count:
                            at, parts = scored(head, tile, first_spot, count, seen)
                            parts = [jnp.exp2(part * scale) for part in parts]
                            total, acc = weighed(head, at, parts)
                        if not fresh:
                            total = before[0][head, tile] + total
                            acc = before[1][head, tile] + acc
                        after(head, tile, total, acc)

        return carry

    def careful(tile, carry):
        furthest = table_ref[3 * blocks + tile]
        visible = query_mask(tile)

        def begin(head, ignored):
            if first:
                nothing = jnp.zeros((lanes_rows, dim), jnp.float32)
                most_out[head, tile] = nothing + low
                write(head, tile, nothing, nothing)
            else:
                total = sum_in[head, tile]
                most_out[head, tile] = jnp.where(
                    calm_in[0] < 1e38,
                    jnp.where(jnp.max(total, axis=1, keepdims=True) > 0, 0.0, low),
                    most_in[head, tile],
                )
                write(head, tile, total, acc_in[head, tile])
            return ignored

        lax.fori_loop(0, heads, begin, 0)

        def one(step, ignored):
            head = step % heads
            spot = step // heads

            @pl.when(list_ref[spot] * block_len <= furthest)
            def _():
                at, parts = scored(head, tile, spot, 1, [visible(spot)])
                was = most_out[head, tile]
                most = jnp.maximum(was, jnp.max(parts[0], axis=1, keepdims=True))
                total, acc = weighed(head, at, [jnp.exp2((parts[0] - most) * scale)])
                shrink = jnp.exp2((was - most) * scale)
                most_out[head, tile] = most
                write(
                    head,
                    tile,
                    sum_out[head, tile] * shrink + total,
                    acc_out[head, tile] * shrink + acc,
                )

            return ignored

        lax.fori_loop(0, spots * heads, one, 0)
        if last:
            for head in range(heads):
                finish(head, tile, sum_out[head, tile], acc_out[head, tile])
        return carry

    @pl.when(calm > 0.5)
    def _():
        lax.fori_loop(0, tiles, quick, 0)

    @pl.when(calm < 0.5)
    def _():
        lax.fori_loop(0, tiles, careful, 0)


def on_device(count, store_kv, block_owner, block_slot, span_len, row_index, fresh_q, fresh_kv):
    stored, block_len, heads, pair_width = store_kv.shape
    dim = pair_width // 2
    blocks = block_slot.shape[1]
    rows = row_index.shape[1]
    group = fresh_q.shape[2] // (heads * dim)
    tiles = rows // tile_rows
    lanes_rows = tile_rows * group
    raw_rows = block_len * 2 * heads

    def flat(array):
        lead = math.prod(array.shape[:-2])
        split = array.reshape(lead, heads, 2, dim)
        return split.transpose(0, 2, 1, 3).reshape(lead * 2 * heads, dim)

    store = flat(store_kv)
    place = lax.axis_index("req").reshape(1)
    row_pos = row_index[0]
    row_cos, row_sin = tables(row_pos.astype(jnp.float32), dim)
    cos, sin = tables(block_len * jnp.arange(blocks, dtype=jnp.float32), dim)
    row_lanes = jnp.broadcast_to(row_pos[:, None], (rows, block_len))
    wide = heads * 2 * dim + dim
    turned, placed, close, table, peak = pl.pallas_call(
        prepare,
        out_shape=(
            pltpu.VMEM((heads, tiles, lanes_rows, dim), jnp.bfloat16),
            pltpu.VMEM((blocks * block_len, wide), jnp.bfloat16),
            pltpu.VMEM(store.shape, jnp.bfloat16),
            pltpu.SMEM((3 * blocks + tiles + 1,), jnp.int32),
            pltpu.SMEM((1,), jnp.float32),
        ),
        in_specs=[anywhere] * 7 + [smem, vmem, vmem],
        out_specs=(vmem, vmem, vmem, smem, smem),
        scratch_shapes=[
            pltpu.VMEM((rows, heads * group * dim), jnp.bfloat16),
            pltpu.VMEM((rows * 2 * heads, dim), jnp.bfloat16),
            pltpu.VMEM((rows * 2 * heads, dim), jnp.float32),
            pltpu.VMEM((rows, wide), jnp.bfloat16),
            pltpu.VMEM((1, rows), jnp.int32),
            pltpu.SMEM((1, rows), jnp.int32),
            pltpu.SMEM((1, blocks), jnp.int32),
            pltpu.SMEM((1, blocks), jnp.int32),
            pltpu.SMEM(span_len.shape, jnp.int32),
            pltpu.SemaphoreType.DMA((tiles + 7,)),
        ],
        compiler_params=params,
        name="prepare",
    )(
        away(fresh_q[0]), away(flat(fresh_kv)), away(store), away(block_owner[:, :, 0]),
        away(block_slot), away(span_len), away(row_index), place, near(row_cos), near(row_sin),
    )

    def attention(number, last, sources, pick, shards, units, state):
        first = len(state) == 1
        state_shape = pltpu.VMEM((heads, tiles, lanes_rows, dim), jnp.float32)
        inputs = [near(source) for source in sources]
        inputs += [held(table), held(state[-1])]
        inputs += [near(array) for array in (turned, placed, cos, sin, row_lanes)]
        specs = [vmem] * len(sources) + [smem] * 2 + [vmem] * 5
        spots = units * unit_blocks
        result = [jax.ShapeDtypeStruct((rows, heads * group * dim), jnp.bfloat16)] if last else []
        return pl.pallas_call(
            functools.partial(attend, shards, pick, units, first, last),
            out_shape=[state_shape] * 3 + [pltpu.SMEM((1,), jnp.float32)] + result,
            in_specs=specs + [vmem] * (len(state) - 1),
            out_specs=[vmem] * 3 + [smem] + [vmem] * len(result),
            input_output_aliases={}
            if first
            else {len(specs) + entry: entry for entry in range(3)},
            scratch_shapes=[
                pltpu.VMEM((chunk, raw_rows, dim), jnp.float32),
                pltpu.VMEM((heads, spots * block_len, dim), jnp.bfloat16),
                pltpu.VMEM((heads, spots * block_len, dim), jnp.bfloat16),
                pltpu.SMEM((blocks + 1,), jnp.int32),
            ],
            compiler_params=params,
            name=f"attend_{number}",
        )(*inputs, *[near(entry) for entry in state[:-1]])

    if count != 4:
        everything = lax.all_gather(store, "req", axis=0, tiled=True)
        return attention(
            0, True, [everything], [lambda at: 0], count, blocks // unit_blocks, (peak,)
        )[-1][None]
    outer = [(0, 1), (1, 0), (2, 3), (3, 2)]
    inner = [(1, 2), (2, 1)]
    outward = [(1, 0), (2, 3)]
    none = -(1 << 16)
    is_end = lambda at: (at == 0) | (at == 3)

    def send(array, pairs):
        return lax.ppermute(array, "req", pairs)

    beside = send(store, outer)
    across = send(store, inner)
    store, close, turned = lax.optimization_barrier((store, close, turned))
    third_in = send(store, [(0, 2), (3, 1)])
    beside, across, close, turned = lax.optimization_barrier((beside, across, close, turned))
    second = send(across, outward)
    state = attention(0, False, [close, beside], [lambda at: at, lambda at: at ^ 1], 1, 2, (peak,))
    second, third_in, state = lax.optimization_barrier((second, third_in, state))
    third = send(third_in, outward)
    state = attention(
        1,
        False,
        [second, across],
        [
            lambda at: jnp.where(is_end(at), jnp.where(at == 0, 2, 1), none),
            lambda at: jnp.where(is_end(at), none, 3 - at),
        ],
        1,
        1,
        state,
    )
    third, state = lax.optimization_barrier((third, state))
    return attention(
        2,
        True,
        [third, third_in],
        [
            lambda at: jnp.where(is_end(at), 3 - at, none),
            lambda at: jnp.where(is_end(at), none, (3 - at) ^ 1),
        ],
        1,
        1,
        state,
    )[-1][None]


def solution(mesh):
    placed = (
        P(("grp", "req"), None, "kvh", None),
        P(("grp", "req"), None, None),
        P(("grp", "req"), None),
        P(("grp", "req"), None),
        P(("grp", "req"), None),
        P(("grp", "req"), None, "kvh"),
        P(("grp", "req"), None, "kvh", None),
    )
    return jax.shard_map(
        functools.partial(on_device, mesh.shape["req"]),
        mesh=mesh,
        in_specs=placed,
        out_specs=P(("grp", "req"), None, "kvh"),
        check_vma=False,
    )
```

```python
import functools
import math

import jax
import jax.numpy as jnp
from jax import lax
from jax.experimental import pallas as pl
from jax.experimental.pallas import tpu as pltpu
from jax.sharding import PartitionSpec as P

rope_base = 500000.0
tile_rows = 64
unit_blocks = 6
low = -1e30
bound = 105.0
grain = 1
chunk = 6
vmem = pl.BlockSpec(memory_space=pltpu.VMEM)
smem = pl.BlockSpec(memory_space=pltpu.SMEM)
anywhere = pl.BlockSpec(memory_space=pl.ANY)
params = pltpu.CompilerParams(vmem_limit_bytes=28 << 20)


def near(array):
    return pltpu.with_memory_space_constraint(array, pltpu.VMEM)


def held(array):
    return pltpu.with_memory_space_constraint(array, pltpu.SMEM)


def away(array):
    return pltpu.with_memory_space_constraint(array, pltpu.HBM)


def tables(position, head_dim):
    lane = lax.broadcasted_iota(jnp.int32, (position.shape[0], head_dim), 1)
    half_dim = head_dim // 2
    pair_index = (lane % half_dim).astype(jnp.float32)
    inv_freq = jnp.exp(pair_index * (-2.0 / head_dim) * jnp.log(jnp.float32(rope_base)))
    angles = position[:, None] * inv_freq
    sine = jnp.sin(angles)
    return jnp.cos(angles), jnp.where(lane < half_dim, -sine, sine)


def turn(field, cosine, sine):
    return field * cosine + pltpu.roll(field, field.shape[1] // 2, 1) * sine


def prepare(
    query_ref, fresh_ref, store_ref, owner_ref, slot_ref, span_ref, pos_ref, place_ref, cos_ref, sin_ref,
    turned_ref, placed_ref, near_ref, table_ref, peak_ref,
    raw_ref, flat_ref, wide_ref, all_ref, lanes_ref, row_smem, owner_smem, slot_smem, span_smem, sems,
):
    heads, tiles, lanes_rows, dim = turned_ref.shape
    group = lanes_rows // tile_rows
    placed_rows = placed_ref.shape[0]
    rows = cos_ref.shape[0]
    blocks = slot_ref.shape[1]

    def load_query(tile):
        at = pl.ds(pl.multiple_of(tile * tile_rows, tile_rows), tile_rows)
        return pltpu.make_async_copy(query_ref.at[at, :], raw_ref.at[at, :], sems.at[tile])

    small = [
        pltpu.make_async_copy(source, target, sems.at[tiles + number])
        for number, (source, target) in enumerate(
            (
                (pos_ref, lanes_ref),
                (fresh_ref, flat_ref),
                (pos_ref, row_smem),
                (owner_ref, owner_smem),
                (slot_ref, slot_smem),
                (span_ref, span_smem),
                (store_ref, near_ref),
            )
        )
    ]
    for copy in small[:-1]:
        copy.start()
    for tile in range(tiles):
        load_query(tile).start()
    small[-1].start()
    for copy in small[:-1]:
        copy.wait()
    wide_ref[...] = flat_ref[...].astype(jnp.float32)
    for head in range(heads):
        key = wide_ref[pl.ds(head, rows, stride=2 * heads), :]
        value = wide_ref[pl.ds(heads + head, rows, stride=2 * heads), :]
        all_ref[:, head * 2 * dim : head * 2 * dim + dim] = turn(
            key, cos_ref[...], sin_ref[...]
        ).astype(jnp.bfloat16)
        all_ref[:, head * 2 * dim + dim : (head + 1) * 2 * dim] = value.astype(jnp.bfloat16)
    all_ref[:, heads * 2 * dim :] = jnp.ones((rows, dim), jnp.bfloat16)
    step = 512

    def place(number, carry):
        at = pl.ds(pl.multiple_of(number * step, step), step)
        spot = lax.broadcasted_iota(jnp.int32, (step, rows), 0) + number * step
        chosen = jnp.where(spot == lanes_ref[...], 1.0, 0.0).astype(jnp.bfloat16)
        placed_ref[at, :] = jnp.dot(
            chosen, all_ref[...], preferred_element_type=jnp.float32
        ).astype(jnp.bfloat16)
        return carry

    lax.fori_loop(0, placed_rows // step, place, 0)

    def note(block, carry):
        began = jnp.int32(0)
        start = jnp.int32(0)
        for span in range(span_ref.shape[1]):
            began = jnp.where(start <= block, start, began)
            start = start + span_smem[0, span]
        table_ref[block] = owner_smem[0, block]
        table_ref[blocks + block] = slot_smem[0, block]
        table_ref[2 * blocks + block] = began
        return carry

    lax.fori_loop(0, blocks, note, 0)
    for tile in range(tiles):
        table_ref[3 * blocks + tile] = row_smem[0, (tile + 1) * tile_rows - 1]
    table_ref[3 * blocks + tiles] = place_ref[0]
    ones = jnp.ones((dim, dim), jnp.bfloat16)

    def turn_tile(tile, peak):
        load_query(tile).wait()
        at = pl.ds(pl.multiple_of(tile * tile_rows, tile_rows), tile_rows)
        cosine = cos_ref[at, :]
        sine = sin_ref[at, :]
        for head in range(heads):
            squares = []
            for member in range(group):
                column = (head * group + member) * dim
                field = raw_ref[at, column : column + dim].astype(jnp.float32)
                turned_ref[head, tile, member * tile_rows : (member + 1) * tile_rows, :] = turn(
                    field, cosine, sine
                ).astype(jnp.bfloat16)
                squares.append((field * field).astype(jnp.bfloat16))
            lengths = jnp.dot(
                jnp.concatenate(squares, axis=0), ones, preferred_element_type=jnp.float32
            )
            peak = jnp.maximum(peak, jnp.max(lengths.reshape(-1, 8, dim), axis=0))
        return peak

    peak = lax.fori_loop(0, tiles, turn_tile, jnp.zeros((8, dim), jnp.float32))
    peak_ref[0] = jnp.max(peak)
    small[-1].wait()


def attend(shards, pick, units, first, last, *refs):
    given = len(pick)
    sources = refs[:given]
    table_ref, calm_in, turned_ref, placed_ref, cos_ref, sin_ref, row_ref = refs[given : given + 7]
    refs = refs[given + 7 :]
    if not first:
        most_in, sum_in, acc_in = refs[:3]
        refs = refs[3:]
    most_out, sum_out, acc_out, calm_out = refs[:4]
    refs = refs[4:]
    if last:
        out_ref = refs[0]
        refs = refs[1:]
    wide_ref, key_ref, value_ref, list_ref = refs
    heads, tiles, lanes_rows, dim = turned_ref.shape
    group = lanes_rows // tile_rows
    blocks = cos_ref.shape[0]
    block_len = placed_ref.shape[0] // blocks
    stride = 2 * heads
    raw_rows = block_len * stride
    slots = sources[0].shape[0] // raw_rows // shards
    scale = dim**-0.5 * math.log2(math.e)
    lowest = [choose(table_ref[3 * blocks + tiles]) for choose in pick]
    spots = units * unit_blocks

    def find(block, found):
        owner = table_ref[block]
        hit = jnp.bool_(False)
        for base in lowest:
            hit = hit | ((owner >= base) & (owner < base + shards))
        list_ref[found] = block
        return found + hit.astype(jnp.int32)

    lax.fori_loop(0, blocks, find, jnp.int32(0))
    ones = jnp.ones((dim, dim), jnp.bfloat16)

    def load(turn_number, peak):
        for lane in range(chunk):
            spot = turn_number * chunk + lane
            block = list_ref[spot]
            owner = table_ref[block]
            raw = None
            for source, base in zip(sources, lowest):
                here = (owner >= base) & (owner < base + shards)
                start = ((owner - base) * slots + table_ref[blocks + block]) * raw_rows
                start = pl.multiple_of(jnp.where(here, start, 0), raw_rows)
                found = source[pl.ds(start, raw_rows), :].astype(jnp.float32)
                raw = found if raw is None else jnp.where(here, found, raw)
            wide_ref[lane] = raw
            began = table_ref[2 * blocks + block]
            cosine = cos_ref[pl.ds(began, 1), :]
            sine = sin_ref[pl.ds(began, 1), :]
            fresh = placed_ref[
                pl.ds(pl.multiple_of(block * block_len, block_len), block_len), :
            ].astype(jnp.float32)
            renewed = fresh[:, heads * 2 * dim :] > 0.5
            at = pl.ds(pl.multiple_of(spot * block_len, block_len), block_len)
            for head in range(heads):
                key = turn(wide_ref[lane, pl.ds(head, block_len, stride=stride), :], cosine, sine)
                value = wide_ref[lane, pl.ds(heads + head, block_len, stride=stride), :]
                begin = head * 2 * dim
                key = jnp.where(renewed, fresh[:, begin : begin + dim], key)
                key_ref[head, at, :] = key.astype(jnp.bfloat16)
                value_ref[head, at, :] = jnp.where(
                    renewed, fresh[:, begin + dim : begin + 2 * dim], value
                ).astype(jnp.bfloat16)
                lengths = jnp.dot(
                    (key * key).astype(jnp.bfloat16), ones, preferred_element_type=jnp.float32
                )
                peak = jnp.maximum(peak, jnp.max(lengths.reshape(-1, 8, dim), axis=0))
        return peak

    peak = lax.fori_loop(0, spots // chunk, load, jnp.zeros((8, dim), jnp.float32))
    room = (calm_in[0] < 1e38) & (calm_in[0] * jnp.max(peak) <= (bound / scale) ** 2)
    calm = room.astype(jnp.float32)
    calm_out[0] = jnp.where(room, calm_in[0], jnp.float32(3e38))

    def query_mask(tile):
        row_at = pl.ds(pl.multiple_of(tile * tile_rows, tile_rows), tile_rows)
        row_pos = row_ref[row_at, :]
        lane = lax.broadcasted_iota(jnp.int32, (tile_rows, block_len), 1)
        return lambda spot: (lane + list_ref[spot] * block_len <= row_pos)[None]

    def scored(head, tile, first_spot, count, seen):
        at = pl.ds(pl.multiple_of(first_spot * block_len, block_len), count * block_len)
        scores = lax.dot_general(
            turned_ref[head, tile],
            key_ref[head, at, :],
            (((1,), (1,)), ((), ())),
            preferred_element_type=jnp.float32,
        )
        return at, [
            jnp.where(
                seen[spot],
                scores[:, spot * block_len : (spot + 1) * block_len].reshape(
                    group, tile_rows, block_len
                ),
                2 * low,
            ).reshape(lanes_rows, block_len)
            for spot in range(count)
        ]

    def weighed(head, at, parts):
        return functools.reduce(jnp.add, parts), jnp.dot(
            jnp.concatenate([part.astype(jnp.bfloat16) for part in parts], axis=1),
            value_ref[head, at, :],
            preferred_element_type=jnp.float32,
        )

    def write(head, tile, total, acc):
        sum_out[head, tile] = total
        acc_out[head, tile] = acc

    def finish(head, tile, total, acc):
        result = (acc / jnp.sum(total, axis=1, keepdims=True)).astype(jnp.bfloat16)
        row_at = pl.ds(pl.multiple_of(tile * tile_rows, tile_rows), tile_rows)
        for member in range(group):
            column = (head * group + member) * dim
            out_ref[row_at, column : column + dim] = result[
                member * tile_rows : (member + 1) * tile_rows
            ]

    def quick(tile, carry):
        furthest = table_ref[3 * blocks + tile]
        visible = query_mask(tile)
        for unit in range(units):
            fresh = first and unit == 0
            ends = last and unit == units - 1
            before = (sum_in, acc_in) if unit == 0 and not first else (sum_out, acc_out)
            first_spot = unit * unit_blocks
            active = jnp.int32(0)
            for spot in range(unit_blocks):
                begins = list_ref[first_spot + spot] * block_len
                active = active + (begins <= furthest).astype(jnp.int32)
            after = finish if ends else write
            for count in range(0, unit_blocks + 1, grain):

                @pl.when((active + grain - 1) // grain == count // grain)
                def _(count=count):
                    if not count and not fresh and not ends:
                        return
                    seen = [visible(first_spot + spot) for spot in range(count)]
                    for head in range(heads):
                        total = acc = jnp.zeros((lanes_rows, dim), jnp.float32)
                        if count:
                            at, parts = scored(head, tile, first_spot, count, seen)
                            parts = [jnp.exp2(part * scale) for part in parts]
                            total, acc = weighed(head, at, parts)
                        if not fresh:
                            total = before[0][head, tile] + total
                            acc = before[1][head, tile] + acc
                        after(head, tile, total, acc)

        return carry

    def careful(tile, carry):
        furthest = table_ref[3 * blocks + tile]
        visible = query_mask(tile)

        def begin(head, ignored):
            if first:
                nothing = jnp.zeros((lanes_rows, dim), jnp.float32)
                most_out[head, tile] = nothing + low
                write(head, tile, nothing, nothing)
            else:
                total = sum_in[head, tile]
                most_out[head, tile] = jnp.where(
                    calm_in[0] < 1e38,
                    jnp.where(jnp.max(total, axis=1, keepdims=True) > 0, 0.0, low),
                    most_in[head, tile],
                )
                write(head, tile, total, acc_in[head, tile])
            return ignored

        lax.fori_loop(0, heads, begin, 0)

        def one(step, ignored):
            head = step % heads
            spot = step // heads

            @pl.when(list_ref[spot] * block_len <= furthest)
            def _():
                at, parts = scored(head, tile, spot, 1, [visible(spot)])
                was = most_out[head, tile]
                most = jnp.maximum(was, jnp.max(parts[0], axis=1, keepdims=True))
                total, acc = weighed(head, at, [jnp.exp2((parts[0] - most) * scale)])
                shrink = jnp.exp2((was - most) * scale)
                most_out[head, tile] = most
                write(
                    head,
                    tile,
                    sum_out[head, tile] * shrink + total,
                    acc_out[head, tile] * shrink + acc,
                )

            return ignored

        lax.fori_loop(0, spots * heads, one, 0)
        if last:
            for head in range(heads):
                finish(head, tile, sum_out[head, tile], acc_out[head, tile])
        return carry

    @pl.when(calm > 0.5)
    def _():
        lax.fori_loop(0, tiles, quick, 0)

    @pl.when(calm < 0.5)
    def _():
        lax.fori_loop(0, tiles, careful, 0)


def on_device(count, store_kv, block_owner, block_slot, span_len, row_index, fresh_q, fresh_kv):
    stored, block_len, heads, pair_width = store_kv.shape
    dim = pair_width // 2
    blocks = block_slot.shape[1]
    rows = row_index.shape[1]
    group = fresh_q.shape[2] // (heads * dim)
    tiles = rows // tile_rows
    lanes_rows = tile_rows * group
    raw_rows = block_len * 2 * heads

    def flat(array):
        lead = math.prod(array.shape[:-2])
        split = array.reshape(lead, heads, 2, dim)
        return split.transpose(0, 2, 1, 3).reshape(lead * 2 * heads, dim)

    store = flat(store_kv)
    place = lax.axis_index("req").reshape(1)
    row_pos = row_index[0]
    row_cos, row_sin = tables(row_pos.astype(jnp.float32), dim)
    cos, sin = tables(block_len * jnp.arange(blocks, dtype=jnp.float32), dim)
    row_lanes = jnp.broadcast_to(row_pos[:, None], (rows, block_len))
    wide = heads * 2 * dim + dim
    turned, placed, close, table, peak = pl.pallas_call(
        prepare,
        out_shape=(
            pltpu.VMEM((heads, tiles, lanes_rows, dim), jnp.bfloat16),
            pltpu.VMEM((blocks * block_len, wide), jnp.bfloat16),
            pltpu.VMEM(store.shape, jnp.bfloat16),
            pltpu.SMEM((3 * blocks + tiles + 1,), jnp.int32),
            pltpu.SMEM((1,), jnp.float32),
        ),
        in_specs=[anywhere] * 7 + [smem, vmem, vmem],
        out_specs=(vmem, vmem, vmem, smem, smem),
        scratch_shapes=[
            pltpu.VMEM((rows, heads * group * dim), jnp.bfloat16),
            pltpu.VMEM((rows * 2 * heads, dim), jnp.bfloat16),
            pltpu.VMEM((rows * 2 * heads, dim), jnp.float32),
            pltpu.VMEM((rows, wide), jnp.bfloat16),
            pltpu.VMEM((1, rows), jnp.int32),
            pltpu.SMEM((1, rows), jnp.int32),
            pltpu.SMEM((1, blocks), jnp.int32),
            pltpu.SMEM((1, blocks), jnp.int32),
            pltpu.SMEM(span_len.shape, jnp.int32),
            pltpu.SemaphoreType.DMA((tiles + 7,)),
        ],
        compiler_params=params,
        name="prepare",
    )(
        away(fresh_q[0]), away(flat(fresh_kv)), away(store), away(block_owner[:, :, 0]),
        away(block_slot), away(span_len), away(row_index), place, near(row_cos), near(row_sin),
    )

    def attention(number, last, sources, pick, shards, units, state):
        first = len(state) == 1
        state_shape = pltpu.VMEM((heads, tiles, lanes_rows, dim), jnp.float32)
        inputs = [near(source) for source in sources]
        inputs += [held(table), held(state[-1])]
        inputs += [near(array) for array in (turned, placed, cos, sin, row_lanes)]
        specs = [vmem] * len(sources) + [smem] * 2 + [vmem] * 5
        spots = units * unit_blocks
        result = [jax.ShapeDtypeStruct((rows, heads * group * dim), jnp.bfloat16)] if last else []
        return pl.pallas_call(
            functools.partial(attend, shards, pick, units, first, last),
            out_shape=[state_shape] * 3 + [pltpu.SMEM((1,), jnp.float32)] + result,
            in_specs=specs + [vmem] * (len(state) - 1),
            out_specs=[vmem] * 3 + [smem] + [vmem] * len(result),
            input_output_aliases={}
            if first
            else {len(specs) + entry: entry for entry in range(3)},
            scratch_shapes=[
                pltpu.VMEM((chunk, raw_rows, dim), jnp.float32),
                pltpu.VMEM((heads, spots * block_len, dim), jnp.bfloat16),
                pltpu.VMEM((heads, spots * block_len, dim), jnp.bfloat16),
                pltpu.SMEM((blocks + 1,), jnp.int32),
            ],
            compiler_params=params,
            name=f"attend_{number}",
        )(*inputs, *[near(entry) for entry in state[:-1]])

    if count != 4:
        everything = lax.all_gather(store, "req", axis=0, tiled=True)
        return attention(
            0, True, [everything], [lambda at: 0], count, blocks // unit_blocks, (peak,)
        )[-1][None]
    outer = [(0, 1), (1, 0), (2, 3), (3, 2)]
    inner = [(1, 2), (2, 1)]
    outward = [(1, 0), (2, 3)]
    none = -(1 << 16)
    is_end = lambda at: (at == 0) | (at == 3)

    def send(array, pairs):
        return lax.ppermute(array, "req", pairs)

    beside = send(store, outer)
    across = send(store, inner)
    beside, close, turned = lax.optimization_barrier((beside, close, turned))
    third_in = send(beside, inner)
    across, close, turned = lax.optimization_barrier((across, close, turned))
    second = send(across, outward)
    state = attention(0, False, [close, beside], [lambda at: at, lambda at: at ^ 1], 1, 2, (peak,))
    second, third_in, state = lax.optimization_barrier((second, third_in, state))
    third = send(third_in, outward)
    state = attention(
        1,
        False,
        [second, across],
        [
            lambda at: jnp.where(is_end(at), jnp.where(at == 0, 2, 1), none),
            lambda at: jnp.where(is_end(at), none, 3 - at),
        ],
        1,
        1,
        state,
    )
    third, state = lax.optimization_barrier((third, state))
    return attention(
        2,
        True,
        [third, third_in],
        [
            lambda at: jnp.where(is_end(at), 3 - at, none),
            lambda at: jnp.where(is_end(at), none, (3 - at) ^ 1),
        ],
        1,
        1,
        state,
    )[-1][None]


def solution(mesh):
    placed = (
        P(("grp", "req"), None, "kvh", None),
        P(("grp", "req"), None, None),
        P(("grp", "req"), None),
        P(("grp", "req"), None),
        P(("grp", "req"), None),
        P(("grp", "req"), None, "kvh"),
        P(("grp", "req"), None, "kvh", None),
    )
    return jax.shard_map(
        functools.partial(on_device, mesh.shape["req"]),
        mesh=mesh,
        in_specs=placed,
        out_specs=P(("grp", "req"), None, "kvh"),
        check_vma=False,
    )
```

```python
import functools
import math

import jax
import jax.numpy as jnp
from jax import lax
from jax.experimental import pallas as pl
from jax.experimental.pallas import tpu as pltpu
from jax.sharding import PartitionSpec as P

rope_base = 500000.0
tile_rows = 64
unit_blocks = 6
low = -1e30
bound = 105.0
grain = 1
chunk = 6
vmem = pl.BlockSpec(memory_space=pltpu.VMEM)
smem = pl.BlockSpec(memory_space=pltpu.SMEM)
anywhere = pl.BlockSpec(memory_space=pl.ANY)
params = pltpu.CompilerParams(vmem_limit_bytes=28 << 20)


def near(array):
    return pltpu.with_memory_space_constraint(array, pltpu.VMEM)


def held(array):
    return pltpu.with_memory_space_constraint(array, pltpu.SMEM)


def away(array):
    return pltpu.with_memory_space_constraint(array, pltpu.HBM)


def tables(position, head_dim):
    lane = lax.broadcasted_iota(jnp.int32, (position.shape[0], head_dim), 1)
    half_dim = head_dim // 2
    pair_index = (lane % half_dim).astype(jnp.float32)
    inv_freq = jnp.exp(pair_index * (-2.0 / head_dim) * jnp.log(jnp.float32(rope_base)))
    angles = position[:, None] * inv_freq
    sine = jnp.sin(angles)
    return jnp.cos(angles), jnp.where(lane < half_dim, -sine, sine)


def turn(field, cosine, sine):
    return field * cosine + pltpu.roll(field, field.shape[1] // 2, 1) * sine


def prepare(
    query_ref, fresh_ref, store_ref, owner_ref, slot_ref, span_ref, pos_ref, place_ref, cos_ref, sin_ref,
    turned_ref, placed_ref, near_ref, table_ref, peak_ref,
    raw_ref, flat_ref, wide_ref, all_ref, lanes_ref, row_smem, owner_smem, slot_smem, span_smem, sems,
):
    heads, tiles, lanes_rows, dim = turned_ref.shape
    group = lanes_rows // tile_rows
    placed_rows = placed_ref.shape[0]
    rows = cos_ref.shape[0]
    blocks = slot_ref.shape[1]

    def load_query(tile):
        at = pl.ds(pl.multiple_of(tile * tile_rows, tile_rows), tile_rows)
        return pltpu.make_async_copy(query_ref.at[at, :], raw_ref.at[at, :], sems.at[tile])

    small = [
        pltpu.make_async_copy(source, target, sems.at[tiles + number])
        for number, (source, target) in enumerate(
            (
                (pos_ref, lanes_ref),
                (fresh_ref, flat_ref),
                (pos_ref, row_smem),
                (owner_ref, owner_smem),
                (slot_ref, slot_smem),
                (span_ref, span_smem),
                (store_ref, near_ref),
            )
        )
    ]
    for copy in small[:-1]:
        copy.start()
    for tile in range(tiles):
        load_query(tile).start()
    small[-1].start()
    for copy in small[:-1]:
        copy.wait()
    wide_ref[...] = flat_ref[...].astype(jnp.float32)
    for head in range(heads):
        key = wide_ref[pl.ds(head, rows, stride=2 * heads), :]
        value = wide_ref[pl.ds(heads + head, rows, stride=2 * heads), :]
        all_ref[:, head * 2 * dim : head * 2 * dim + dim] = turn(
            key, cos_ref[...], sin_ref[...]
        ).astype(jnp.bfloat16)
        all_ref[:, head * 2 * dim + dim : (head + 1) * 2 * dim] = value.astype(jnp.bfloat16)
    all_ref[:, heads * 2 * dim :] = jnp.ones((rows, dim), jnp.bfloat16)
    step = 512

    def place(number, carry):
        at = pl.ds(pl.multiple_of(number * step, step), step)
        spot = lax.broadcasted_iota(jnp.int32, (step, rows), 0) + number * step
        chosen = jnp.where(spot == lanes_ref[...], 1.0, 0.0).astype(jnp.bfloat16)
        placed_ref[at, :] = jnp.dot(
            chosen, all_ref[...], preferred_element_type=jnp.float32
        ).astype(jnp.bfloat16)
        return carry

    lax.fori_loop(0, placed_rows // step, place, 0)

    def note(block, carry):
        began = jnp.int32(0)
        start = jnp.int32(0)
        for span in range(span_ref.shape[1]):
            began = jnp.where(start <= block, start, began)
            start = start + span_smem[0, span]
        table_ref[block] = owner_smem[0, block]
        table_ref[blocks + block] = slot_smem[0, block]
        table_ref[2 * blocks + block] = began
        return carry

    lax.fori_loop(0, blocks, note, 0)
    for tile in range(tiles):
        table_ref[3 * blocks + tile] = row_smem[0, (tile + 1) * tile_rows - 1]
    table_ref[3 * blocks + tiles] = place_ref[0]
    ones = jnp.ones((dim, dim), jnp.bfloat16)

    def turn_tile(tile, peak):
        load_query(tile).wait()
        at = pl.ds(pl.multiple_of(tile * tile_rows, tile_rows), tile_rows)
        cosine = cos_ref[at, :]
        sine = sin_ref[at, :]
        for head in range(heads):
            squares = []
            for member in range(group):
                column = (head * group + member) * dim
                field = raw_ref[at, column : column + dim].astype(jnp.float32)
                turned_ref[head, tile, member * tile_rows : (member + 1) * tile_rows, :] = turn(
                    field, cosine, sine
                ).astype(jnp.bfloat16)
                squares.append((field * field).astype(jnp.bfloat16))
            lengths = jnp.dot(
                jnp.concatenate(squares, axis=0), ones, preferred_element_type=jnp.float32
            )
            peak = jnp.maximum(peak, jnp.max(lengths.reshape(-1, 8, dim), axis=0))
        return peak

    peak = lax.fori_loop(0, tiles, turn_tile, jnp.zeros((8, dim), jnp.float32))
    peak_ref[0] = jnp.max(peak)
    small[-1].wait()


def attend(shards, pick, units, first, last, *refs):
    given = len(pick)
    sources = refs[:given]
    table_ref, calm_in, turned_ref, placed_ref, cos_ref, sin_ref, row_ref = refs[given : given + 7]
    refs = refs[given + 7 :]
    if not first:
        most_in, sum_in, acc_in = refs[:3]
        refs = refs[3:]
    most_out, sum_out, acc_out, calm_out = refs[:4]
    refs = refs[4:]
    if last:
        out_ref = refs[0]
        refs = refs[1:]
    wide_ref, key_ref, value_ref, list_ref = refs
    heads, tiles, lanes_rows, dim = turned_ref.shape
    group = lanes_rows // tile_rows
    blocks = cos_ref.shape[0]
    block_len = placed_ref.shape[0] // blocks
    stride = 2 * heads
    raw_rows = block_len * stride
    slots = sources[0].shape[0] // raw_rows // shards
    scale = dim**-0.5 * math.log2(math.e)
    lowest = [choose(table_ref[3 * blocks + tiles]) for choose in pick]
    spots = units * unit_blocks

    def find(block, found):
        owner = table_ref[block]
        hit = jnp.bool_(False)
        for base in lowest:
            hit = hit | ((owner >= base) & (owner < base + shards))
        list_ref[found] = block
        return found + hit.astype(jnp.int32)

    lax.fori_loop(0, blocks, find, jnp.int32(0))
    ones = jnp.ones((dim, dim), jnp.bfloat16)

    def load(turn_number, peak):
        for lane in range(chunk):
            spot = turn_number * chunk + lane
            block = list_ref[spot]
            owner = table_ref[block]
            raw = None
            for source, base in zip(sources, lowest):
                here = (owner >= base) & (owner < base + shards)
                start = ((owner - base) * slots + table_ref[blocks + block]) * raw_rows
                start = pl.multiple_of(jnp.where(here, start, 0), raw_rows)
                found = source[pl.ds(start, raw_rows), :].astype(jnp.float32)
                raw = found if raw is None else jnp.where(here, found, raw)
            wide_ref[lane] = raw
            began = table_ref[2 * blocks + block]
            cosine = cos_ref[pl.ds(began, 1), :]
            sine = sin_ref[pl.ds(began, 1), :]
            fresh = placed_ref[
                pl.ds(pl.multiple_of(block * block_len, block_len), block_len), :
            ].astype(jnp.float32)
            renewed = fresh[:, heads * 2 * dim :] > 0.5
            at = pl.ds(pl.multiple_of(spot * block_len, block_len), block_len)
            for head in range(heads):
                key = turn(wide_ref[lane, pl.ds(head, block_len, stride=stride), :], cosine, sine)
                value = wide_ref[lane, pl.ds(heads + head, block_len, stride=stride), :]
                begin = head * 2 * dim
                key = jnp.where(renewed, fresh[:, begin : begin + dim], key)
                key_ref[head, at, :] = key.astype(jnp.bfloat16)
                value_ref[head, at, :] = jnp.where(
                    renewed, fresh[:, begin + dim : begin + 2 * dim], value
                ).astype(jnp.bfloat16)
                lengths = jnp.dot(
                    (key * key).astype(jnp.bfloat16), ones, preferred_element_type=jnp.float32
                )
                peak = jnp.maximum(peak, jnp.max(lengths.reshape(-1, 8, dim), axis=0))
        return peak

    peak = lax.fori_loop(0, spots // chunk, load, jnp.zeros((8, dim), jnp.float32))
    room = (calm_in[0] < 1e38) & (calm_in[0] * jnp.max(peak) <= (bound / scale) ** 2)
    calm = room.astype(jnp.float32)
    calm_out[0] = jnp.where(room, calm_in[0], jnp.float32(3e38))

    def query_mask(tile):
        row_at = pl.ds(pl.multiple_of(tile * tile_rows, tile_rows), tile_rows)
        row_pos = row_ref[row_at, :]
        lane = lax.broadcasted_iota(jnp.int32, (tile_rows, block_len), 1)
        return lambda spot: (lane + list_ref[spot] * block_len <= row_pos)[None]

    def scored(head, tile, first_spot, count, seen):
        at = pl.ds(pl.multiple_of(first_spot * block_len, block_len), count * block_len)
        scores = lax.dot_general(
            turned_ref[head, tile],
            key_ref[head, at, :],
            (((1,), (1,)), ((), ())),
            preferred_element_type=jnp.float32,
        )
        return at, [
            jnp.where(
                seen[spot],
                scores[:, spot * block_len : (spot + 1) * block_len].reshape(
                    group, tile_rows, block_len
                ),
                2 * low,
            ).reshape(lanes_rows, block_len)
            for spot in range(count)
        ]

    def weighed(head, at, parts):
        return functools.reduce(jnp.add, parts), jnp.dot(
            jnp.concatenate([part.astype(jnp.bfloat16) for part in parts], axis=1),
            value_ref[head, at, :],
            preferred_element_type=jnp.float32,
        )

    def write(head, tile, total, acc):
        sum_out[head, tile] = total
        acc_out[head, tile] = acc

    def finish(head, tile, total, acc):
        result = (acc / jnp.sum(total, axis=1, keepdims=True)).astype(jnp.bfloat16)
        row_at = pl.ds(pl.multiple_of(tile * tile_rows, tile_rows), tile_rows)
        for member in range(group):
            column = (head * group + member) * dim
            out_ref[row_at, column : column + dim] = result[
                member * tile_rows : (member + 1) * tile_rows
            ]

    def quick(tile, carry):
        furthest = table_ref[3 * blocks + tile]
        visible = query_mask(tile)
        for unit in range(units):
            fresh = first and unit == 0
            ends = last and unit == units - 1
            before = (sum_in, acc_in) if unit == 0 and not first else (sum_out, acc_out)
            first_spot = unit * unit_blocks
            active = jnp.int32(0)
            for spot in range(unit_blocks):
                begins = list_ref[first_spot + spot] * block_len
                active = active + (begins <= furthest).astype(jnp.int32)
            after = finish if ends else write
            for count in range(0, unit_blocks + 1, grain):

                @pl.when((active + grain - 1) // grain == count // grain)
                def _(count=count):
                    if not count and not fresh and not ends:
                        return
                    seen = [visible(first_spot + spot) for spot in range(count)]
                    for head in range(heads):
                        total = acc = jnp.zeros((lanes_rows, dim), jnp.float32)
                        if count:
                            at, parts = scored(head, tile, first_spot, count, seen)
                            parts = [jnp.exp2(part * scale) for part in parts]
                            total, acc = weighed(head, at, parts)
                        if not fresh:
                            total = before[0][head, tile] + total
                            acc = before[1][head, tile] + acc
                        after(head, tile, total, acc)

        return carry

    def careful(tile, carry):
        furthest = table_ref[3 * blocks + tile]
        visible = query_mask(tile)

        def begin(head, ignored):
            if first:
                nothing = jnp.zeros((lanes_rows, dim), jnp.float32)
                most_out[head, tile] = nothing + low
                write(head, tile, nothing, nothing)
            else:
                total = sum_in[head, tile]
                most_out[head, tile] = jnp.where(
                    calm_in[0] < 1e38,
                    jnp.where(jnp.max(total, axis=1, keepdims=True) > 0, 0.0, low),
                    most_in[head, tile],
                )
                write(head, tile, total, acc_in[head, tile])
            return ignored

        lax.fori_loop(0, heads, begin, 0)

        def one(step, ignored):
            head = step % heads
            spot = step // heads

            @pl.when(list_ref[spot] * block_len <= furthest)
            def _():
                at, parts = scored(head, tile, spot, 1, [visible(spot)])
                was = most_out[head, tile]
                most = jnp.maximum(was, jnp.max(parts[0], axis=1, keepdims=True))
                total, acc = weighed(head, at, [jnp.exp2((parts[0] - most) * scale)])
                shrink = jnp.exp2((was - most) * scale)
                most_out[head, tile] = most
                write(
                    head,
                    tile,
                    sum_out[head, tile] * shrink + total,
                    acc_out[head, tile] * shrink + acc,
                )

            return ignored

        lax.fori_loop(0, spots * heads, one, 0)
        if last:
            for head in range(heads):
                finish(head, tile, sum_out[head, tile], acc_out[head, tile])
        return carry

    @pl.when(calm > 0.5)
    def _():
        lax.fori_loop(0, tiles, quick, 0)

    @pl.when(calm < 0.5)
    def _():
        lax.fori_loop(0, tiles, careful, 0)


def on_device(count, store_kv, block_owner, block_slot, span_len, row_index, fresh_q, fresh_kv):
    stored, block_len, heads, pair_width = store_kv.shape
    dim = pair_width // 2
    blocks = block_slot.shape[1]
    rows = row_index.shape[1]
    group = fresh_q.shape[2] // (heads * dim)
    tiles = rows // tile_rows
    lanes_rows = tile_rows * group
    raw_rows = block_len * 2 * heads

    def flat(array):
        lead = math.prod(array.shape[:-2])
        split = array.reshape(lead, heads, 2, dim)
        return split.transpose(0, 2, 1, 3).reshape(lead * 2 * heads, dim)

    store = flat(store_kv)
    place = lax.axis_index("req").reshape(1)
    row_pos = row_index[0]
    row_cos, row_sin = tables(row_pos.astype(jnp.float32), dim)
    starts = block_len * jnp.arange(blocks, dtype=jnp.float32)
    cos, sin = tables(starts, dim)
    row_lanes = jnp.broadcast_to(row_pos[:, None], (rows, block_len))
    wide = heads * 2 * dim + dim
    turned, placed, close, table, peak = pl.pallas_call(
        prepare,
        out_shape=(
            pltpu.VMEM((heads, tiles, lanes_rows, dim), jnp.bfloat16),
            pltpu.VMEM((blocks * block_len, wide), jnp.bfloat16),
            pltpu.VMEM(store.shape, jnp.bfloat16),
            pltpu.SMEM((3 * blocks + tiles + 1,), jnp.int32),
            pltpu.SMEM((1,), jnp.float32),
        ),
        in_specs=[anywhere] * 7 + [smem, vmem, vmem],
        out_specs=(vmem, vmem, vmem, smem, smem),
        scratch_shapes=[
            pltpu.VMEM((rows, heads * group * dim), jnp.bfloat16),
            pltpu.VMEM((rows * 2 * heads, dim), jnp.bfloat16),
            pltpu.VMEM((rows * 2 * heads, dim), jnp.float32),
            pltpu.VMEM((rows, wide), jnp.bfloat16),
            pltpu.VMEM((1, rows), jnp.int32),
            pltpu.SMEM((1, rows), jnp.int32),
            pltpu.SMEM((1, blocks), jnp.int32),
            pltpu.SMEM((1, blocks), jnp.int32),
            pltpu.SMEM(span_len.shape, jnp.int32),
            pltpu.SemaphoreType.DMA((tiles + 7,)),
        ],
        compiler_params=params,
        name="prepare",
    )(
        away(fresh_q[0]), away(flat(fresh_kv)), away(store), away(block_owner[:, :, 0]),
        away(block_slot), away(span_len), away(row_index), place, near(row_cos), near(row_sin),
    )

    def attention(number, last, sources, pick, shards, units, state):
        first = len(state) == 1
        state_shape = pltpu.VMEM((heads, tiles, lanes_rows, dim), jnp.float32)
        inputs = [near(source) for source in sources]
        inputs += [held(table), held(state[-1])]
        inputs += [near(array) for array in (turned, placed, cos, sin, row_lanes)]
        specs = [vmem] * len(sources) + [smem] * 2 + [vmem] * 5
        spots = units * unit_blocks
        result = [jax.ShapeDtypeStruct((rows, heads * group * dim), jnp.bfloat16)] if last else []
        return pl.pallas_call(
            functools.partial(attend, shards, pick, units, first, last),
            out_shape=[state_shape] * 3 + [pltpu.SMEM((1,), jnp.float32)] + result,
            in_specs=specs + [vmem] * (len(state) - 1),
            out_specs=[vmem] * 3 + [smem] + [vmem] * len(result),
            input_output_aliases={}
            if first
            else {len(specs) + entry: entry for entry in range(3)},
            scratch_shapes=[
                pltpu.VMEM((chunk, raw_rows, dim), jnp.float32),
                pltpu.VMEM((heads, spots * block_len, dim), jnp.bfloat16),
                pltpu.VMEM((heads, spots * block_len, dim), jnp.bfloat16),
                pltpu.SMEM((blocks + 1,), jnp.int32),
            ],
            compiler_params=params,
            name=f"attend_{number}",
        )(*inputs, *[near(entry) for entry in state[:-1]])

    if count != 4:
        everything = lax.all_gather(store, "req", axis=0, tiled=True)
        return attention(
            0, True, [everything], [lambda at: 0], count, blocks // unit_blocks, (peak,)
        )[-1][None]
    outer = [(0, 1), (1, 0), (2, 3), (3, 2)]
    inner = [(1, 2), (2, 1)]
    outward = [(1, 0), (2, 3)]
    none = -(1 << 16)
    is_end = lambda at: (at == 0) | (at == 3)

    def send(array, pairs):
        return lax.ppermute(array, "req", pairs)

    beside = send(store, outer)
    across = send(store, inner)
    store, close, turned = lax.optimization_barrier((store, close, turned))
    third_in = send(store, [(0, 2), (3, 1)])
    beside, starts = lax.optimization_barrier((beside, starts))
    cos, sin = tables(starts, dim)
    across, close, turned, cos, sin = lax.optimization_barrier((across, close, turned, cos, sin))
    second = send(across, outward)
    state = attention(0, False, [close, beside], [lambda at: at, lambda at: at ^ 1], 1, 2, (peak,))
    second, third_in, state = lax.optimization_barrier((second, third_in, state))
    third = send(third_in, outward)
    state = attention(
        1,
        False,
        [second, across],
        [
            lambda at: jnp.where(is_end(at), jnp.where(at == 0, 2, 1), none),
            lambda at: jnp.where(is_end(at), none, 3 - at),
        ],
        1,
        1,
        state,
    )
    third, state = lax.optimization_barrier((third, state))
    return attention(
        2,
        True,
        [third, third_in],
        [
            lambda at: jnp.where(is_end(at), 3 - at, none),
            lambda at: jnp.where(is_end(at), none, (3 - at) ^ 1),
        ],
        1,
        1,
        state,
    )[-1][None]


def solution(mesh):
    placed = (
        P(("grp", "req"), None, "kvh", None),
        P(("grp", "req"), None, None),
        P(("grp", "req"), None),
        P(("grp", "req"), None),
        P(("grp", "req"), None),
        P(("grp", "req"), None, "kvh"),
        P(("grp", "req"), None, "kvh", None),
    )
    return jax.shard_map(
        functools.partial(on_device, mesh.shape["req"]),
        mesh=mesh,
        in_specs=placed,
        out_specs=P(("grp", "req"), None, "kvh"),
        check_vma=False,
    )
```

```python
import functools
import math

import jax
import jax.numpy as jnp
from jax import lax
from jax.experimental import pallas as pl
from jax.experimental.pallas import tpu as pltpu
from jax.sharding import PartitionSpec as P

rope_base = 500000.0
tile_rows = 64
unit_blocks = 6
low = -1e30
bound = 105.0
grain = 1
chunk = 6
vmem = pl.BlockSpec(memory_space=pltpu.VMEM)
smem = pl.BlockSpec(memory_space=pltpu.SMEM)
anywhere = pl.BlockSpec(memory_space=pl.ANY)
params = pltpu.CompilerParams(vmem_limit_bytes=28 << 20)


def near(array):
    return pltpu.with_memory_space_constraint(array, pltpu.VMEM)


def held(array):
    return pltpu.with_memory_space_constraint(array, pltpu.SMEM)


def away(array):
    return pltpu.with_memory_space_constraint(array, pltpu.HBM)


def tables(position, head_dim):
    lane = lax.broadcasted_iota(jnp.int32, (position.shape[0], head_dim), 1)
    half_dim = head_dim // 2
    pair_index = (lane % half_dim).astype(jnp.float32)
    inv_freq = jnp.exp(pair_index * (-2.0 / head_dim) * jnp.log(jnp.float32(rope_base)))
    angles = position[:, None] * inv_freq
    sine = jnp.sin(angles)
    return jnp.cos(angles), jnp.where(lane < half_dim, -sine, sine)


def turn(field, cosine, sine):
    return field * cosine + pltpu.roll(field, field.shape[1] // 2, 1) * sine


def prepare(
    query_ref, fresh_ref, store_ref, owner_ref, slot_ref, span_ref, pos_ref, place_ref, cos_ref, sin_ref,
    turned_ref, placed_ref, near_ref, table_ref, peak_ref,
    raw_ref, flat_ref, wide_ref, all_ref, lanes_ref, row_smem, owner_smem, slot_smem, span_smem, sems,
):
    heads, tiles, lanes_rows, dim = turned_ref.shape
    group = lanes_rows // tile_rows
    placed_rows = placed_ref.shape[0]
    rows = cos_ref.shape[0]
    blocks = slot_ref.shape[1]

    def load_query(tile):
        at = pl.ds(pl.multiple_of(tile * tile_rows, tile_rows), tile_rows)
        return pltpu.make_async_copy(query_ref.at[at, :], raw_ref.at[at, :], sems.at[tile])

    small = [
        pltpu.make_async_copy(source, target, sems.at[tiles + number])
        for number, (source, target) in enumerate(
            (
                (pos_ref, lanes_ref),
                (fresh_ref, flat_ref),
                (pos_ref, row_smem),
                (owner_ref, owner_smem),
                (slot_ref, slot_smem),
                (span_ref, span_smem),
                (store_ref, near_ref),
            )
        )
    ]
    for copy in small[:-1]:
        copy.start()
    for tile in range(tiles):
        load_query(tile).start()
    small[-1].start()
    for copy in small[:-1]:
        copy.wait()
    wide_ref[...] = flat_ref[...].astype(jnp.float32)
    for head in range(heads):
        key = wide_ref[pl.ds(head, rows, stride=2 * heads), :]
        value = wide_ref[pl.ds(heads + head, rows, stride=2 * heads), :]
        all_ref[:, head * 2 * dim : head * 2 * dim + dim] = turn(
            key, cos_ref[...], sin_ref[...]
        ).astype(jnp.bfloat16)
        all_ref[:, head * 2 * dim + dim : (head + 1) * 2 * dim] = value.astype(jnp.bfloat16)
    all_ref[:, heads * 2 * dim :] = jnp.ones((rows, dim), jnp.bfloat16)
    step = 512

    def place(number, carry):
        at = pl.ds(pl.multiple_of(number * step, step), step)
        spot = lax.broadcasted_iota(jnp.int32, (step, rows), 0) + number * step
        chosen = jnp.where(spot == lanes_ref[...], 1.0, 0.0).astype(jnp.bfloat16)
        placed_ref[at, :] = jnp.dot(
            chosen, all_ref[...], preferred_element_type=jnp.float32
        ).astype(jnp.bfloat16)
        return carry

    lax.fori_loop(0, placed_rows // step, place, 0)

    def note(block, carry):
        began = jnp.int32(0)
        start = jnp.int32(0)
        for span in range(span_ref.shape[1]):
            began = jnp.where(start <= block, start, began)
            start = start + span_smem[0, span]
        table_ref[block] = owner_smem[0, block]
        table_ref[blocks + block] = slot_smem[0, block]
        table_ref[2 * blocks + block] = began
        return carry

    lax.fori_loop(0, blocks, note, 0)
    for tile in range(tiles):
        table_ref[3 * blocks + tile] = row_smem[0, (tile + 1) * tile_rows - 1]
    table_ref[3 * blocks + tiles] = place_ref[0]
    ones = jnp.ones((dim, dim), jnp.bfloat16)

    def turn_tile(tile, peak):
        load_query(tile).wait()
        at = pl.ds(pl.multiple_of(tile * tile_rows, tile_rows), tile_rows)
        cosine = cos_ref[at, :]
        sine = sin_ref[at, :]
        for head in range(heads):
            squares = []
            for member in range(group):
                column = (head * group + member) * dim
                field = raw_ref[at, column : column + dim].astype(jnp.float32)
                turned_ref[head, tile, member * tile_rows : (member + 1) * tile_rows, :] = turn(
                    field, cosine, sine
                ).astype(jnp.bfloat16)
                squares.append((field * field).astype(jnp.bfloat16))
            lengths = jnp.dot(
                jnp.concatenate(squares, axis=0), ones, preferred_element_type=jnp.float32
            )
            peak = jnp.maximum(peak, jnp.max(lengths.reshape(-1, 8, dim), axis=0))
        return peak

    peak = lax.fori_loop(0, tiles, turn_tile, jnp.zeros((8, dim), jnp.float32))
    peak_ref[0] = jnp.max(peak)
    small[-1].wait()


def attend(shards, pick, units, first, last, *refs):
    given = len(pick)
    sources = refs[:given]
    table_ref, calm_in, turned_ref, placed_ref, cos_ref, sin_ref, row_ref = refs[given : given + 7]
    refs = refs[given + 7 :]
    if not first:
        most_in, sum_in, acc_in = refs[:3]
        refs = refs[3:]
    most_out, sum_out, acc_out, calm_out = refs[:4]
    refs = refs[4:]
    if last:
        out_ref = refs[0]
        refs = refs[1:]
    wide_ref, key_ref, value_ref, list_ref = refs
    heads, tiles, lanes_rows, dim = turned_ref.shape
    group = lanes_rows // tile_rows
    blocks = cos_ref.shape[0]
    block_len = placed_ref.shape[0] // blocks
    stride = 2 * heads
    raw_rows = block_len * stride
    slots = sources[0].shape[0] // raw_rows // shards
    scale = dim**-0.5 * math.log2(math.e)
    lowest = [choose(table_ref[3 * blocks + tiles]) for choose in pick]
    spots = units * unit_blocks

    def find(block, found):
        owner = table_ref[block]
        hit = jnp.bool_(False)
        for base in lowest:
            hit = hit | ((owner >= base) & (owner < base + shards))
        list_ref[found] = block
        return found + hit.astype(jnp.int32)

    lax.fori_loop(0, blocks, find, jnp.int32(0))
    ones = jnp.ones((dim, dim), jnp.bfloat16)

    def load(turn_number, peak):
        for lane in range(chunk):
            spot = turn_number * chunk + lane
            block = list_ref[spot]
            owner = table_ref[block]
            raw = None
            for source, base in zip(sources, lowest):
                here = (owner >= base) & (owner < base + shards)
                start = ((owner - base) * slots + table_ref[blocks + block]) * raw_rows
                start = pl.multiple_of(jnp.where(here, start, 0), raw_rows)
                found = source[pl.ds(start, raw_rows), :].astype(jnp.float32)
                raw = found if raw is None else jnp.where(here, found, raw)
            wide_ref[lane] = raw
            began = table_ref[2 * blocks + block]
            cosine = cos_ref[pl.ds(began, 1), :]
            sine = sin_ref[pl.ds(began, 1), :]
            fresh = placed_ref[
                pl.ds(pl.multiple_of(block * block_len, block_len), block_len), :
            ].astype(jnp.float32)
            renewed = fresh[:, heads * 2 * dim :] > 0.5
            at = pl.ds(pl.multiple_of(spot * block_len, block_len), block_len)
            for head in range(heads):
                key = turn(wide_ref[lane, pl.ds(head, block_len, stride=stride), :], cosine, sine)
                value = wide_ref[lane, pl.ds(heads + head, block_len, stride=stride), :]
                begin = head * 2 * dim
                key = jnp.where(renewed, fresh[:, begin : begin + dim], key)
                key_ref[head, at, :] = key.astype(jnp.bfloat16)
                value_ref[head, at, :] = jnp.where(
                    renewed, fresh[:, begin + dim : begin + 2 * dim], value
                ).astype(jnp.bfloat16)
                lengths = jnp.dot(
                    (key * key).astype(jnp.bfloat16), ones, preferred_element_type=jnp.float32
                )
                peak = jnp.maximum(peak, jnp.max(lengths.reshape(-1, 8, dim), axis=0))
        return peak

    peak = lax.fori_loop(0, spots // chunk, load, jnp.zeros((8, dim), jnp.float32))
    room = (calm_in[0] < 1e38) & (calm_in[0] * jnp.max(peak) <= (bound / scale) ** 2)
    calm = room.astype(jnp.float32)
    calm_out[0] = jnp.where(room, calm_in[0], jnp.float32(3e38))

    def query_mask(tile):
        row_at = pl.ds(pl.multiple_of(tile * tile_rows, tile_rows), tile_rows)
        row_pos = row_ref[row_at, :]
        lane = lax.broadcasted_iota(jnp.int32, (tile_rows, block_len), 1)
        return lambda spot: (lane + list_ref[spot] * block_len <= row_pos)[None]

    def scored(head, tile, first_spot, count, seen):
        at = pl.ds(pl.multiple_of(first_spot * block_len, block_len), count * block_len)
        scores = lax.dot_general(
            turned_ref[head, tile],
            key_ref[head, at, :],
            (((1,), (1,)), ((), ())),
            preferred_element_type=jnp.float32,
        )
        return at, [
            jnp.where(
                seen[spot],
                scores[:, spot * block_len : (spot + 1) * block_len].reshape(
                    group, tile_rows, block_len
                ),
                2 * low,
            ).reshape(lanes_rows, block_len)
            for spot in range(count)
        ]

    def weighed(head, at, parts):
        return functools.reduce(jnp.add, parts), jnp.dot(
            jnp.concatenate([part.astype(jnp.bfloat16) for part in parts], axis=1),
            value_ref[head, at, :],
            preferred_element_type=jnp.float32,
        )

    def write(head, tile, total, acc):
        sum_out[head, tile] = total
        acc_out[head, tile] = acc

    def finish(head, tile, total, acc):
        result = (acc / jnp.sum(total, axis=1, keepdims=True)).astype(jnp.bfloat16)
        row_at = pl.ds(pl.multiple_of(tile * tile_rows, tile_rows), tile_rows)
        for member in range(group):
            column = (head * group + member) * dim
            out_ref[row_at, column : column + dim] = result[
                member * tile_rows : (member + 1) * tile_rows
            ]

    def quick(tile, carry):
        furthest = table_ref[3 * blocks + tile]
        visible = query_mask(tile)
        for unit in range(units):
            fresh = first and unit == 0
            ends = last and unit == units - 1
            before = (sum_in, acc_in) if unit == 0 and not first else (sum_out, acc_out)
            first_spot = unit * unit_blocks
            active = jnp.int32(0)
            for spot in range(unit_blocks):
                begins = list_ref[first_spot + spot] * block_len
                active = active + (begins <= furthest).astype(jnp.int32)
            after = finish if ends else write
            for count in range(0, unit_blocks + 1, grain):

                @pl.when((active + grain - 1) // grain == count // grain)
                def _(count=count):
                    if not count and not fresh and not ends:
                        return
                    seen = [visible(first_spot + spot) for spot in range(count)]
                    for head in range(heads):
                        total = acc = jnp.zeros((lanes_rows, dim), jnp.float32)
                        if count:
                            at, parts = scored(head, tile, first_spot, count, seen)
                            parts = [jnp.exp2(part * scale) for part in parts]
                            total, acc = weighed(head, at, parts)
                        if not fresh:
                            total = before[0][head, tile] + total
                            acc = before[1][head, tile] + acc
                        after(head, tile, total, acc)

        return carry

    def careful(tile, carry):
        furthest = table_ref[3 * blocks + tile]
        visible = query_mask(tile)

        def begin(head, ignored):
            if first:
                nothing = jnp.zeros((lanes_rows, dim), jnp.float32)
                most_out[head, tile] = nothing + low
                write(head, tile, nothing, nothing)
            else:
                total = sum_in[head, tile]
                most_out[head, tile] = jnp.where(
                    calm_in[0] < 1e38,
                    jnp.where(jnp.max(total, axis=1, keepdims=True) > 0, 0.0, low),
                    most_in[head, tile],
                )
                write(head, tile, total, acc_in[head, tile])
            return ignored

        lax.fori_loop(0, heads, begin, 0)

        def one(step, ignored):
            head = step % heads
            spot = step // heads

            @pl.when(list_ref[spot] * block_len <= furthest)
            def _():
                at, parts = scored(head, tile, spot, 1, [visible(spot)])
                was = most_out[head, tile]
                most = jnp.maximum(was, jnp.max(parts[0], axis=1, keepdims=True))
                total, acc = weighed(head, at, [jnp.exp2((parts[0] - most) * scale)])
                shrink = jnp.exp2((was - most) * scale)
                most_out[head, tile] = most
                write(
                    head,
                    tile,
                    sum_out[head, tile] * shrink + total,
                    acc_out[head, tile] * shrink + acc,
                )

            return ignored

        lax.fori_loop(0, spots * heads, one, 0)
        if last:
            for head in range(heads):
                finish(head, tile, sum_out[head, tile], acc_out[head, tile])
        return carry

    @pl.when(calm > 0.5)
    def _():
        lax.fori_loop(0, tiles, quick, 0)

    @pl.when(calm < 0.5)
    def _():
        lax.fori_loop(0, tiles, careful, 0)


def on_device(count, store_kv, block_owner, block_slot, span_len, row_index, fresh_q, fresh_kv):
    stored, block_len, heads, pair_width = store_kv.shape
    dim = pair_width // 2
    blocks = block_slot.shape[1]
    rows = row_index.shape[1]
    group = fresh_q.shape[2] // (heads * dim)
    tiles = rows // tile_rows
    lanes_rows = tile_rows * group
    raw_rows = block_len * 2 * heads

    def flat(array):
        lead = math.prod(array.shape[:-2])
        split = array.reshape(lead, heads, 2, dim)
        return split.transpose(0, 2, 1, 3).reshape(lead * 2 * heads, dim)

    store = flat(store_kv)
    place = lax.axis_index("req").reshape(1)
    row_pos = row_index[0]
    row_cos, row_sin = tables(row_pos.astype(jnp.float32), dim)
    cos, sin = tables(block_len * jnp.arange(blocks, dtype=jnp.float32), dim)
    row_lanes = jnp.broadcast_to(row_pos[:, None], (rows, block_len))
    wide = heads * 2 * dim + dim
    turned, placed, close, table, peak = pl.pallas_call(
        prepare,
        out_shape=(
            pltpu.VMEM((heads, tiles, lanes_rows, dim), jnp.bfloat16),
            pltpu.VMEM((blocks * block_len, wide), jnp.bfloat16),
            pltpu.VMEM(store.shape, jnp.bfloat16),
            pltpu.SMEM((3 * blocks + tiles + 1,), jnp.int32),
            pltpu.SMEM((1,), jnp.float32),
        ),
        in_specs=[anywhere] * 7 + [smem, vmem, vmem],
        out_specs=(vmem, vmem, vmem, smem, smem),
        scratch_shapes=[
            pltpu.VMEM((rows, heads * group * dim), jnp.bfloat16),
            pltpu.VMEM((rows * 2 * heads, dim), jnp.bfloat16),
            pltpu.VMEM((rows * 2 * heads, dim), jnp.float32),
            pltpu.VMEM((rows, wide), jnp.bfloat16),
            pltpu.VMEM((1, rows), jnp.int32),
            pltpu.SMEM((1, rows), jnp.int32),
            pltpu.SMEM((1, blocks), jnp.int32),
            pltpu.SMEM((1, blocks), jnp.int32),
            pltpu.SMEM(span_len.shape, jnp.int32),
            pltpu.SemaphoreType.DMA((tiles + 7,)),
        ],
        compiler_params=params,
        name="prepare",
    )(
        away(fresh_q[0]), away(flat(fresh_kv)), away(store), away(block_owner[:, :, 0]),
        away(block_slot), away(span_len), away(row_index), place, near(row_cos), near(row_sin),
    )

    def attention(number, last, sources, pick, shards, units, state):
        first = len(state) == 1
        state_shape = pltpu.VMEM((heads, tiles, lanes_rows, dim), jnp.float32)
        inputs = [near(source) for source in sources]
        inputs += [held(table), held(state[-1])]
        inputs += [near(array) for array in (turned, placed, cos, sin, row_lanes)]
        specs = [vmem] * len(sources) + [smem] * 2 + [vmem] * 5
        spots = units * unit_blocks
        result = [jax.ShapeDtypeStruct((rows, heads * group * dim), jnp.bfloat16)] if last else []
        return pl.pallas_call(
            functools.partial(attend, shards, pick, units, first, last),
            out_shape=[state_shape] * 3 + [pltpu.SMEM((1,), jnp.float32)] + result,
            in_specs=specs + [vmem] * (len(state) - 1),
            out_specs=[vmem] * 3 + [smem] + [vmem] * len(result),
            input_output_aliases={}
            if first
            else {len(specs) + entry: entry for entry in range(3)},
            scratch_shapes=[
                pltpu.VMEM((chunk, raw_rows, dim), jnp.float32),
                pltpu.VMEM((heads, spots * block_len, dim), jnp.bfloat16),
                pltpu.VMEM((heads, spots * block_len, dim), jnp.bfloat16),
                pltpu.SMEM((blocks + 1,), jnp.int32),
            ],
            compiler_params=params,
            name=f"attend_{number}",
        )(*inputs, *[near(entry) for entry in state[:-1]])

    if count != 4:
        everything = lax.all_gather(store, "req", axis=0, tiled=True)
        return attention(
            0, True, [everything], [lambda at: 0], count, blocks // unit_blocks, (peak,)
        )[-1][None]
    outer = [(0, 1), (1, 0), (2, 3), (3, 2)]
    inner = [(1, 2), (2, 1)]
    outward = [(1, 0), (2, 3)]
    none = -(1 << 16)
    is_end = lambda at: (at == 0) | (at == 3)

    def send(array, pairs):
        return lax.ppermute(array, "req", pairs)

    beside = send(store, outer)
    across = send(store, inner)
    store, close, turned = lax.optimization_barrier((store, close, turned))
    third_in = send(store, [(0, 2), (3, 1)])
    across, close, turned = lax.optimization_barrier((across, close, turned))
    second = send(across, outward)
    state = attention(0, False, [close, beside], [lambda at: at, lambda at: at ^ 1], 1, 2, (peak,))
    second, third_in, state = lax.optimization_barrier((second, third_in, state))
    third = send(third_in, outward)
    state = attention(
        1,
        False,
        [second, across],
        [
            lambda at: jnp.where(is_end(at), jnp.where(at == 0, 2, 1), none),
            lambda at: jnp.where(is_end(at), none, 3 - at),
        ],
        1,
        1,
        state,
    )
    third, state = lax.optimization_barrier((third, state))
    return attention(
        2,
        True,
        [third, third_in],
        [
            lambda at: jnp.where(is_end(at), 3 - at, none),
            lambda at: jnp.where(is_end(at), none, (3 - at) ^ 1),
        ],
        1,
        1,
        state,
    )[-1][None]


def solution(mesh):
    placed = (
        P(("grp", "req"), None, "kvh", None),
        P(("grp", "req"), None, None),
        P(("grp", "req"), None),
        P(("grp", "req"), None),
        P(("grp", "req"), None),
        P(("grp", "req"), None, "kvh"),
        P(("grp", "req"), None, "kvh", None),
    )
    return jax.shard_map(
        functools.partial(on_device, mesh.shape["req"]),
        mesh=mesh,
        in_specs=placed,
        out_specs=P(("grp", "req"), None, "kvh"),
        check_vma=False,
    )
```

```python
import functools
import math

import jax
import jax.numpy as jnp
from jax import lax
from jax.experimental import pallas as pl
from jax.experimental.pallas import tpu as pltpu
from jax.sharding import PartitionSpec as P

rope_base = 500000.0
tile_rows = 64
unit_blocks = 6
low = -1e30
bound = 105.0
grain = 1
chunk = 6
vmem = pl.BlockSpec(memory_space=pltpu.VMEM)
smem = pl.BlockSpec(memory_space=pltpu.SMEM)
anywhere = pl.BlockSpec(memory_space=pl.ANY)
params = pltpu.CompilerParams(vmem_limit_bytes=28 << 20)


def near(array):
    return pltpu.with_memory_space_constraint(array, pltpu.VMEM)


def held(array):
    return pltpu.with_memory_space_constraint(array, pltpu.SMEM)


def away(array):
    return pltpu.with_memory_space_constraint(array, pltpu.HBM)


def tables(position, head_dim):
    lane = lax.broadcasted_iota(jnp.int32, (position.shape[0], head_dim), 1)
    half_dim = head_dim // 2
    pair_index = (lane % half_dim).astype(jnp.float32)
    inv_freq = jnp.exp(pair_index * (-2.0 / head_dim) * jnp.log(jnp.float32(rope_base)))
    angles = position[:, None] * inv_freq
    sine = jnp.sin(angles)
    return jnp.cos(angles), jnp.where(lane < half_dim, -sine, sine)


def turn(field, cosine, sine):
    return field * cosine + pltpu.roll(field, field.shape[1] // 2, 1) * sine


def prepare(
    query_ref, fresh_ref, store_ref, owner_ref, slot_ref, span_ref, pos_ref, place_ref, cos_ref, sin_ref,
    turned_ref, placed_ref, near_ref, table_ref, peak_ref,
    raw_ref, flat_ref, wide_ref, all_ref, lanes_ref, row_smem, owner_smem, slot_smem, span_smem, sems,
):
    heads, tiles, lanes_rows, dim = turned_ref.shape
    group = lanes_rows // tile_rows
    placed_rows = placed_ref.shape[0]
    rows = cos_ref.shape[0]
    blocks = slot_ref.shape[1]

    def load_query(tile):
        at = pl.ds(pl.multiple_of(tile * tile_rows, tile_rows), tile_rows)
        return pltpu.make_async_copy(query_ref.at[at, :], raw_ref.at[at, :], sems.at[tile])

    small = [
        pltpu.make_async_copy(source, target, sems.at[tiles + number])
        for number, (source, target) in enumerate(
            (
                (pos_ref, lanes_ref),
                (fresh_ref, flat_ref),
                (pos_ref, row_smem),
                (owner_ref, owner_smem),
                (slot_ref, slot_smem),
                (span_ref, span_smem),
                (store_ref, near_ref),
            )
        )
    ]
    for copy in small[:-1]:
        copy.start()
    for tile in range(tiles):
        load_query(tile).start()
    small[-1].start()
    for copy in small[:-1]:
        copy.wait()
    wide_ref[...] = flat_ref[...].astype(jnp.float32)
    for head in range(heads):
        key = wide_ref[pl.ds(head, rows, stride=2 * heads), :]
        value = wide_ref[pl.ds(heads + head, rows, stride=2 * heads), :]
        all_ref[:, head * 2 * dim : head * 2 * dim + dim] = turn(
            key, cos_ref[...], sin_ref[...]
        ).astype(jnp.bfloat16)
        all_ref[:, head * 2 * dim + dim : (head + 1) * 2 * dim] = value.astype(jnp.bfloat16)
    all_ref[:, heads * 2 * dim :] = jnp.ones((rows, dim), jnp.bfloat16)
    step = 512

    def place(number, carry):
        at = pl.ds(pl.multiple_of(number * step, step), step)
        spot = lax.broadcasted_iota(jnp.int32, (step, rows), 0) + number * step
        chosen = jnp.where(spot == lanes_ref[...], 1.0, 0.0).astype(jnp.bfloat16)
        placed_ref[at, :] = jnp.dot(
            chosen, all_ref[...], preferred_element_type=jnp.float32
        ).astype(jnp.bfloat16)
        return carry

    lax.fori_loop(0, placed_rows // step, place, 0)

    def note(block, carry):
        began = jnp.int32(0)
        start = jnp.int32(0)
        for span in range(span_ref.shape[1]):
            began = jnp.where(start <= block, start, began)
            start = start + span_smem[0, span]
        table_ref[block] = owner_smem[0, block]
        table_ref[blocks + block] = slot_smem[0, block]
        table_ref[2 * blocks + block] = began
        return carry

    lax.fori_loop(0, blocks, note, 0)
    for tile in range(tiles):
        table_ref[3 * blocks + tile] = row_smem[0, (tile + 1) * tile_rows - 1]
    table_ref[3 * blocks + tiles] = place_ref[0]
    ones = jnp.ones((dim, dim), jnp.bfloat16)

    def turn_tile(tile, peak):
        load_query(tile).wait()
        at = pl.ds(pl.multiple_of(tile * tile_rows, tile_rows), tile_rows)
        cosine = cos_ref[at, :]
        sine = sin_ref[at, :]
        for head in range(heads):
            squares = []
            for member in range(group):
                column = (head * group + member) * dim
                field = raw_ref[at, column : column + dim].astype(jnp.float32)
                turned_ref[head, tile, member * tile_rows : (member + 1) * tile_rows, :] = turn(
                    field, cosine, sine
                ).astype(jnp.bfloat16)
                squares.append((field * field).astype(jnp.bfloat16))
            lengths = jnp.dot(
                jnp.concatenate(squares, axis=0), ones, preferred_element_type=jnp.float32
            )
            peak = jnp.maximum(peak, jnp.max(lengths.reshape(-1, 8, dim), axis=0))
        return peak

    peak = lax.fori_loop(0, tiles, turn_tile, jnp.zeros((8, dim), jnp.float32))
    peak_ref[0] = jnp.max(peak)
    small[-1].wait()


def attend(shards, pick, units, first, last, *refs):
    given = len(pick)
    sources = refs[:given]
    table_ref, calm_in, turned_ref, placed_ref, cos_ref, sin_ref, row_ref = refs[given : given + 7]
    refs = refs[given + 7 :]
    if not first:
        most_in, sum_in, acc_in = refs[:3]
        refs = refs[3:]
    most_out, sum_out, acc_out, calm_out = refs[:4]
    refs = refs[4:]
    if last:
        whole_ref = refs[0]
        out_ref, out_sems = refs[-2:]
        refs = refs[1:-2]
    wide_ref, key_ref, value_ref, list_ref = refs
    heads, tiles, lanes_rows, dim = turned_ref.shape
    group = lanes_rows // tile_rows
    blocks = cos_ref.shape[0]
    block_len = placed_ref.shape[0] // blocks
    stride = 2 * heads
    raw_rows = block_len * stride
    slots = sources[0].shape[0] // raw_rows // shards
    scale = dim**-0.5 * math.log2(math.e)
    lowest = [choose(table_ref[3 * blocks + tiles]) for choose in pick]
    spots = units * unit_blocks

    def find(block, found):
        owner = table_ref[block]
        hit = jnp.bool_(False)
        for base in lowest:
            hit = hit | ((owner >= base) & (owner < base + shards))
        list_ref[found] = block
        return found + hit.astype(jnp.int32)

    lax.fori_loop(0, blocks, find, jnp.int32(0))
    ones = jnp.ones((dim, dim), jnp.bfloat16)

    def load(turn_number, peak):
        for lane in range(chunk):
            spot = turn_number * chunk + lane
            block = list_ref[spot]
            owner = table_ref[block]
            raw = None
            for source, base in zip(sources, lowest):
                here = (owner >= base) & (owner < base + shards)
                start = ((owner - base) * slots + table_ref[blocks + block]) * raw_rows
                start = pl.multiple_of(jnp.where(here, start, 0), raw_rows)
                found = source[pl.ds(start, raw_rows), :].astype(jnp.float32)
                raw = found if raw is None else jnp.where(here, found, raw)
            wide_ref[lane] = raw
            began = table_ref[2 * blocks + block]
            cosine = cos_ref[pl.ds(began, 1), :]
            sine = sin_ref[pl.ds(began, 1), :]
            fresh = placed_ref[
                pl.ds(pl.multiple_of(block * block_len, block_len), block_len), :
            ].astype(jnp.float32)
            renewed = fresh[:, heads * 2 * dim :] > 0.5
            at = pl.ds(pl.multiple_of(spot * block_len, block_len), block_len)
            for head in range(heads):
                key = turn(wide_ref[lane, pl.ds(head, block_len, stride=stride), :], cosine, sine)
                value = wide_ref[lane, pl.ds(heads + head, block_len, stride=stride), :]
                begin = head * 2 * dim
                key = jnp.where(renewed, fresh[:, begin : begin + dim], key)
                key_ref[head, at, :] = key.astype(jnp.bfloat16)
                value_ref[head, at, :] = jnp.where(
                    renewed, fresh[:, begin + dim : begin + 2 * dim], value
                ).astype(jnp.bfloat16)
                lengths = jnp.dot(
                    (key * key).astype(jnp.bfloat16), ones, preferred_element_type=jnp.float32
                )
                peak = jnp.maximum(peak, jnp.max(lengths.reshape(-1, 8, dim), axis=0))
        return peak

    peak = lax.fori_loop(0, spots // chunk, load, jnp.zeros((8, dim), jnp.float32))
    room = (calm_in[0] < 1e38) & (calm_in[0] * jnp.max(peak) <= (bound / scale) ** 2)
    calm = room.astype(jnp.float32)
    calm_out[0] = jnp.where(room, calm_in[0], jnp.float32(3e38))

    def query_mask(tile):
        row_at = pl.ds(pl.multiple_of(tile * tile_rows, tile_rows), tile_rows)
        row_pos = row_ref[row_at, :]
        lane = lax.broadcasted_iota(jnp.int32, (tile_rows, block_len), 1)
        return lambda spot: (lane + list_ref[spot] * block_len <= row_pos)[None]

    def scored(head, tile, first_spot, count, seen):
        at = pl.ds(pl.multiple_of(first_spot * block_len, block_len), count * block_len)
        scores = lax.dot_general(
            turned_ref[head, tile],
            key_ref[head, at, :],
            (((1,), (1,)), ((), ())),
            preferred_element_type=jnp.float32,
        )
        return at, [
            jnp.where(
                seen[spot],
                scores[:, spot * block_len : (spot + 1) * block_len].reshape(
                    group, tile_rows, block_len
                ),
                2 * low,
            ).reshape(lanes_rows, block_len)
            for spot in range(count)
        ]

    def weighed(head, at, parts):
        return functools.reduce(jnp.add, parts), jnp.dot(
            jnp.concatenate([part.astype(jnp.bfloat16) for part in parts], axis=1),
            value_ref[head, at, :],
            preferred_element_type=jnp.float32,
        )

    def write(head, tile, total, acc):
        sum_out[head, tile] = total
        acc_out[head, tile] = acc

    def finish(head, tile, total, acc):
        result = (acc / jnp.sum(total, axis=1, keepdims=True)).astype(jnp.bfloat16)
        row_at = pl.ds(pl.multiple_of(tile * tile_rows, tile_rows), tile_rows)
        for member in range(group):
            column = (head * group + member) * dim
            out_ref[row_at, column : column + dim] = result[
                member * tile_rows : (member + 1) * tile_rows
            ]

    def leave(tile):
        row_at = pl.ds(pl.multiple_of(tile * tile_rows, tile_rows), tile_rows)
        return pltpu.make_async_copy(
            out_ref.at[row_at, :], whole_ref.at[row_at, :], out_sems.at[tile]
        )

    def quick(tile, carry):
        furthest = table_ref[3 * blocks + tile]
        visible = query_mask(tile)
        for unit in range(units):
            fresh = first and unit == 0
            ends = last and unit == units - 1
            before = (sum_in, acc_in) if unit == 0 and not first else (sum_out, acc_out)
            first_spot = unit * unit_blocks
            active = jnp.int32(0)
            for spot in range(unit_blocks):
                begins = list_ref[first_spot + spot] * block_len
                active = active + (begins <= furthest).astype(jnp.int32)
            after = finish if ends else write
            for count in range(0, unit_blocks + 1, grain):

                @pl.when((active + grain - 1) // grain == count // grain)
                def _(count=count):
                    if not count and not fresh and not ends:
                        return
                    seen = [visible(first_spot + spot) for spot in range(count)]
                    for head in range(heads):
                        total = acc = jnp.zeros((lanes_rows, dim), jnp.float32)
                        if count:
                            at, parts = scored(head, tile, first_spot, count, seen)
                            parts = [jnp.exp2(part * scale) for part in parts]
                            total, acc = weighed(head, at, parts)
                        if not fresh:
                            total = before[0][head, tile] + total
                            acc = before[1][head, tile] + acc
                        after(head, tile, total, acc)

        if last:
            leave(tile).start()
        return carry

    def careful(tile, carry):
        furthest = table_ref[3 * blocks + tile]
        visible = query_mask(tile)

        def begin(head, ignored):
            if first:
                nothing = jnp.zeros((lanes_rows, dim), jnp.float32)
                most_out[head, tile] = nothing + low
                write(head, tile, nothing, nothing)
            else:
                total = sum_in[head, tile]
                most_out[head, tile] = jnp.where(
                    calm_in[0] < 1e38,
                    jnp.where(jnp.max(total, axis=1, keepdims=True) > 0, 0.0, low),
                    most_in[head, tile],
                )
                write(head, tile, total, acc_in[head, tile])
            return ignored

        lax.fori_loop(0, heads, begin, 0)

        def one(step, ignored):
            head = step % heads
            spot = step // heads

            @pl.when(list_ref[spot] * block_len <= furthest)
            def _():
                at, parts = scored(head, tile, spot, 1, [visible(spot)])
                was = most_out[head, tile]
                most = jnp.maximum(was, jnp.max(parts[0], axis=1, keepdims=True))
                total, acc = weighed(head, at, [jnp.exp2((parts[0] - most) * scale)])
                shrink = jnp.exp2((was - most) * scale)
                most_out[head, tile] = most
                write(
                    head,
                    tile,
                    sum_out[head, tile] * shrink + total,
                    acc_out[head, tile] * shrink + acc,
                )

            return ignored

        lax.fori_loop(0, spots * heads, one, 0)
        if last:
            for head in range(heads):
                finish(head, tile, sum_out[head, tile], acc_out[head, tile])
            leave(tile).start()
        return carry

    @pl.when(calm > 0.5)
    def _():
        lax.fori_loop(0, tiles, quick, 0)

    @pl.when(calm < 0.5)
    def _():
        lax.fori_loop(0, tiles, careful, 0)

    if last:
        for tile in range(tiles):
            leave(tile).wait()


def on_device(count, store_kv, block_owner, block_slot, span_len, row_index, fresh_q, fresh_kv):
    stored, block_len, heads, pair_width = store_kv.shape
    dim = pair_width // 2
    blocks = block_slot.shape[1]
    rows = row_index.shape[1]
    group = fresh_q.shape[2] // (heads * dim)
    tiles = rows // tile_rows
    lanes_rows = tile_rows * group
    raw_rows = block_len * 2 * heads

    def flat(array):
        lead = math.prod(array.shape[:-2])
        split = array.reshape(lead, heads, 2, dim)
        return split.transpose(0, 2, 1, 3).reshape(lead * 2 * heads, dim)

    store = flat(store_kv)
    place = lax.axis_index("req").reshape(1)
    row_pos = row_index[0]
    row_cos, row_sin = tables(row_pos.astype(jnp.float32), dim)
    cos, sin = tables(block_len * jnp.arange(blocks, dtype=jnp.float32), dim)
    row_lanes = jnp.broadcast_to(row_pos[:, None], (rows, block_len))
    wide = heads * 2 * dim + dim
    turned, placed, close, table, peak = pl.pallas_call(
        prepare,
        out_shape=(
            pltpu.VMEM((heads, tiles, lanes_rows, dim), jnp.bfloat16),
            pltpu.VMEM((blocks * block_len, wide), jnp.bfloat16),
            pltpu.VMEM(store.shape, jnp.bfloat16),
            pltpu.SMEM((3 * blocks + tiles + 1,), jnp.int32),
            pltpu.SMEM((1,), jnp.float32),
        ),
        in_specs=[anywhere] * 7 + [smem, vmem, vmem],
        out_specs=(vmem, vmem, vmem, smem, smem),
        scratch_shapes=[
            pltpu.VMEM((rows, heads * group * dim), jnp.bfloat16),
            pltpu.VMEM((rows * 2 * heads, dim), jnp.bfloat16),
            pltpu.VMEM((rows * 2 * heads, dim), jnp.float32),
            pltpu.VMEM((rows, wide), jnp.bfloat16),
            pltpu.VMEM((1, rows), jnp.int32),
            pltpu.SMEM((1, rows), jnp.int32),
            pltpu.SMEM((1, blocks), jnp.int32),
            pltpu.SMEM((1, blocks), jnp.int32),
            pltpu.SMEM(span_len.shape, jnp.int32),
            pltpu.SemaphoreType.DMA((tiles + 7,)),
        ],
        compiler_params=params,
        name="prepare",
    )(
        away(fresh_q[0]), away(flat(fresh_kv)), away(store), away(block_owner[:, :, 0]),
        away(block_slot), away(span_len), away(row_index), place, near(row_cos), near(row_sin),
    )

    def attention(number, last, sources, pick, shards, units, state):
        first = len(state) == 1
        state_shape = pltpu.VMEM((heads, tiles, lanes_rows, dim), jnp.float32)
        inputs = [near(source) for source in sources]
        inputs += [held(table), held(state[-1])]
        inputs += [near(array) for array in (turned, placed, cos, sin, row_lanes)]
        specs = [vmem] * len(sources) + [smem] * 2 + [vmem] * 5
        spots = units * unit_blocks
        result = [jax.ShapeDtypeStruct((rows, heads * group * dim), jnp.bfloat16)] if last else []
        return pl.pallas_call(
            functools.partial(attend, shards, pick, units, first, last),
            out_shape=[state_shape] * 3 + [pltpu.SMEM((1,), jnp.float32)] + result,
            in_specs=specs + [vmem] * (len(state) - 1),
            out_specs=[vmem] * 3 + [smem] + [anywhere] * len(result),
            input_output_aliases={}
            if first
            else {len(specs) + entry: entry for entry in range(3)},
            scratch_shapes=[
                pltpu.VMEM((chunk, raw_rows, dim), jnp.float32),
                pltpu.VMEM((heads, spots * block_len, dim), jnp.bfloat16),
                pltpu.VMEM((heads, spots * block_len, dim), jnp.bfloat16),
                pltpu.SMEM((blocks + 1,), jnp.int32),
            ]
            + (
                [
                    pltpu.VMEM((rows, heads * group * dim), jnp.bfloat16),
                    pltpu.SemaphoreType.DMA((tiles,)),
                ]
                if last
                else []
            ),
            compiler_params=params,
            name=f"attend_{number}",
        )(*inputs, *[near(entry) for entry in state[:-1]])

    if count != 4:
        everything = lax.all_gather(store, "req", axis=0, tiled=True)
        return attention(
            0, True, [everything], [lambda at: 0], count, blocks // unit_blocks, (peak,)
        )[-1][None]
    outer = [(0, 1), (1, 0), (2, 3), (3, 2)]
    inner = [(1, 2), (2, 1)]
    outward = [(1, 0), (2, 3)]
    none = -(1 << 16)
    is_end = lambda at: (at == 0) | (at == 3)

    def send(array, pairs):
        return lax.ppermute(array, "req", pairs)

    beside = send(store, outer)
    across = send(store, inner)
    store, close, turned = lax.optimization_barrier((store, close, turned))
    third_in = send(store, [(0, 2), (3, 1)])
    across, turned = lax.optimization_barrier((across, turned))
    second = send(across, outward)
    beside, close, placed = lax.optimization_barrier((beside, close, placed))
    state = attention(0, False, [close, beside], [lambda at: at, lambda at: at ^ 1], 1, 2, (peak,))
    third_in, table, state = lax.optimization_barrier((third_in, table, state))
    third = send(third_in, outward)
    state = attention(
        1,
        False,
        [second, across],
        [
            lambda at: jnp.where(is_end(at), jnp.where(at == 0, 2, 1), none),
            lambda at: jnp.where(is_end(at), none, 3 - at),
        ],
        1,
        1,
        state,
    )
    third, state = lax.optimization_barrier((third, state))
    return attention(
        2,
        True,
        [third, third_in],
        [
            lambda at: jnp.where(is_end(at), 3 - at, none),
            lambda at: jnp.where(is_end(at), none, (3 - at) ^ 1),
        ],
        1,
        1,
        state,
    )[-1][None]


def solution(mesh):
    placed = (
        P(("grp", "req"), None, "kvh", None),
        P(("grp", "req"), None, None),
        P(("grp", "req"), None),
        P(("grp", "req"), None),
        P(("grp", "req"), None),
        P(("grp", "req"), None, "kvh"),
        P(("grp", "req"), None, "kvh", None),
    )
    return jax.shard_map(
        functools.partial(on_device, mesh.shape["req"]),
        mesh=mesh,
        in_specs=placed,
        out_specs=P(("grp", "req"), None, "kvh"),
        check_vma=False,
    )
```

```python
import functools
import math

import jax
import jax.numpy as jnp
from jax import lax
from jax.experimental import pallas as pl
from jax.experimental.pallas import tpu as pltpu
from jax.sharding import PartitionSpec as P

rope_base = 500000.0
tile_rows = 64
unit_blocks = 6
low = -1e30
bound = 105.0
grain = 1
chunk = 6
vmem = pl.BlockSpec(memory_space=pltpu.VMEM)
smem = pl.BlockSpec(memory_space=pltpu.SMEM)
anywhere = pl.BlockSpec(memory_space=pl.ANY)
params = pltpu.CompilerParams(vmem_limit_bytes=28 << 20)


def near(array):
    return pltpu.with_memory_space_constraint(array, pltpu.VMEM)


def held(array):
    return pltpu.with_memory_space_constraint(array, pltpu.SMEM)


def away(array):
    return pltpu.with_memory_space_constraint(array, pltpu.HBM)


def tables(position, head_dim):
    lane = lax.broadcasted_iota(jnp.int32, (position.shape[0], head_dim), 1)
    half_dim = head_dim // 2
    pair_index = (lane % half_dim).astype(jnp.float32)
    inv_freq = jnp.exp(pair_index * (-2.0 / head_dim) * jnp.log(jnp.float32(rope_base)))
    angles = position[:, None] * inv_freq
    sine = jnp.sin(angles)
    return jnp.cos(angles), jnp.where(lane < half_dim, -sine, sine)


def turn(field, cosine, sine):
    return field * cosine + pltpu.roll(field, field.shape[1] // 2, 1) * sine


def prepare(
    query_ref, fresh_ref, store_ref, owner_ref, slot_ref, span_ref, pos_ref, place_ref, cos_ref, sin_ref,
    turned_ref, placed_ref, near_ref, table_ref, peak_ref,
    raw_ref, flat_ref, wide_ref, all_ref, lanes_ref, row_smem, owner_smem, slot_smem, span_smem, sems,
):
    heads, tiles, lanes_rows, dim = turned_ref.shape
    group = lanes_rows // tile_rows
    placed_rows = placed_ref.shape[0]
    rows = cos_ref.shape[0]
    blocks = slot_ref.shape[1]

    def load_query(tile):
        at = pl.ds(pl.multiple_of(tile * tile_rows, tile_rows), tile_rows)
        return pltpu.make_async_copy(query_ref.at[at, :], raw_ref.at[at, :], sems.at[tile])

    small = [
        pltpu.make_async_copy(source, target, sems.at[tiles + number])
        for number, (source, target) in enumerate(
            (
                (pos_ref, lanes_ref),
                (fresh_ref, flat_ref),
                (pos_ref, row_smem),
                (owner_ref, owner_smem),
                (slot_ref, slot_smem),
                (span_ref, span_smem),
                (store_ref, near_ref),
            )
        )
    ]
    for copy in small[:-1]:
        copy.start()
    for tile in range(tiles):
        load_query(tile).start()
    small[-1].start()
    for copy in small[:-1]:
        copy.wait()
    wide_ref[...] = flat_ref[...].astype(jnp.float32)
    for head in range(heads):
        key = wide_ref[pl.ds(head, rows, stride=2 * heads), :]
        value = wide_ref[pl.ds(heads + head, rows, stride=2 * heads), :]
        all_ref[:, head * 2 * dim : head * 2 * dim + dim] = turn(
            key, cos_ref[...], sin_ref[...]
        ).astype(jnp.bfloat16)
        all_ref[:, head * 2 * dim + dim : (head + 1) * 2 * dim] = value.astype(jnp.bfloat16)
    all_ref[:, heads * 2 * dim :] = jnp.ones((rows, dim), jnp.bfloat16)
    step = 512

    def place(number, carry):
        at = pl.ds(pl.multiple_of(number * step, step), step)
        spot = lax.broadcasted_iota(jnp.int32, (step, rows), 0) + number * step
        chosen = jnp.where(spot == lanes_ref[...], 1.0, 0.0).astype(jnp.bfloat16)
        placed_ref[at, :] = jnp.dot(
            chosen, all_ref[...], preferred_element_type=jnp.float32
        ).astype(jnp.bfloat16)
        return carry

    lax.fori_loop(0, placed_rows // step, place, 0)

    def note(block, carry):
        began = jnp.int32(0)
        start = jnp.int32(0)
        for span in range(span_ref.shape[1]):
            began = jnp.where(start <= block, start, began)
            start = start + span_smem[0, span]
        table_ref[block] = owner_smem[0, block]
        table_ref[blocks + block] = slot_smem[0, block]
        table_ref[2 * blocks + block] = began
        return carry

    lax.fori_loop(0, blocks, note, 0)
    for tile in range(tiles):
        table_ref[3 * blocks + tile] = row_smem[0, (tile + 1) * tile_rows - 1]
    table_ref[3 * blocks + tiles] = place_ref[0]
    ones = jnp.ones((dim, dim), jnp.bfloat16)

    def turn_tile(tile, peak):
        load_query(tile).wait()
        at = pl.ds(pl.multiple_of(tile * tile_rows, tile_rows), tile_rows)
        cosine = cos_ref[at, :]
        sine = sin_ref[at, :]
        for head in range(heads):
            squares = []
            for member in range(group):
                column = (head * group + member) * dim
                field = raw_ref[at, column : column + dim].astype(jnp.float32)
                turned_ref[head, tile, member * tile_rows : (member + 1) * tile_rows, :] = turn(
                    field, cosine, sine
                ).astype(jnp.bfloat16)
                squares.append((field * field).astype(jnp.bfloat16))
            lengths = jnp.dot(
                jnp.concatenate(squares, axis=0), ones, preferred_element_type=jnp.float32
            )
            peak = jnp.maximum(peak, jnp.max(lengths.reshape(-1, 8, dim), axis=0))
        return peak

    peak = lax.fori_loop(0, tiles, turn_tile, jnp.zeros((8, dim), jnp.float32))
    peak_ref[0] = jnp.max(peak)
    small[-1].wait()


def attend(shards, pick, units, first, last, *refs):
    given = len(pick)
    sources = refs[:given]
    table_ref, calm_in, turned_ref, placed_ref, cos_ref, sin_ref, row_ref = refs[given : given + 7]
    refs = refs[given + 7 :]
    if not first:
        most_in, sum_in, acc_in = refs[:3]
        refs = refs[3:]
    most_out, sum_out, acc_out, calm_out = refs[:4]
    refs = refs[4:]
    if last:
        whole_ref = refs[0]
        out_ref, out_sems = refs[-2:]
        refs = refs[1:-2]
    wide_ref, key_ref, value_ref, list_ref = refs
    heads, tiles, lanes_rows, dim = turned_ref.shape
    group = lanes_rows // tile_rows
    blocks = cos_ref.shape[0]
    block_len = placed_ref.shape[0] // blocks
    stride = 2 * heads
    raw_rows = block_len * stride
    slots = sources[0].shape[0] // raw_rows // shards
    scale = dim**-0.5 * math.log2(math.e)
    lowest = [choose(table_ref[3 * blocks + tiles]) for choose in pick]
    spots = units * unit_blocks

    def find(block, found):
        owner = table_ref[block]
        hit = jnp.bool_(False)
        for base in lowest:
            hit = hit | ((owner >= base) & (owner < base + shards))
        list_ref[found] = block
        return found + hit.astype(jnp.int32)

    lax.fori_loop(0, blocks, find, jnp.int32(0))
    ones = jnp.ones((dim, dim), jnp.bfloat16)

    def load(turn_number, peak):
        for lane in range(chunk):
            spot = turn_number * chunk + lane
            block = list_ref[spot]
            owner = table_ref[block]
            raw = None
            for source, base in zip(sources, lowest):
                here = (owner >= base) & (owner < base + shards)
                start = ((owner - base) * slots + table_ref[blocks + block]) * raw_rows
                start = pl.multiple_of(jnp.where(here, start, 0), raw_rows)
                found = source[pl.ds(start, raw_rows), :].astype(jnp.float32)
                raw = found if raw is None else jnp.where(here, found, raw)
            wide_ref[lane] = raw
            began = table_ref[2 * blocks + block]
            cosine = cos_ref[pl.ds(began, 1), :]
            sine = sin_ref[pl.ds(began, 1), :]
            fresh = placed_ref[
                pl.ds(pl.multiple_of(block * block_len, block_len), block_len), :
            ].astype(jnp.float32)
            renewed = fresh[:, heads * 2 * dim :] > 0.5
            at = pl.ds(pl.multiple_of(spot * block_len, block_len), block_len)
            for head in range(heads):
                key = turn(wide_ref[lane, pl.ds(head, block_len, stride=stride), :], cosine, sine)
                value = wide_ref[lane, pl.ds(heads + head, block_len, stride=stride), :]
                begin = head * 2 * dim
                key = jnp.where(renewed, fresh[:, begin : begin + dim], key)
                key_ref[head, at, :] = key.astype(jnp.bfloat16)
                value_ref[head, at, :] = jnp.where(
                    renewed, fresh[:, begin + dim : begin + 2 * dim], value
                ).astype(jnp.bfloat16)
                lengths = jnp.dot(
                    (key * key).astype(jnp.bfloat16), ones, preferred_element_type=jnp.float32
                )
                peak = jnp.maximum(peak, jnp.max(lengths.reshape(-1, 8, dim), axis=0))
        return peak

    peak = lax.fori_loop(0, spots // chunk, load, jnp.zeros((8, dim), jnp.float32))
    room = (calm_in[0] < 1e38) & (calm_in[0] * jnp.max(peak) <= (bound / scale) ** 2)
    calm = room.astype(jnp.float32)
    calm_out[0] = jnp.where(room, calm_in[0], jnp.float32(3e38))

    def query_mask(tile):
        row_at = pl.ds(pl.multiple_of(tile * tile_rows, tile_rows), tile_rows)
        row_pos = row_ref[row_at, :]
        lane = lax.broadcasted_iota(jnp.int32, (tile_rows, block_len), 1)
        return lambda spot: (lane + list_ref[spot] * block_len <= row_pos)[None]

    def scored(head, tile, first_spot, count, seen):
        at = pl.ds(pl.multiple_of(first_spot * block_len, block_len), count * block_len)
        scores = lax.dot_general(
            turned_ref[head, tile],
            key_ref[head, at, :],
            (((1,), (1,)), ((), ())),
            preferred_element_type=jnp.float32,
        )
        return at, [
            jnp.where(
                seen[spot],
                scores[:, spot * block_len : (spot + 1) * block_len].reshape(
                    group, tile_rows, block_len
                ),
                2 * low,
            ).reshape(lanes_rows, block_len)
            for spot in range(count)
        ]

    def weighed(head, at, parts):
        return functools.reduce(jnp.add, parts), jnp.dot(
            jnp.concatenate([part.astype(jnp.bfloat16) for part in parts], axis=1),
            value_ref[head, at, :],
            preferred_element_type=jnp.float32,
        )

    def write(head, tile, total, acc):
        sum_out[head, tile] = total
        acc_out[head, tile] = acc

    def finish(head, tile, total, acc):
        result = (acc / jnp.sum(total, axis=1, keepdims=True)).astype(jnp.bfloat16)
        row_at = pl.ds(pl.multiple_of(tile * tile_rows, tile_rows), tile_rows)
        for member in range(group):
            column = (head * group + member) * dim
            out_ref[row_at, column : column + dim] = result[
                member * tile_rows : (member + 1) * tile_rows
            ]

    def leave(tile):
        row_at = pl.ds(pl.multiple_of(tile * tile_rows, tile_rows), tile_rows)
        return pltpu.make_async_copy(
            out_ref.at[row_at, :], whole_ref.at[row_at, :], out_sems.at[tile]
        )

    def quick(tile, carry):
        furthest = table_ref[3 * blocks + tile]
        visible = query_mask(tile)
        for unit in range(units):
            fresh = first and unit == 0
            ends = last and unit == units - 1
            before = (sum_in, acc_in) if unit == 0 and not first else (sum_out, acc_out)
            first_spot = unit * unit_blocks
            active = jnp.int32(0)
            for spot in range(unit_blocks):
                begins = list_ref[first_spot + spot] * block_len
                active = active + (begins <= furthest).astype(jnp.int32)
            after = finish if ends else write
            for count in range(0, unit_blocks + 1, grain):

                @pl.when((active + grain - 1) // grain == count // grain)
                def _(count=count):
                    if not count and not fresh and not ends:
                        return
                    seen = [visible(first_spot + spot) for spot in range(count)]
                    for head in range(heads):
                        total = acc = jnp.zeros((lanes_rows, dim), jnp.float32)
                        if count:
                            at, parts = scored(head, tile, first_spot, count, seen)
                            parts = [jnp.exp2(part * scale) for part in parts]
                            total, acc = weighed(head, at, parts)
                        if not fresh:
                            total = before[0][head, tile] + total
                            acc = before[1][head, tile] + acc
                        after(head, tile, total, acc)

        if last:
            leave(tile).start()
        return carry

    def careful(tile, carry):
        furthest = table_ref[3 * blocks + tile]
        visible = query_mask(tile)

        def begin(head, ignored):
            if first:
                nothing = jnp.zeros((lanes_rows, dim), jnp.float32)
                most_out[head, tile] = nothing + low
                write(head, tile, nothing, nothing)
            else:
                total = sum_in[head, tile]
                most_out[head, tile] = jnp.where(
                    calm_in[0] < 1e38,
                    jnp.where(jnp.max(total, axis=1, keepdims=True) > 0, 0.0, low),
                    most_in[head, tile],
                )
                write(head, tile, total, acc_in[head, tile])
            return ignored

        lax.fori_loop(0, heads, begin, 0)

        def one(step, ignored):
            head = step % heads
            spot = step // heads

            @pl.when(list_ref[spot] * block_len <= furthest)
            def _():
                at, parts = scored(head, tile, spot, 1, [visible(spot)])
                was = most_out[head, tile]
                most = jnp.maximum(was, jnp.max(parts[0], axis=1, keepdims=True))
                total, acc = weighed(head, at, [jnp.exp2((parts[0] - most) * scale)])
                shrink = jnp.exp2((was - most) * scale)
                most_out[head, tile] = most
                write(
                    head,
                    tile,
                    sum_out[head, tile] * shrink + total,
                    acc_out[head, tile] * shrink + acc,
                )

            return ignored

        lax.fori_loop(0, spots * heads, one, 0)
        if last:
            for head in range(heads):
                finish(head, tile, sum_out[head, tile], acc_out[head, tile])
            leave(tile).start()
        return carry

    @pl.when(calm > 0.5)
    def _():
        lax.fori_loop(0, tiles, quick, 0)

    @pl.when(calm < 0.5)
    def _():
        lax.fori_loop(0, tiles, careful, 0)

    if last:
        for tile in range(tiles):
            leave(tile).wait()


def on_device(count, store_kv, block_owner, block_slot, span_len, row_index, fresh_q, fresh_kv):
    stored, block_len, heads, pair_width = store_kv.shape
    dim = pair_width // 2
    blocks = block_slot.shape[1]
    rows = row_index.shape[1]
    group = fresh_q.shape[2] // (heads * dim)
    tiles = rows // tile_rows
    lanes_rows = tile_rows * group
    raw_rows = block_len * 2 * heads

    def flat(array):
        lead = math.prod(array.shape[:-2])
        split = array.reshape(lead, heads, 2, dim)
        return split.transpose(0, 2, 1, 3).reshape(lead * 2 * heads, dim)

    store = flat(store_kv)
    place = lax.axis_index("req").reshape(1)
    row_pos = row_index[0]
    row_cos, row_sin = tables(row_pos.astype(jnp.float32), dim)
    cos, sin = tables(block_len * jnp.arange(blocks, dtype=jnp.float32), dim)
    row_lanes = jnp.broadcast_to(row_pos[:, None], (rows, block_len))
    wide = heads * 2 * dim + dim
    turned, placed, close, table, peak = pl.pallas_call(
        prepare,
        out_shape=(
            pltpu.VMEM((heads, tiles, lanes_rows, dim), jnp.bfloat16),
            pltpu.VMEM((blocks * block_len, wide), jnp.bfloat16),
            pltpu.VMEM(store.shape, jnp.bfloat16),
            pltpu.SMEM((3 * blocks + tiles + 1,), jnp.int32),
            pltpu.SMEM((1,), jnp.float32),
        ),
        in_specs=[anywhere] * 7 + [smem, vmem, vmem],
        out_specs=(vmem, vmem, vmem, smem, smem),
        scratch_shapes=[
            pltpu.VMEM((rows, heads * group * dim), jnp.bfloat16),
            pltpu.VMEM((rows * 2 * heads, dim), jnp.bfloat16),
            pltpu.VMEM((rows * 2 * heads, dim), jnp.float32),
            pltpu.VMEM((rows, wide), jnp.bfloat16),
            pltpu.VMEM((1, rows), jnp.int32),
            pltpu.SMEM((1, rows), jnp.int32),
            pltpu.SMEM((1, blocks), jnp.int32),
            pltpu.SMEM((1, blocks), jnp.int32),
            pltpu.SMEM(span_len.shape, jnp.int32),
            pltpu.SemaphoreType.DMA((tiles + 7,)),
        ],
        compiler_params=params,
        name="prepare",
    )(
        away(fresh_q[0]), away(flat(fresh_kv)), away(store), away(block_owner[:, :, 0]),
        away(block_slot), away(span_len), away(row_index), place, near(row_cos), near(row_sin),
    )

    def attention(number, last, sources, pick, shards, units, state):
        first = len(state) == 1
        state_shape = pltpu.VMEM((heads, tiles, lanes_rows, dim), jnp.float32)
        inputs = [near(source) for source in sources]
        inputs += [held(table), held(state[-1])]
        inputs += [near(array) for array in (turned, placed, cos, sin, row_lanes)]
        specs = [vmem] * len(sources) + [smem] * 2 + [vmem] * 5
        spots = units * unit_blocks
        result = [jax.ShapeDtypeStruct((rows, heads * group * dim), jnp.bfloat16)] if last else []
        return pl.pallas_call(
            functools.partial(attend, shards, pick, units, first, last),
            out_shape=[state_shape] * 3 + [pltpu.SMEM((1,), jnp.float32)] + result,
            in_specs=specs + [vmem] * (len(state) - 1),
            out_specs=[vmem] * 3 + [smem] + [anywhere] * len(result),
            input_output_aliases={}
            if first
            else {len(specs) + entry: entry for entry in range(3)},
            scratch_shapes=[
                pltpu.VMEM((chunk, raw_rows, dim), jnp.float32),
                pltpu.VMEM((heads, spots * block_len, dim), jnp.bfloat16),
                pltpu.VMEM((heads, spots * block_len, dim), jnp.bfloat16),
                pltpu.SMEM((blocks + 1,), jnp.int32),
            ]
            + (
                [
                    pltpu.VMEM((rows, heads * group * dim), jnp.bfloat16),
                    pltpu.SemaphoreType.DMA((tiles,)),
                ]
                if last
                else []
            ),
            compiler_params=params,
            name=f"attend_{number}",
        )(*inputs, *[near(entry) for entry in state[:-1]])

    if count != 4:
        everything = lax.all_gather(store, "req", axis=0, tiled=True)
        return attention(
            0, True, [everything], [lambda at: 0], count, blocks // unit_blocks, (peak,)
        )[-1][None]
    outer = [(0, 1), (1, 0), (2, 3), (3, 2)]
    inner = [(1, 2), (2, 1)]
    outward = [(1, 0), (2, 3)]
    none = -(1 << 16)
    is_end = lambda at: (at == 0) | (at == 3)

    def send(array, pairs):
        return lax.ppermute(array, "req", pairs)

    beside = send(store, outer)
    across = send(store, inner)
    store, close, turned = lax.optimization_barrier((store, close, turned))
    third_in = send(store, [(0, 2), (3, 1)])
    across, close, turned = lax.optimization_barrier((across, close, turned))
    second = send(across, outward)
    state = attention(0, False, [close], [lambda at: at], 1, 1, (peak,))
    third_in, beside, state = lax.optimization_barrier((third_in, beside, state))
    third = send(third_in, outward)
    state = attention(1, False, [beside], [lambda at: at ^ 1], 1, 1, state)
    second, state = lax.optimization_barrier((second, state))
    state = attention(
        2,
        False,
        [second, across],
        [
            lambda at: jnp.where(is_end(at), jnp.where(at == 0, 2, 1), none),
            lambda at: jnp.where(is_end(at), none, 3 - at),
        ],
        1,
        1,
        state,
    )
    third, state = lax.optimization_barrier((third, state))
    return attention(
        3,
        True,
        [third, third_in],
        [
            lambda at: jnp.where(is_end(at), 3 - at, none),
            lambda at: jnp.where(is_end(at), none, (3 - at) ^ 1),
        ],
        1,
        1,
        state,
    )[-1][None]


def solution(mesh):
    placed = (
        P(("grp", "req"), None, "kvh", None),
        P(("grp", "req"), None, None),
        P(("grp", "req"), None),
        P(("grp", "req"), None),
        P(("grp", "req"), None),
        P(("grp", "req"), None, "kvh"),
        P(("grp", "req"), None, "kvh", None),
    )
    return jax.shard_map(
        functools.partial(on_device, mesh.shape["req"]),
        mesh=mesh,
        in_specs=placed,
        out_specs=P(("grp", "req"), None, "kvh"),
        check_vma=False,
    )
```

```python
import functools
import math

import jax
import jax.numpy as jnp
from jax import lax
from jax.experimental import pallas as pl
from jax.experimental.pallas import tpu as pltpu
from jax.sharding import PartitionSpec as P

rope_base = 500000.0
tile_rows = 96
unit_blocks = 6
low = -1e30
bound = 105.0
grain = 1
chunk = 6
vmem = pl.BlockSpec(memory_space=pltpu.VMEM)
smem = pl.BlockSpec(memory_space=pltpu.SMEM)
anywhere = pl.BlockSpec(memory_space=pl.ANY)
params = pltpu.CompilerParams(vmem_limit_bytes=28 << 20)


def near(array):
    return pltpu.with_memory_space_constraint(array, pltpu.VMEM)


def held(array):
    return pltpu.with_memory_space_constraint(array, pltpu.SMEM)


def away(array):
    return pltpu.with_memory_space_constraint(array, pltpu.HBM)


def tables(position, head_dim):
    lane = lax.broadcasted_iota(jnp.int32, (position.shape[0], head_dim), 1)
    half_dim = head_dim // 2
    pair_index = (lane % half_dim).astype(jnp.float32)
    inv_freq = jnp.exp(pair_index * (-2.0 / head_dim) * jnp.log(jnp.float32(rope_base)))
    angles = position[:, None] * inv_freq
    sine = jnp.sin(angles)
    return jnp.cos(angles), jnp.where(lane < half_dim, -sine, sine)


def turn(field, cosine, sine):
    return field * cosine + pltpu.roll(field, field.shape[1] // 2, 1) * sine


def prepare(
    query_ref, fresh_ref, store_ref, owner_ref, slot_ref, span_ref, pos_ref, place_ref, cos_ref, sin_ref,
    turned_ref, placed_ref, near_ref, table_ref, peak_ref,
    raw_ref, flat_ref, wide_ref, all_ref, lanes_ref, row_smem, owner_smem, slot_smem, span_smem, sems,
):
    heads, tiles, lanes_rows, dim = turned_ref.shape
    group = lanes_rows // tile_rows
    placed_rows = placed_ref.shape[0]
    rows = cos_ref.shape[0]
    blocks = slot_ref.shape[1]

    def load_query(tile):
        at = pl.ds(pl.multiple_of(tile * tile_rows, tile_rows), tile_rows)
        return pltpu.make_async_copy(query_ref.at[at, :], raw_ref.at[at, :], sems.at[tile])

    small = [
        pltpu.make_async_copy(source, target, sems.at[tiles + number])
        for number, (source, target) in enumerate(
            (
                (pos_ref, lanes_ref),
                (fresh_ref, flat_ref),
                (pos_ref, row_smem),
                (owner_ref, owner_smem),
                (slot_ref, slot_smem),
                (span_ref, span_smem),
                (store_ref, near_ref),
            )
        )
    ]
    for copy in small[:-1]:
        copy.start()
    for tile in range(tiles):
        load_query(tile).start()
    small[-1].start()
    for copy in small[:-1]:
        copy.wait()
    wide_ref[...] = flat_ref[...].astype(jnp.float32)
    for head in range(heads):
        key = wide_ref[pl.ds(head, rows, stride=2 * heads), :]
        value = wide_ref[pl.ds(heads + head, rows, stride=2 * heads), :]
        all_ref[:, head * 2 * dim : head * 2 * dim + dim] = turn(
            key, cos_ref[...], sin_ref[...]
        ).astype(jnp.bfloat16)
        all_ref[:, head * 2 * dim + dim : (head + 1) * 2 * dim] = value.astype(jnp.bfloat16)
    all_ref[:, heads * 2 * dim :] = jnp.ones((rows, dim), jnp.bfloat16)
    step = 512

    def place(number, carry):
        at = pl.ds(pl.multiple_of(number * step, step), step)
        spot = lax.broadcasted_iota(jnp.int32, (step, rows), 0) + number * step
        chosen = jnp.where(spot == lanes_ref[...], 1.0, 0.0).astype(jnp.bfloat16)
        placed_ref[at, :] = jnp.dot(
            chosen, all_ref[...], preferred_element_type=jnp.float32
        ).astype(jnp.bfloat16)
        return carry

    lax.fori_loop(0, placed_rows // step, place, 0)

    def note(block, carry):
        began = jnp.int32(0)
        start = jnp.int32(0)
        for span in range(span_ref.shape[1]):
            began = jnp.where(start <= block, start, began)
            start = start + span_smem[0, span]
        table_ref[block] = owner_smem[0, block]
        table_ref[blocks + block] = slot_smem[0, block]
        table_ref[2 * blocks + block] = began
        return carry

    lax.fori_loop(0, blocks, note, 0)
    for tile in range(tiles):
        table_ref[3 * blocks + tile] = row_smem[0, (tile + 1) * tile_rows - 1]
    table_ref[3 * blocks + tiles] = place_ref[0]
    ones = jnp.ones((dim, dim), jnp.bfloat16)

    def turn_tile(tile, peak):
        load_query(tile).wait()
        at = pl.ds(pl.multiple_of(tile * tile_rows, tile_rows), tile_rows)
        cosine = cos_ref[at, :]
        sine = sin_ref[at, :]
        for head in range(heads):
            squares = []
            for member in range(group):
                column = (head * group + member) * dim
                field = raw_ref[at, column : column + dim].astype(jnp.float32)
                turned_ref[head, tile, member * tile_rows : (member + 1) * tile_rows, :] = turn(
                    field, cosine, sine
                ).astype(jnp.bfloat16)
                squares.append((field * field).astype(jnp.bfloat16))
            lengths = jnp.dot(
                jnp.concatenate(squares, axis=0), ones, preferred_element_type=jnp.float32
            )
            peak = jnp.maximum(peak, jnp.max(lengths.reshape(-1, 8, dim), axis=0))
        return peak

    peak = lax.fori_loop(0, tiles, turn_tile, jnp.zeros((8, dim), jnp.float32))
    peak_ref[0] = jnp.max(peak)
    small[-1].wait()


def attend(shards, pick, units, first, last, *refs):
    given = len(pick)
    sources = refs[:given]
    table_ref, calm_in, turned_ref, placed_ref, cos_ref, sin_ref, row_ref = refs[given : given + 7]
    refs = refs[given + 7 :]
    if not first:
        most_in, sum_in, acc_in = refs[:3]
        refs = refs[3:]
    most_out, sum_out, acc_out, calm_out = refs[:4]
    refs = refs[4:]
    if last:
        whole_ref = refs[0]
        out_ref, out_sems = refs[-2:]
        refs = refs[1:-2]
    wide_ref, key_ref, value_ref, list_ref = refs
    heads, tiles, lanes_rows, dim = turned_ref.shape
    group = lanes_rows // tile_rows
    blocks = cos_ref.shape[0]
    block_len = placed_ref.shape[0] // blocks
    stride = 2 * heads
    raw_rows = block_len * stride
    slots = sources[0].shape[0] // raw_rows // shards
    scale = dim**-0.5 * math.log2(math.e)
    lowest = [choose(table_ref[3 * blocks + tiles]) for choose in pick]
    spots = units * unit_blocks

    def find(block, found):
        owner = table_ref[block]
        hit = jnp.bool_(False)
        for base in lowest:
            hit = hit | ((owner >= base) & (owner < base + shards))
        list_ref[found] = block
        return found + hit.astype(jnp.int32)

    lax.fori_loop(0, blocks, find, jnp.int32(0))
    ones = jnp.ones((dim, dim), jnp.bfloat16)

    def load(turn_number, peak):
        for lane in range(chunk):
            spot = turn_number * chunk + lane
            block = list_ref[spot]
            owner = table_ref[block]
            raw = None
            for source, base in zip(sources, lowest):
                here = (owner >= base) & (owner < base + shards)
                start = ((owner - base) * slots + table_ref[blocks + block]) * raw_rows
                start = pl.multiple_of(jnp.where(here, start, 0), raw_rows)
                found = source[pl.ds(start, raw_rows), :].astype(jnp.float32)
                raw = found if raw is None else jnp.where(here, found, raw)
            wide_ref[lane] = raw
            began = table_ref[2 * blocks + block]
            cosine = cos_ref[pl.ds(began, 1), :]
            sine = sin_ref[pl.ds(began, 1), :]
            fresh = placed_ref[
                pl.ds(pl.multiple_of(block * block_len, block_len), block_len), :
            ].astype(jnp.float32)
            renewed = fresh[:, heads * 2 * dim :] > 0.5
            at = pl.ds(pl.multiple_of(spot * block_len, block_len), block_len)
            for head in range(heads):
                key = turn(wide_ref[lane, pl.ds(head, block_len, stride=stride), :], cosine, sine)
                value = wide_ref[lane, pl.ds(heads + head, block_len, stride=stride), :]
                begin = head * 2 * dim
                key = jnp.where(renewed, fresh[:, begin : begin + dim], key)
                key_ref[head, at, :] = key.astype(jnp.bfloat16)
                value_ref[head, at, :] = jnp.where(
                    renewed, fresh[:, begin + dim : begin + 2 * dim], value
                ).astype(jnp.bfloat16)
                lengths = jnp.dot(
                    (key * key).astype(jnp.bfloat16), ones, preferred_element_type=jnp.float32
                )
                peak = jnp.maximum(peak, jnp.max(lengths.reshape(-1, 8, dim), axis=0))
        return peak

    peak = lax.fori_loop(0, spots // chunk, load, jnp.zeros((8, dim), jnp.float32))
    room = (calm_in[0] < 1e38) & (calm_in[0] * jnp.max(peak) <= (bound / scale) ** 2)
    calm = room.astype(jnp.float32)
    calm_out[0] = jnp.where(room, calm_in[0], jnp.float32(3e38))

    def query_mask(tile):
        row_at = pl.ds(pl.multiple_of(tile * tile_rows, tile_rows), tile_rows)
        row_pos = row_ref[row_at, :]
        lane = lax.broadcasted_iota(jnp.int32, (tile_rows, block_len), 1)
        return lambda spot: (lane + list_ref[spot] * block_len <= row_pos)[None]

    def scored(head, tile, first_spot, count, seen):
        at = pl.ds(pl.multiple_of(first_spot * block_len, block_len), count * block_len)
        scores = lax.dot_general(
            turned_ref[head, tile],
            key_ref[head, at, :],
            (((1,), (1,)), ((), ())),
            preferred_element_type=jnp.float32,
        )
        return at, [
            jnp.where(
                seen[spot],
                scores[:, spot * block_len : (spot + 1) * block_len].reshape(
                    group, tile_rows, block_len
                ),
                2 * low,
            ).reshape(lanes_rows, block_len)
            for spot in range(count)
        ]

    def weighed(head, at, parts):
        return functools.reduce(jnp.add, parts), jnp.dot(
            jnp.concatenate([part.astype(jnp.bfloat16) for part in parts], axis=1),
            value_ref[head, at, :],
            preferred_element_type=jnp.float32,
        )

    def write(head, tile, total, acc):
        sum_out[head, tile] = total
        acc_out[head, tile] = acc

    def finish(head, tile, total, acc):
        result = (acc / jnp.sum(total, axis=1, keepdims=True)).astype(jnp.bfloat16)
        row_at = pl.ds(pl.multiple_of(tile * tile_rows, tile_rows), tile_rows)
        for member in range(group):
            column = (head * group + member) * dim
            out_ref[row_at, column : column + dim] = result[
                member * tile_rows : (member + 1) * tile_rows
            ]

    def leave(tile):
        row_at = pl.ds(pl.multiple_of(tile * tile_rows, tile_rows), tile_rows)
        return pltpu.make_async_copy(
            out_ref.at[row_at, :], whole_ref.at[row_at, :], out_sems.at[tile]
        )

    def quick(tile, carry):
        furthest = table_ref[3 * blocks + tile]
        visible = query_mask(tile)
        for unit in range(units):
            fresh = first and unit == 0
            ends = last and unit == units - 1
            before = (sum_in, acc_in) if unit == 0 and not first else (sum_out, acc_out)
            first_spot = unit * unit_blocks
            active = jnp.int32(0)
            for spot in range(unit_blocks):
                begins = list_ref[first_spot + spot] * block_len
                active = active + (begins <= furthest).astype(jnp.int32)
            after = finish if ends else write
            for count in range(0, unit_blocks + 1, grain):

                @pl.when((active + grain - 1) // grain == count // grain)
                def _(count=count):
                    if not count and not fresh and not ends:
                        return
                    seen = [visible(first_spot + spot) for spot in range(count)]
                    for head in range(heads):
                        total = acc = jnp.zeros((lanes_rows, dim), jnp.float32)
                        if count:
                            at, parts = scored(head, tile, first_spot, count, seen)
                            parts = [jnp.exp2(part * scale) for part in parts]
                            total, acc = weighed(head, at, parts)
                        if not fresh:
                            total = before[0][head, tile] + total
                            acc = before[1][head, tile] + acc
                        after(head, tile, total, acc)

        if last:
            leave(tile).start()
        return carry

    def careful(tile, carry):
        furthest = table_ref[3 * blocks + tile]
        visible = query_mask(tile)

        def begin(head, ignored):
            if first:
                nothing = jnp.zeros((lanes_rows, dim), jnp.float32)
                most_out[head, tile] = nothing + low
                write(head, tile, nothing, nothing)
            else:
                total = sum_in[head, tile]
                most_out[head, tile] = jnp.where(
                    calm_in[0] < 1e38,
                    jnp.where(jnp.max(total, axis=1, keepdims=True) > 0, 0.0, low),
                    most_in[head, tile],
                )
                write(head, tile, total, acc_in[head, tile])
            return ignored

        lax.fori_loop(0, heads, begin, 0)

        def one(step, ignored):
            head = step % heads
            spot = step // heads

            @pl.when(list_ref[spot] * block_len <= furthest)
            def _():
                at, parts = scored(head, tile, spot, 1, [visible(spot)])
                was = most_out[head, tile]
                most = jnp.maximum(was, jnp.max(parts[0], axis=1, keepdims=True))
                total, acc = weighed(head, at, [jnp.exp2((parts[0] - most) * scale)])
                shrink = jnp.exp2((was - most) * scale)
                most_out[head, tile] = most
                write(
                    head,
                    tile,
                    sum_out[head, tile] * shrink + total,
                    acc_out[head, tile] * shrink + acc,
                )

            return ignored

        lax.fori_loop(0, spots * heads, one, 0)
        if last:
            for head in range(heads):
                finish(head, tile, sum_out[head, tile], acc_out[head, tile])
            leave(tile).start()
        return carry

    @pl.when(calm > 0.5)
    def _():
        lax.fori_loop(0, tiles, quick, 0)

    @pl.when(calm < 0.5)
    def _():
        lax.fori_loop(0, tiles, careful, 0)

    if last:
        for tile in range(tiles):
            leave(tile).wait()


def on_device(count, store_kv, block_owner, block_slot, span_len, row_index, fresh_q, fresh_kv):
    stored, block_len, heads, pair_width = store_kv.shape
    dim = pair_width // 2
    blocks = block_slot.shape[1]
    rows = row_index.shape[1]
    group = fresh_q.shape[2] // (heads * dim)
    tiles = rows // tile_rows
    lanes_rows = tile_rows * group
    raw_rows = block_len * 2 * heads

    def flat(array):
        lead = math.prod(array.shape[:-2])
        split = array.reshape(lead, heads, 2, dim)
        return split.transpose(0, 2, 1, 3).reshape(lead * 2 * heads, dim)

    store = flat(store_kv)
    place = lax.axis_index("req").reshape(1)
    row_pos = row_index[0]
    row_cos, row_sin = tables(row_pos.astype(jnp.float32), dim)
    cos, sin = tables(block_len * jnp.arange(blocks, dtype=jnp.float32), dim)
    row_lanes = jnp.broadcast_to(row_pos[:, None], (rows, block_len))
    wide = heads * 2 * dim + dim
    turned, placed, close, table, peak = pl.pallas_call(
        prepare,
        out_shape=(
            pltpu.VMEM((heads, tiles, lanes_rows, dim), jnp.bfloat16),
            pltpu.VMEM((blocks * block_len, wide), jnp.bfloat16),
            pltpu.VMEM(store.shape, jnp.bfloat16),
            pltpu.SMEM((3 * blocks + tiles + 1,), jnp.int32),
            pltpu.SMEM((1,), jnp.float32),
        ),
        in_specs=[anywhere] * 7 + [smem, vmem, vmem],
        out_specs=(vmem, vmem, vmem, smem, smem),
        scratch_shapes=[
            pltpu.VMEM((rows, heads * group * dim), jnp.bfloat16),
            pltpu.VMEM((rows * 2 * heads, dim), jnp.bfloat16),
            pltpu.VMEM((rows * 2 * heads, dim), jnp.float32),
            pltpu.VMEM((rows, wide), jnp.bfloat16),
            pltpu.VMEM((1, rows), jnp.int32),
            pltpu.SMEM((1, rows), jnp.int32),
            pltpu.SMEM((1, blocks), jnp.int32),
            pltpu.SMEM((1, blocks), jnp.int32),
            pltpu.SMEM(span_len.shape, jnp.int32),
            pltpu.SemaphoreType.DMA((tiles + 7,)),
        ],
        compiler_params=params,
        name="prepare",
    )(
        away(fresh_q[0]), away(flat(fresh_kv)), away(store), away(block_owner[:, :, 0]),
        away(block_slot), away(span_len), away(row_index), place, near(row_cos), near(row_sin),
    )

    def attention(number, last, sources, pick, shards, units, state):
        first = len(state) == 1
        state_shape = pltpu.VMEM((heads, tiles, lanes_rows, dim), jnp.float32)
        inputs = [near(source) for source in sources]
        inputs += [held(table), held(state[-1])]
        inputs += [near(array) for array in (turned, placed, cos, sin, row_lanes)]
        specs = [vmem] * len(sources) + [smem] * 2 + [vmem] * 5
        spots = units * unit_blocks
        result = [jax.ShapeDtypeStruct((rows, heads * group * dim), jnp.bfloat16)] if last else []
        return pl.pallas_call(
            functools.partial(attend, shards, pick, units, first, last),
            out_shape=[state_shape] * 3 + [pltpu.SMEM((1,), jnp.float32)] + result,
            in_specs=specs + [vmem] * (len(state) - 1),
            out_specs=[vmem] * 3 + [smem] + [anywhere] * len(result),
            input_output_aliases={}
            if first
            else {len(specs) + entry: entry for entry in range(3)},
            scratch_shapes=[
                pltpu.VMEM((chunk, raw_rows, dim), jnp.float32),
                pltpu.VMEM((heads, spots * block_len, dim), jnp.bfloat16),
                pltpu.VMEM((heads, spots * block_len, dim), jnp.bfloat16),
                pltpu.SMEM((blocks + 1,), jnp.int32),
            ]
            + (
                [
                    pltpu.VMEM((rows, heads * group * dim), jnp.bfloat16),
                    pltpu.SemaphoreType.DMA((tiles,)),
                ]
                if last
                else []
            ),
            compiler_params=params,
            name=f"attend_{number}",
        )(*inputs, *[near(entry) for entry in state[:-1]])

    if count != 4:
        everything = lax.all_gather(store, "req", axis=0, tiled=True)
        return attention(
            0, True, [everything], [lambda at: 0], count, blocks // unit_blocks, (peak,)
        )[-1][None]
    outer = [(0, 1), (1, 0), (2, 3), (3, 2)]
    inner = [(1, 2), (2, 1)]
    outward = [(1, 0), (2, 3)]
    none = -(1 << 16)
    is_end = lambda at: (at == 0) | (at == 3)

    def send(array, pairs):
        return lax.ppermute(array, "req", pairs)

    beside = send(store, outer)
    across = send(store, inner)
    store, close, turned = lax.optimization_barrier((store, close, turned))
    third_in = send(store, [(0, 2), (3, 1)])
    across, close, turned = lax.optimization_barrier((across, close, turned))
    second = send(across, outward)
    state = attention(0, False, [close], [lambda at: at], 1, 1, (peak,))
    third_in, beside, state = lax.optimization_barrier((third_in, beside, state))
    third = send(third_in, outward)
    state = attention(1, False, [beside], [lambda at: at ^ 1], 1, 1, state)
    second, state = lax.optimization_barrier((second, state))
    state = attention(
        2,
        False,
        [second, across],
        [
            lambda at: jnp.where(is_end(at), jnp.where(at == 0, 2, 1), none),
            lambda at: jnp.where(is_end(at), none, 3 - at),
        ],
        1,
        1,
        state,
    )
    third, state = lax.optimization_barrier((third, state))
    return attention(
        3,
        True,
        [third, third_in],
        [
            lambda at: jnp.where(is_end(at), 3 - at, none),
            lambda at: jnp.where(is_end(at), none, (3 - at) ^ 1),
        ],
        1,
        1,
        state,
    )[-1][None]


def solution(mesh):
    placed = (
        P(("grp", "req"), None, "kvh", None),
        P(("grp", "req"), None, None),
        P(("grp", "req"), None),
        P(("grp", "req"), None),
        P(("grp", "req"), None),
        P(("grp", "req"), None, "kvh"),
        P(("grp", "req"), None, "kvh", None),
    )
    return jax.shard_map(
        functools.partial(on_device, mesh.shape["req"]),
        mesh=mesh,
        in_specs=placed,
        out_specs=P(("grp", "req"), None, "kvh"),
        check_vma=False,
    )
```

```python
import functools
import math

import jax
import jax.numpy as jnp
from jax import lax
from jax.experimental import pallas as pl
from jax.experimental.pallas import tpu as pltpu
from jax.sharding import PartitionSpec as P

rope_base = 500000.0
tile_rows = 128
unit_blocks = 6
low = -1e30
bound = 105.0
grain = 1
chunk = 6
vmem = pl.BlockSpec(memory_space=pltpu.VMEM)
smem = pl.BlockSpec(memory_space=pltpu.SMEM)
anywhere = pl.BlockSpec(memory_space=pl.ANY)
params = pltpu.CompilerParams(vmem_limit_bytes=28 << 20)


def near(array):
    return pltpu.with_memory_space_constraint(array, pltpu.VMEM)


def held(array):
    return pltpu.with_memory_space_constraint(array, pltpu.SMEM)


def away(array):
    return pltpu.with_memory_space_constraint(array, pltpu.HBM)


def tables(position, head_dim):
    lane = lax.broadcasted_iota(jnp.int32, (position.shape[0], head_dim), 1)
    half_dim = head_dim // 2
    pair_index = (lane % half_dim).astype(jnp.float32)
    inv_freq = jnp.exp(pair_index * (-2.0 / head_dim) * jnp.log(jnp.float32(rope_base)))
    angles = position[:, None] * inv_freq
    sine = jnp.sin(angles)
    return jnp.cos(angles), jnp.where(lane < half_dim, -sine, sine)


def turn(field, cosine, sine):
    return field * cosine + pltpu.roll(field, field.shape[1] // 2, 1) * sine


def prepare(
    query_ref, fresh_ref, store_ref, owner_ref, slot_ref, span_ref, pos_ref, place_ref, cos_ref, sin_ref,
    turned_ref, placed_ref, near_ref, table_ref, peak_ref,
    raw_ref, flat_ref, wide_ref, all_ref, lanes_ref, row_smem, owner_smem, slot_smem, span_smem, sems,
):
    heads, tiles, lanes_rows, dim = turned_ref.shape
    group = lanes_rows // tile_rows
    placed_rows = placed_ref.shape[0]
    rows = cos_ref.shape[0]
    blocks = slot_ref.shape[1]

    def load_query(tile):
        at = pl.ds(pl.multiple_of(tile * tile_rows, tile_rows), tile_rows)
        return pltpu.make_async_copy(query_ref.at[at, :], raw_ref.at[at, :], sems.at[tile])

    small = [
        pltpu.make_async_copy(source, target, sems.at[tiles + number])
        for number, (source, target) in enumerate(
            (
                (pos_ref, lanes_ref),
                (fresh_ref, flat_ref),
                (pos_ref, row_smem),
                (owner_ref, owner_smem),
                (slot_ref, slot_smem),
                (span_ref, span_smem),
                (store_ref, near_ref),
            )
        )
    ]
    for copy in small[:-1]:
        copy.start()
    for tile in range(tiles):
        load_query(tile).start()
    small[-1].start()
    for copy in small[:-1]:
        copy.wait()
    wide_ref[...] = flat_ref[...].astype(jnp.float32)
    for head in range(heads):
        key = wide_ref[pl.ds(head, rows, stride=2 * heads), :]
        value = wide_ref[pl.ds(heads + head, rows, stride=2 * heads), :]
        all_ref[:, head * 2 * dim : head * 2 * dim + dim] = turn(
            key, cos_ref[...], sin_ref[...]
        ).astype(jnp.bfloat16)
        all_ref[:, head * 2 * dim + dim : (head + 1) * 2 * dim] = value.astype(jnp.bfloat16)
    all_ref[:, heads * 2 * dim :] = jnp.ones((rows, dim), jnp.bfloat16)
    step = 512

    def place(number, carry):
        at = pl.ds(pl.multiple_of(number * step, step), step)
        spot = lax.broadcasted_iota(jnp.int32, (step, rows), 0) + number * step
        chosen = jnp.where(spot == lanes_ref[...], 1.0, 0.0).astype(jnp.bfloat16)
        placed_ref[at, :] = jnp.dot(
            chosen, all_ref[...], preferred_element_type=jnp.float32
        ).astype(jnp.bfloat16)
        return carry

    lax.fori_loop(0, placed_rows // step, place, 0)

    def note(block, carry):
        began = jnp.int32(0)
        start = jnp.int32(0)
        for span in range(span_ref.shape[1]):
            began = jnp.where(start <= block, start, began)
            start = start + span_smem[0, span]
        table_ref[block] = owner_smem[0, block]
        table_ref[blocks + block] = slot_smem[0, block]
        table_ref[2 * blocks + block] = began
        return carry

    lax.fori_loop(0, blocks, note, 0)
    for tile in range(tiles):
        table_ref[3 * blocks + tile] = row_smem[0, (tile + 1) * tile_rows - 1]
    table_ref[3 * blocks + tiles] = place_ref[0]
    ones = jnp.ones((dim, dim), jnp.bfloat16)

    def turn_tile(tile, peak):
        load_query(tile).wait()
        at = pl.ds(pl.multiple_of(tile * tile_rows, tile_rows), tile_rows)
        cosine = cos_ref[at, :]
        sine = sin_ref[at, :]
        for head in range(heads):
            squares = []
            for member in range(group):
                column = (head * group + member) * dim
                field = raw_ref[at, column : column + dim].astype(jnp.float32)
                turned_ref[head, tile, member * tile_rows : (member + 1) * tile_rows, :] = turn(
                    field, cosine, sine
                ).astype(jnp.bfloat16)
                squares.append((field * field).astype(jnp.bfloat16))
            lengths = jnp.dot(
                jnp.concatenate(squares, axis=0), ones, preferred_element_type=jnp.float32
            )
            peak = jnp.maximum(peak, jnp.max(lengths.reshape(-1, 8, dim), axis=0))
        return peak

    peak = lax.fori_loop(0, tiles, turn_tile, jnp.zeros((8, dim), jnp.float32))
    peak_ref[0] = jnp.max(peak)
    small[-1].wait()


def attend(shards, pick, units, first, last, *refs):
    given = len(pick)
    sources = refs[:given]
    table_ref, calm_in, turned_ref, placed_ref, cos_ref, sin_ref, row_ref = refs[given : given + 7]
    refs = refs[given + 7 :]
    if not first:
        most_in, sum_in, acc_in = refs[:3]
        refs = refs[3:]
    most_out, sum_out, acc_out, calm_out = refs[:4]
    refs = refs[4:]
    if last:
        whole_ref = refs[0]
        out_ref, out_sems = refs[-2:]
        refs = refs[1:-2]
    wide_ref, key_ref, value_ref, list_ref = refs
    heads, tiles, lanes_rows, dim = turned_ref.shape
    group = lanes_rows // tile_rows
    blocks = cos_ref.shape[0]
    block_len = placed_ref.shape[0] // blocks
    stride = 2 * heads
    raw_rows = block_len * stride
    slots = sources[0].shape[0] // raw_rows // shards
    scale = dim**-0.5 * math.log2(math.e)
    lowest = [choose(table_ref[3 * blocks + tiles]) for choose in pick]
    spots = units * unit_blocks

    def find(block, found):
        owner = table_ref[block]
        hit = jnp.bool_(False)
        for base in lowest:
            hit = hit | ((owner >= base) & (owner < base + shards))
        list_ref[found] = block
        return found + hit.astype(jnp.int32)

    lax.fori_loop(0, blocks, find, jnp.int32(0))
    ones = jnp.ones((dim, dim), jnp.bfloat16)

    def load(turn_number, peak):
        for lane in range(chunk):
            spot = turn_number * chunk + lane
            block = list_ref[spot]
            owner = table_ref[block]
            raw = None
            for source, base in zip(sources, lowest):
                here = (owner >= base) & (owner < base + shards)
                start = ((owner - base) * slots + table_ref[blocks + block]) * raw_rows
                start = pl.multiple_of(jnp.where(here, start, 0), raw_rows)
                found = source[pl.ds(start, raw_rows), :].astype(jnp.float32)
                raw = found if raw is None else jnp.where(here, found, raw)
            wide_ref[lane] = raw
            began = table_ref[2 * blocks + block]
            cosine = cos_ref[pl.ds(began, 1), :]
            sine = sin_ref[pl.ds(began, 1), :]
            fresh = placed_ref[
                pl.ds(pl.multiple_of(block * block_len, block_len), block_len), :
            ].astype(jnp.float32)
            renewed = fresh[:, heads * 2 * dim :] > 0.5
            at = pl.ds(pl.multiple_of(spot * block_len, block_len), block_len)
            for head in range(heads):
                key = turn(wide_ref[lane, pl.ds(head, block_len, stride=stride), :], cosine, sine)
                value = wide_ref[lane, pl.ds(heads + head, block_len, stride=stride), :]
                begin = head * 2 * dim
                key = jnp.where(renewed, fresh[:, begin : begin + dim], key)
                key_ref[head, at, :] = key.astype(jnp.bfloat16)
                value_ref[head, at, :] = jnp.where(
                    renewed, fresh[:, begin + dim : begin + 2 * dim], value
                ).astype(jnp.bfloat16)
                lengths = jnp.dot(
                    (key * key).astype(jnp.bfloat16), ones, preferred_element_type=jnp.float32
                )
                peak = jnp.maximum(peak, jnp.max(lengths.reshape(-1, 8, dim), axis=0))
        return peak

    peak = lax.fori_loop(0, spots // chunk, load, jnp.zeros((8, dim), jnp.float32))
    room = (calm_in[0] < 1e38) & (calm_in[0] * jnp.max(peak) <= (bound / scale) ** 2)
    calm = room.astype(jnp.float32)
    calm_out[0] = jnp.where(room, calm_in[0], jnp.float32(3e38))

    def query_mask(tile):
        row_at = pl.ds(pl.multiple_of(tile * tile_rows, tile_rows), tile_rows)
        row_pos = row_ref[row_at, :]
        lane = lax.broadcasted_iota(jnp.int32, (tile_rows, block_len), 1)
        return lambda spot: (lane + list_ref[spot] * block_len <= row_pos)[None]

    def scored(head, tile, first_spot, count, seen):
        at = pl.ds(pl.multiple_of(first_spot * block_len, block_len), count * block_len)
        scores = lax.dot_general(
            turned_ref[head, tile],
            key_ref[head, at, :],
            (((1,), (1,)), ((), ())),
            preferred_element_type=jnp.float32,
        )
        return at, [
            jnp.where(
                seen[spot],
                scores[:, spot * block_len : (spot + 1) * block_len].reshape(
                    group, tile_rows, block_len
                ),
                2 * low,
            ).reshape(lanes_rows, block_len)
            for spot in range(count)
        ]

    def weighed(head, at, parts):
        return functools.reduce(jnp.add, parts), jnp.dot(
            jnp.concatenate([part.astype(jnp.bfloat16) for part in parts], axis=1),
            value_ref[head, at, :],
            preferred_element_type=jnp.float32,
        )

    def write(head, tile, total, acc):
        sum_out[head, tile] = total
        acc_out[head, tile] = acc

    def finish(head, tile, total, acc):
        result = (acc / jnp.sum(total, axis=1, keepdims=True)).astype(jnp.bfloat16)
        row_at = pl.ds(pl.multiple_of(tile * tile_rows, tile_rows), tile_rows)
        for member in range(group):
            column = (head * group + member) * dim
            out_ref[row_at, column : column + dim] = result[
                member * tile_rows : (member + 1) * tile_rows
            ]

    def leave(tile):
        row_at = pl.ds(pl.multiple_of(tile * tile_rows, tile_rows), tile_rows)
        return pltpu.make_async_copy(
            out_ref.at[row_at, :], whole_ref.at[row_at, :], out_sems.at[tile]
        )

    def quick(tile, carry):
        furthest = table_ref[3 * blocks + tile]
        visible = query_mask(tile)
        for unit in range(units):
            fresh = first and unit == 0
            ends = last and unit == units - 1
            before = (sum_in, acc_in) if unit == 0 and not first else (sum_out, acc_out)
            first_spot = unit * unit_blocks
            active = jnp.int32(0)
            for spot in range(unit_blocks):
                begins = list_ref[first_spot + spot] * block_len
                active = active + (begins <= furthest).astype(jnp.int32)
            after = finish if ends else write
            for count in range(0, unit_blocks + 1, grain):

                @pl.when((active + grain - 1) // grain == count // grain)
                def _(count=count):
                    if not count and not fresh and not ends:
                        return
                    seen = [visible(first_spot + spot) for spot in range(count)]
                    for head in range(heads):
                        total = acc = jnp.zeros((lanes_rows, dim), jnp.float32)
                        if count:
                            at, parts = scored(head, tile, first_spot, count, seen)
                            parts = [jnp.exp2(part * scale) for part in parts]
                            total, acc = weighed(head, at, parts)
                        if not fresh:
                            total = before[0][head, tile] + total
                            acc = before[1][head, tile] + acc
                        after(head, tile, total, acc)

        if last:
            leave(tile).start()
        return carry

    def careful(tile, carry):
        furthest = table_ref[3 * blocks + tile]
        visible = query_mask(tile)

        def begin(head, ignored):
            if first:
                nothing = jnp.zeros((lanes_rows, dim), jnp.float32)
                most_out[head, tile] = nothing + low
                write(head, tile, nothing, nothing)
            else:
                total = sum_in[head, tile]
                most_out[head, tile] = jnp.where(
                    calm_in[0] < 1e38,
                    jnp.where(jnp.max(total, axis=1, keepdims=True) > 0, 0.0, low),
                    most_in[head, tile],
                )
                write(head, tile, total, acc_in[head, tile])
            return ignored

        lax.fori_loop(0, heads, begin, 0)

        def one(step, ignored):
            head = step % heads
            spot = step // heads

            @pl.when(list_ref[spot] * block_len <= furthest)
            def _():
                at, parts = scored(head, tile, spot, 1, [visible(spot)])
                was = most_out[head, tile]
                most = jnp.maximum(was, jnp.max(parts[0], axis=1, keepdims=True))
                total, acc = weighed(head, at, [jnp.exp2((parts[0] - most) * scale)])
                shrink = jnp.exp2((was - most) * scale)
                most_out[head, tile] = most
                write(
                    head,
                    tile,
                    sum_out[head, tile] * shrink + total,
                    acc_out[head, tile] * shrink + acc,
                )

            return ignored

        lax.fori_loop(0, spots * heads, one, 0)
        if last:
            for head in range(heads):
                finish(head, tile, sum_out[head, tile], acc_out[head, tile])
            leave(tile).start()
        return carry

    @pl.when(calm > 0.5)
    def _():
        lax.fori_loop(0, tiles, quick, 0)

    @pl.when(calm < 0.5)
    def _():
        lax.fori_loop(0, tiles, careful, 0)

    if last:
        for tile in range(tiles):
            leave(tile).wait()


def on_device(count, store_kv, block_owner, block_slot, span_len, row_index, fresh_q, fresh_kv):
    stored, block_len, heads, pair_width = store_kv.shape
    dim = pair_width // 2
    blocks = block_slot.shape[1]
    rows = row_index.shape[1]
    group = fresh_q.shape[2] // (heads * dim)
    tiles = rows // tile_rows
    lanes_rows = tile_rows * group
    raw_rows = block_len * 2 * heads

    def flat(array):
        lead = math.prod(array.shape[:-2])
        split = array.reshape(lead, heads, 2, dim)
        return split.transpose(0, 2, 1, 3).reshape(lead * 2 * heads, dim)

    store = flat(store_kv)
    place = lax.axis_index("req").reshape(1)
    row_pos = row_index[0]
    row_cos, row_sin = tables(row_pos.astype(jnp.float32), dim)
    cos, sin = tables(block_len * jnp.arange(blocks, dtype=jnp.float32), dim)
    row_lanes = jnp.broadcast_to(row_pos[:, None], (rows, block_len))
    wide = heads * 2 * dim + dim
    turned, placed, close, table, peak = pl.pallas_call(
        prepare,
        out_shape=(
            pltpu.VMEM((heads, tiles, lanes_rows, dim), jnp.bfloat16),
            pltpu.VMEM((blocks * block_len, wide), jnp.bfloat16),
            pltpu.VMEM(store.shape, jnp.bfloat16),
            pltpu.SMEM((3 * blocks + tiles + 1,), jnp.int32),
            pltpu.SMEM((1,), jnp.float32),
        ),
        in_specs=[anywhere] * 7 + [smem, vmem, vmem],
        out_specs=(vmem, vmem, vmem, smem, smem),
        scratch_shapes=[
            pltpu.VMEM((rows, heads * group * dim), jnp.bfloat16),
            pltpu.VMEM((rows * 2 * heads, dim), jnp.bfloat16),
            pltpu.VMEM((rows * 2 * heads, dim), jnp.float32),
            pltpu.VMEM((rows, wide), jnp.bfloat16),
            pltpu.VMEM((1, rows), jnp.int32),
            pltpu.SMEM((1, rows), jnp.int32),
            pltpu.SMEM((1, blocks), jnp.int32),
            pltpu.SMEM((1, blocks), jnp.int32),
            pltpu.SMEM(span_len.shape, jnp.int32),
            pltpu.SemaphoreType.DMA((tiles + 7,)),
        ],
        compiler_params=params,
        name="prepare",
    )(
        away(fresh_q[0]), away(flat(fresh_kv)), away(store), away(block_owner[:, :, 0]),
        away(block_slot), away(span_len), away(row_index), place, near(row_cos), near(row_sin),
    )

    def attention(number, last, sources, pick, shards, units, state):
        first = len(state) == 1
        state_shape = pltpu.VMEM((heads, tiles, lanes_rows, dim), jnp.float32)
        inputs = [near(source) for source in sources]
        inputs += [held(table), held(state[-1])]
        inputs += [near(array) for array in (turned, placed, cos, sin, row_lanes)]
        specs = [vmem] * len(sources) + [smem] * 2 + [vmem] * 5
        spots = units * unit_blocks
        result = [jax.ShapeDtypeStruct((rows, heads * group * dim), jnp.bfloat16)] if last else []
        return pl.pallas_call(
            functools.partial(attend, shards, pick, units, first, last),
            out_shape=[state_shape] * 3 + [pltpu.SMEM((1,), jnp.float32)] + result,
            in_specs=specs + [vmem] * (len(state) - 1),
            out_specs=[vmem] * 3 + [smem] + [anywhere] * len(result),
            input_output_aliases={}
            if first
            else {len(specs) + entry: entry for entry in range(3)},
            scratch_shapes=[
                pltpu.VMEM((chunk, raw_rows, dim), jnp.float32),
                pltpu.VMEM((heads, spots * block_len, dim), jnp.bfloat16),
                pltpu.VMEM((heads, spots * block_len, dim), jnp.bfloat16),
                pltpu.SMEM((blocks + 1,), jnp.int32),
            ]
            + (
                [
                    pltpu.VMEM((rows, heads * group * dim), jnp.bfloat16),
                    pltpu.SemaphoreType.DMA((tiles,)),
                ]
                if last
                else []
            ),
            compiler_params=params,
            name=f"attend_{number}",
        )(*inputs, *[near(entry) for entry in state[:-1]])

    if count != 4:
        everything = lax.all_gather(store, "req", axis=0, tiled=True)
        return attention(
            0, True, [everything], [lambda at: 0], count, blocks // unit_blocks, (peak,)
        )[-1][None]
    outer = [(0, 1), (1, 0), (2, 3), (3, 2)]
    inner = [(1, 2), (2, 1)]
    outward = [(1, 0), (2, 3)]
    none = -(1 << 16)
    is_end = lambda at: (at == 0) | (at == 3)

    def send(array, pairs):
        return lax.ppermute(array, "req", pairs)

    beside = send(store, outer)
    across = send(store, inner)
    store, close, turned = lax.optimization_barrier((store, close, turned))
    third_in = send(store, [(0, 2), (3, 1)])
    across, close, turned = lax.optimization_barrier((across, close, turned))
    second = send(across, outward)
    state = attention(0, False, [close], [lambda at: at], 1, 1, (peak,))
    third_in, beside, state = lax.optimization_barrier((third_in, beside, state))
    third = send(third_in, outward)
    state = attention(1, False, [beside], [lambda at: at ^ 1], 1, 1, state)
    second, state = lax.optimization_barrier((second, state))
    state = attention(
        2,
        False,
        [second, across],
        [
            lambda at: jnp.where(is_end(at), jnp.where(at == 0, 2, 1), none),
            lambda at: jnp.where(is_end(at), none, 3 - at),
        ],
        1,
        1,
        state,
    )
    third, state = lax.optimization_barrier((third, state))
    return attention(
        3,
        True,
        [third, third_in],
        [
            lambda at: jnp.where(is_end(at), 3 - at, none),
            lambda at: jnp.where(is_end(at), none, (3 - at) ^ 1),
        ],
        1,
        1,
        state,
    )[-1][None]


def solution(mesh):
    placed = (
        P(("grp", "req"), None, "kvh", None),
        P(("grp", "req"), None, None),
        P(("grp", "req"), None),
        P(("grp", "req"), None),
        P(("grp", "req"), None),
        P(("grp", "req"), None, "kvh"),
        P(("grp", "req"), None, "kvh", None),
    )
    return jax.shard_map(
        functools.partial(on_device, mesh.shape["req"]),
        mesh=mesh,
        in_specs=placed,
        out_specs=P(("grp", "req"), None, "kvh"),
        check_vma=False,
    )
```
